32 devices in a mesh: fsdp: 4 (over y, core), ctx: 4 (over z), tp: 2 (over x).
Axes of the slice: x: 2, y: 2, z: 4, core: 2. Of those that a mesh axis runs over, the one named last changes fastest.
Arguments:
- tokens_in: bfloat16 [64, 512, 768], P('fsdp', 'ctx'), may hold values from -6 to 6
- seq_lengths: int32 [64], P('fsdp'), may hold values from 256 to 512, as said below
- query_weight: bfloat16 [768, 768], P('fsdp', 'tp'), may hold values from -0.21875 to 0.21875
- query_bias: bfloat16 [12, 64], P('tp', 'fsdp'), may hold values from -3 to 3
- key_weight: bfloat16 [768, 768], P('fsdp', 'tp'), may hold values from -0.21875 to 0.21875
- value_weight: bfloat16 [768, 768], P('fsdp', 'tp'), may hold values from -0.21875 to 0.21875
- value_bias: bfloat16 [12, 64], P('tp', 'fsdp'), may hold values from -1.1953125 to 1.1953125
- output_weight: bfloat16 [768, 768], P('tp', 'fsdp'), may hold values from -0.875 to 0.875
- output_bias: bfloat16 [768], P('fsdp'), may hold values from -3 to 3
- attn_gain: bfloat16 [768], P('fsdp'), may hold values from 0.5 to 1.5
- attn_shift: bfloat16 [768], P('fsdp'), may hold values from -2 to 2
- inner_weight: bfloat16 [768, 3072], P('fsdp', 'tp'), may hold values from -0.21875 to 0.21875
- inner_bias: bfloat16 [24, 128], P('tp', 'fsdp'), may hold values from -3 to 3
- outer_weight: bfloat16 [3072, 768], P('tp', 'fsdp'), may hold values from -0.109375 to 0.109375
- outer_bias: bfloat16 [768], P('fsdp'), may hold values from -2 to 2
- ffn_gain: bfloat16 [768], P('fsdp'), may hold values from 0.5 to 1.5
- ffn_shift: bfloat16 [768], P('fsdp'), may hold values from -2 to 2
- cotangent: bfloat16 [64, 512, 768], P('fsdp', 'ctx'), may hold values from -6 to 6
Outputs:
- layer_out: bfloat16 [64, 512, 768], P('fsdp', 'ctx')
- input_grad: float32 [64, 512, 768], P('fsdp', 'ctx')
- query_weight_grad: float32 [768, 768], P('fsdp', 'tp')
- query_bias_grad: float32 [12, 64], P('tp', 'fsdp')
- key_weight_grad: float32 [768, 768], P('fsdp', 'tp')
- value_weight_grad: float32 [768, 768], P('fsdp', 'tp')
- value_bias_grad: float32 [12, 64], P('tp', 'fsdp')
- output_weight_grad: float32 [768, 768], P('tp', 'fsdp')
- output_bias_grad: float32 [768], P('fsdp')
- attn_gain_grad: float32 [768], P('fsdp')
- attn_shift_grad: float32 [768], P('fsdp')
- inner_weight_grad: float32 [768, 3072], P('fsdp', 'tp')
- inner_bias_grad: float32 [24, 128], P('tp', 'fsdp')
- outer_weight_grad: float32 [3072, 768], P('tp', 'fsdp')
- outer_bias_grad: float32 [768], P('fsdp')
- ffn_gain_grad: float32 [768], P('fsdp')
- ffn_shift_grad: float32 [768], P('fsdp')
The draws below stay inside these ranges and needn't reach their ends.
Inputs may be any that keep to these rules, and one draw needn't show every extreme that they name: `seq_lengths`: slots 0 to length - 1 of a sequence hold tokens, the rest padding. Some sequence has length 512 and some has length 256.
All inputs are finite; a program needn't handle non-finite values.
Results may differ from the reference program's by a relative error of at most 0.019.
Values may be sent and summed in bfloat16 or wider, within the bound.
No kernel may reach another device: no remote copies, remote signals or barrier semaphores. Data moves between devices by JAX's collectives and lax.ppermute only.
A program may use at most 256 MiB of HBM per device.

```python
import math
import jax
import jax.numpy as jnp
from jax import lax

D = 768
H = 12
HD = 64
FF = 3072
SEQ_LEN = 512
LEN_MIN = 256
SEQS = 64


def draw_seq_lengths(key, part):
    lengths_drawn = jax.random.randint(key, (SEQS,), LEN_MIN, SEQ_LEN + 1, dtype=jnp.int32)
    picked = jax.random.permutation(jax.random.fold_in(key, 7), SEQS)
    lengths_drawn = lengths_drawn.at[picked[0]].set(SEQ_LEN)
    return lengths_drawn.at[picked[1]].set(LEN_MIN)


def raised(values, own_key, source, target, parts, factor):
    owner, partner = [(jnp.arange(values.shape[dim]) // (values.shape[dim] // parts)).reshape([-1 if axis == dim else 1 for axis in range(values.ndim)]) for dim in (source, target)]
    chosen = jax.random.permutation(own_key, parts)[partner]
    strong = (owner == chosen) | (owner == (partner + parts // 2) % parts)
    return jnp.where(strong, factor * values, values)


def shard_levels(key, shape, pieces, least, high):
    def one(position, parts):
        steps = jax.random.uniform(jax.random.fold_in(jax.random.fold_in(key, 6), position), (parts,), jnp.float32, least / len(pieces), high / len(pieces))
        return jnp.repeat(jnp.exp(steps), shape[position] // parts).reshape((-1,) + (1,) * (len(shape) - position - 1))

    loudness = one(*pieces[0])
    for cut in pieces[1:]:
        loudness = loudness * one(*cut)
    return loudness


def scatter_about(stream_key, dims, scale, limit, shards=(), kind=jnp.bfloat16):
    values = scale * jax.random.normal(stream_key, dims, jnp.float32)
    if shards:
        values = values * shard_levels(stream_key, dims, shards, -0.22, 0.18)
    return jnp.clip(values, -limit, limit).astype(kind)


def bell_draw_with(own_key, dims, scale, most, split, heavy, kind=jnp.bfloat16):
    array = scale * jax.random.normal(own_key, dims, jnp.float32)
    if split:
        array = array * shard_levels(own_key, dims, split, -0.22, 0.18)
    return jnp.clip(raised(array, jax.random.fold_in(own_key, 3), *heavy), -most, most).astype(kind)


def setup_inputs(seed: int = 0) -> dict:
    key_of = jax.random.split(jax.random.key(seed), 19)
    return {
        "tokens_in": scatter_about(key_of[0], (SEQS, SEQ_LEN, D), 1.0, 6.0, ((0, 4), (1, 4))),
        "seq_lengths": draw_seq_lengths(jax.random.fold_in(key_of[18], 71), 0),
        "query_weight": scatter_about(key_of[2], (D, D), D ** -0.5, 0.21875, ((0, 4), (1, 2))),
        "query_bias": scatter_about(key_of[3], (H, HD), 0.5, 3.0, ((0, 2), (1, 4))),
        "key_weight": scatter_about(key_of[4], (D, D), D ** -0.5, 0.21875, ((0, 4), (1, 2))),
        "value_weight": scatter_about(key_of[5], (D, D), D ** -0.5, 0.21875, ((0, 4), (1, 2))),
        "value_bias": scatter_about(key_of[6], (H, HD), 0.2, 1.1953125, ((0, 2), (1, 4))),
        "output_weight": scatter_about(key_of[7], (D, D), (D // 16) ** -0.5, 0.875, ((0, 2), (1, 4))),
        "output_bias": scatter_about(key_of[8], (D,), 0.5, 3.0, ((0, 4),)),
        "attn_gain": jnp.clip(1.0 + 0.1 * jax.random.normal(key_of[9], (D,), jnp.float32), 0.5, 1.5).astype(jnp.bfloat16),
        "attn_shift": scatter_about(key_of[10], (D,), 0.3, 2.0, ((0, 4),)),
        "inner_weight": scatter_about(key_of[11], (D, FF), D ** -0.5, 0.21875, ((0, 4), (1, 2))),
        "inner_bias": scatter_about(key_of[12], (FF // 128, 128), 0.5, 3.0, ((0, 2), (1, 4))),
        "outer_weight": scatter_about(key_of[13], (FF, D), FF ** -0.5, 0.109375, ((0, 2), (1, 4))),
        "outer_bias": scatter_about(key_of[14], (D,), 0.3, 2.0, ((0, 4),)),
        "ffn_gain": jnp.clip(1.0 + 0.1 * jax.random.normal(key_of[15], (D,), jnp.float32), 0.5, 1.5).astype(jnp.bfloat16),
        "ffn_shift": scatter_about(key_of[16], (D,), 0.3, 2.0, ((0, 4),)),
        "cotangent": bell_draw_with(key_of[17], (SEQS, SEQ_LEN, D), 1.0, 6.0, ((0, 4), (1, 4)), (0, 2, 4, 2.0)),
    }


@jax.custom_vjp
def low(v):
    return lax.optimization_barrier(v.astype(jnp.bfloat16)).astype(jnp.float32)

@jax.custom_vjp
def low_back(v):
    return v

def low_keep(v):
    return (low(v), None)

def low_pass(kept, grad):
    return (grad,)

def back_keep(v):
    return (v, None)

def back_low(kept, grad):
    return (low(grad),)
low.defvjp(low_keep, low_pass)
low_back.defvjp(back_keep, back_low)
HIGHEST = lax.Precision.HIGHEST

def rounded_both(value):
    return low_back(low(value))

def layer_norm(values, gain_vec, offset_vec):
    centre = values - lax.optimization_barrier(jnp.mean(values, axis=-1, keepdims=True))
    spread = lax.optimization_barrier(jnp.mean(centre * centre, axis=-1, keepdims=True))
    return centre * lax.rsqrt(spread + 1e-12) * gain_vec + offset_vec

def attend(blocks):
    queries, keys, values, key_valid = blocks
    scores = low_back(jnp.einsum('qhd,khd->hqk', queries, keys, precision=HIGHEST) * (1.0 / math.sqrt(HD)))
    masked = jnp.where(key_valid[None, None, :], scores, -1e+30)
    largest = lax.optimization_barrier(jnp.max(masked, axis=-1, keepdims=True))
    exponent = jnp.where(key_valid[None, None, :], jnp.exp(masked - largest), 0.0)
    weights = exponent / lax.optimization_barrier(jnp.sum(exponent, axis=-1, keepdims=True))
    return rounded_both(jnp.einsum('hqk,khd->qhd', low(weights), values, precision=HIGHEST))

def forward(tokens, query_weight, query_bias, key_weight, value_weight, value_bias, output_weight, output_bias, attn_gain, attn_shift, inner_weight, inner_bias, outer_weight, outer_bias, ffn_gain, ffn_shift, key_valid, row_keep):
    token_rows = tokens.reshape(-1, D)
    queries = rounded_both(jnp.dot(token_rows, query_weight, precision=HIGHEST) + query_bias.reshape(-1))
    keys = rounded_both(jnp.dot(token_rows, key_weight, precision=HIGHEST))
    values = rounded_both(jnp.dot(token_rows, value_weight, precision=HIGHEST) + value_bias.reshape(-1))
    head_shape = (SEQS, SEQ_LEN, H, HD)
    mixed_heads = lax.map(jax.checkpoint(attend), (queries.reshape(head_shape), keys.reshape(head_shape), values.reshape(head_shape), key_valid))
    attn_out = low_back(jnp.dot(mixed_heads.reshape(-1, D), output_weight, precision=HIGHEST) + output_bias)
    normed = layer_norm(token_rows + attn_out, attn_gain, attn_shift)
    inner_pre = low_back(jnp.dot(low(normed), inner_weight, precision=HIGHEST) + inner_bias.reshape(-1))
    active = low(jax.nn.gelu(inner_pre, approximate=True))
    outer_out = low_back(jnp.dot(active, outer_weight, precision=HIGHEST) + outer_bias)
    result = layer_norm(normed + outer_out, ffn_gain, ffn_shift) * row_keep.reshape(-1, 1)
    return result.reshape(SEQS, SEQ_LEN, D)

def reference(tokens_in, seq_lengths, query_weight, query_bias, key_weight, value_weight, value_bias, output_weight, output_bias, attn_gain, attn_shift, inner_weight, inner_bias, outer_weight, outer_bias, ffn_gain, ffn_shift, cotangent):
    key_valid = jnp.arange(SEQ_LEN, dtype=jnp.int32)[None, :] < seq_lengths[:, None]
    row_keep = key_valid.astype(jnp.float32)

    def closed(tokens, *params):
        return forward(tokens, *params, key_valid, row_keep)
    params = [weight.astype(jnp.float32) for weight in (query_weight, query_bias, key_weight, value_weight, value_bias, output_weight, output_bias, attn_gain, attn_shift, inner_weight, inner_bias, outer_weight, outer_bias, ffn_gain, ffn_shift)]
    layer_out, pull_back = jax.vjp(closed, tokens_in.astype(jnp.float32), *params)
    gradients = pull_back(cotangent.astype(jnp.float32))
    return (layer_out.astype(jnp.bfloat16), gradients[0], gradients[1], gradients[2], gradients[3], gradients[4], gradients[5], gradients[6], gradients[7], gradients[8], gradients[9], gradients[10], gradients[11], gradients[12], gradients[13], gradients[14], gradients[15])
```

```python
import functools
import math

import jax
import jax.numpy as jnp
from jax import lax
from jax.experimental import pallas as pl
from jax.experimental.pallas import tpu as pltpu
from jax.sharding import PartitionSpec as P

HD = 64
BF = jnp.bfloat16
F32 = jnp.float32
ANY = pl.BlockSpec(memory_space=pl.ANY)
SMEM = pl.BlockSpec(memory_space=pltpu.SMEM)
VMEM_LIMIT = 60 * 1024 * 1024


def dot_nn(a, b):
    return lax.dot_general(a, b, (((1,), (0,)), ((), ())), preferred_element_type=F32)


def dot_nt(a, b):
    return lax.dot_general(a, b, (((1,), (1,)), ((), ())), preferred_element_type=F32)


def dot_tn(a, b):
    return lax.dot_general(a, b, (((0,), (0,)), ((), ())), preferred_element_type=F32)


def const_spec(shape):
    zeros = (0,) * len(shape)
    return pl.BlockSpec(shape, lambda *_: zeros)


def cost(flops, moved, exps=0):
    return pl.CostEstimate(flops=int(flops), bytes_accessed=int(moved), transcendentals=int(exps))


def head_columns(pair, half_cols):
    per = half_cols // 128
    return pl.multiple_of(pair // per * (3 * half_cols) + pair % per * 128, 128)


def front_kernel(dims, meta, bias, *refs):
    F, C, T, ns, span, D = dims
    xs, ws = refs[:C], refs[C : C + F * T]
    x_out, w_out, qkv, e_out, linv_out, ctx, sems = refs[C + F * T :]
    step = pl.program_id(0)
    NP = D // 128
    L = C * span
    Dl, half = D // F, D // T
    f = meta[0]
    c = meta[1]

    @pl.when(step == 0)
    def _():
        copies = [pltpu.make_async_copy(xs[k], x_out.at[k], sems.at[k]) for k in range(C)]
        for df in range(F):
            for dt in range(T):
                n = df * T + dt
                row = pl.multiple_of((f ^ df) * Dl, 16)
                copies.append(
                    pltpu.make_async_copy(
                        ws[n],
                        w_out.at[pl.ds(row, Dl), pl.ds(dt * 3 * half, 3 * half)],
                        sems.at[C + n],
                    )
                )
        for copy in copies:
            copy.start()
        for copy in copies:
            copy.wait()
        x = x_out[...].reshape(L * ns, D)

        def project(j, carry):
            cols = pl.ds(pl.multiple_of(j * 384, 128), 384)
            y = dot_nn(x_out[...].reshape(L * ns, D), w_out[:, cols]) + bias[:, cols]
            qkv[:, :, :, cols] = y.astype(BF).reshape(C, ns, span, 384)
            return carry

        lax.fori_loop(0, 3 * D // 384, project, 0)

    s = step // NP
    pair = step % NP
    q_col = head_columns(pair, half)
    q = qkv[:, s, :, pl.ds(q_col, 128)].reshape(L, 128)
    k = qkv[:, s, :, pl.ds(pl.multiple_of(q_col + half, 128), 128)].reshape(L, 128)
    v = qkv[:, s, :, pl.ds(pl.multiple_of(q_col + 2 * half, 128), 128)].reshape(L, 128)
    low = lax.broadcasted_iota(jnp.int32, (L, 128), 1) < HD
    zero = jnp.zeros((), BF)
    one = jnp.ones((L, 128), BF)
    lane = lax.broadcasted_iota(jnp.int32, (1, L), 1)
    pos = ((lane // span) ^ c) * span + lane % span
    mask = jnp.where(pos < meta[2 + s], 0.0, -1e30)
    values = []
    for h in range(2):
        mine = low if h == 0 else jnp.logical_not(low)
        scores = dot_nt(q, jnp.where(mine, k, zero)) * (math.log2(math.e) / math.sqrt(HD)) + mask
        top = jnp.max(scores, axis=-1, keepdims=True)
        e_out[0, h * L : (h + 1) * L, :] = jnp.exp2(scores - top).astype(BF)
        values.append(
            jnp.concatenate([jnp.where(mine, v, zero), jnp.where(mine, one, zero)], axis=1)
        )
    acc = dot_nn(e_out[0, :L, :], values[0]) + dot_nn(e_out[0, L:, :], values[1])
    linv = 1.0 / acc[:, 128:]
    linv_out[0] = linv
    ctx[:, s, :, pl.ds(pl.multiple_of(pair * 128, 128), 128)] = (
        (acc[:, :128] * linv).astype(BF).reshape(C, span, 128)
    )


def front_call(dims, meta, bias, xs, ws):
    F, C, T, ns, span, D = dims
    NP, L = D // 128, C * span
    rows = ns * span
    shapes = [
        jax.ShapeDtypeStruct((C, rows, D), BF),
        jax.ShapeDtypeStruct((D, 3 * D), BF),
        jax.ShapeDtypeStruct((C, ns, span, 3 * D), BF),
        jax.ShapeDtypeStruct((ns * NP, 2 * L, L), BF),
        jax.ShapeDtypeStruct((ns * NP, L, 128), F32),
        jax.ShapeDtypeStruct((C, ns, span, D), BF),
    ]
    return pl.pallas_call(
        functools.partial(front_kernel, dims),
        name="front",
        grid=(ns * NP,),
        out_shape=shapes,
        in_specs=[SMEM, const_spec((1, 3 * D))] + [ANY] * (C + F * T),
        out_specs=[
            const_spec(shapes[0].shape),
            const_spec(shapes[1].shape),
            const_spec(shapes[2].shape),
            pl.BlockSpec((1, 2 * L, L), lambda i: (i, 0, 0)),
            pl.BlockSpec((1, L, 128), lambda i: (i, 0, 0)),
            const_spec(shapes[5].shape),
        ],
        scratch_shapes=[pltpu.SemaphoreType.DMA((C + F * T,))],
        compiler_params=pltpu.CompilerParams(vmem_limit_bytes=VMEM_LIMIT),
        cost_estimate=cost(2 * L * ns * D * 3 * D, 40e6, ns * 12 * L * L),
    )(meta, bias, *xs, *ws)


def normalised(values):
    centre = values - jnp.mean(values, axis=-1, keepdims=True)
    spread = jnp.mean(centre * centre, axis=-1, keepdims=True)
    rstd = lax.rsqrt(spread + 1e-12)
    return centre * rstd, rstd


def norm_back(grad, gain, xhat, rstd):
    scaled = grad * gain
    first = jnp.mean(scaled, axis=-1, keepdims=True)
    second = jnp.mean(scaled * xhat, axis=-1, keepdims=True)
    return rstd * (scaled - first - xhat * second)


def rows_kernel(dims, FF, meta, vec, inner_bias, x_ref, ctx_ref, *refs):
    F, C, T, ns, span, D = dims
    n_w = F * T
    cots, wis, bds = refs[:C], refs[C : C + n_w], refs[C + n_w : C + 2 * n_w]
    refs = refs[C + 2 * n_w :]
    los = refs[:C]
    (
        first_out, dctx_out, nl_out, act_out, og_out, ig_out, ag_out, sums, inner_sums,
        cot_s, lo_s, wi, wo, wout, gp_s, sems, out_sems,
    ) = refs[C:]
    k = pl.program_id(0)
    R = ns * span
    Dl, half, fhalf = D // F, D // T, FF // T
    f = meta[0]
    c = meta[1]

    def weight_copies():
        copies = []
        for df in range(F):
            row = pl.multiple_of((f ^ df) * Dl, 16)
            for dt in range(T):
                n = df * T + dt
                rows = pl.ds(row, Dl)
                copies.append((
                    pltpu.make_async_copy(
                        bds[n].at[:, pl.ds(0, half)],
                        wo.at[rows, pl.ds(dt * half, half)], sems.at[n]),
                    pltpu.make_async_copy(
                        wis[n], wi.at[rows, pl.ds(dt * fhalf, fhalf)], sems.at[n_w + n]),
                    pltpu.make_async_copy(
                        bds[n].at[:, pl.ds(half, fhalf)],
                        wout.at[rows, pl.ds(dt * fhalf, fhalf)], sems.at[2 * n_w + n]),
                ))
        return copies

    def cot_copies():
        return [
            pltpu.make_async_copy(cots[i], cot_s.at[i], sems.at[3 * n_w + i]) for i in range(C)
        ]

    @pl.when(k == 0)
    def _():
        copies = weight_copies()
        for which in range(3):
            for group in copies:
                group[which].start()
        for copy in cot_copies():
            copy.start()
        sums[...] = jnp.zeros_like(sums)
        inner_sums[...] = jnp.zeros_like(inner_sums)
        for which in range(3):
            for group in copies:
                group[which].wait()
        for copy in cot_copies():
            copy.wait()

    def add_sum(row, value):
        sums[row : row + 1, :] += jnp.sum(value, axis=0, keepdims=True)

    out_bias, gain1, shift1 = vec[0:1, :], vec[1:2, :], vec[2:3, :]
    outer_bias, gain2, shift2 = vec[3:4, :], vec[4:5, :], vec[5:6, :]
    ctx_low = ctx_ref[0]
    before = x_ref[0].astype(F32) + dot_nt(ctx_low, wo[...]) + out_bias
    xhat1, rstd1 = normalised(before)
    normed = xhat1 * gain1 + shift1
    nl = normed.astype(BF)
    nl_out[0] = nl
    root = math.sqrt(2.0 / math.pi)
    chunk = 768
    for j in range(FF // chunk):
        cols = slice(j * chunk, (j + 1) * chunk)
        pre = dot_nn(nl, wi[:, cols]) + inner_bias[:, cols]
        square = pre * pre
        th = jnp.tanh(pre * (root + (root * 0.044715) * square))
        hp = 0.5 + 0.5 * th
        act_out[0, :, cols] = (pre * hp).astype(BF)
        gp_s[:, cols] = hp + (0.5 * pre) * (1.0 - th * th) * (
            root + (3.0 * root * 0.044715) * square
        )
    before2 = normed + dot_nt(act_out[0], wout[...]) + outer_bias
    xhat2, rstd2 = normalised(before2)
    row = lax.broadcasted_iota(jnp.int32, (R, 1), 0)
    position = (c ^ k) * span + row % span
    length = jnp.full((R, 1), meta[2], jnp.int32)
    for s in range(1, ns):
        length = jnp.where(row >= s * span, meta[2 + s], length)
    live = (position < length).astype(F32)
    lo_s[k] = (live * (xhat2 * gain2 + shift2)).astype(BF)
    for i in range(C):
        @pl.when(k == i)
        def _():
            pltpu.make_async_copy(lo_s.at[i], los[i], out_sems.at[i]).start()
    grad = cot_s[k].astype(F32) * live
    add_sum(4, grad * xhat2)
    add_sum(5, grad)
    second = norm_back(grad, gain2, xhat2, rstd2)
    og = second.astype(BF)
    og_out[0] = og
    add_sum(3, og.astype(F32))
    for j in range(FF // chunk):
        cols = slice(j * chunk, (j + 1) * chunk)
        ig = (dot_nn(og, wout[:, cols]) * gp_s[:, cols]).astype(BF)
        ig_out[0, :, cols] = ig
        inner_sums[:, cols] += jnp.sum(ig.astype(F32), axis=0, keepdims=True)
    ngrad = dot_nt(ig_out[0], wi[...]) + second
    add_sum(1, ngrad * xhat1)
    add_sum(2, ngrad)
    first = norm_back(ngrad, gain1, xhat1, rstd1)
    first_out[0] = first
    ag = first.astype(BF)
    ag_out[0] = ag
    add_sum(0, ag.astype(F32))
    dctx_out[0] = dot_nn(ag, wo[...]).astype(BF)

    @pl.when(k == C - 1)
    def _():
        for i in range(C):
            pltpu.make_async_copy(lo_s.at[i], los[i], out_sems.at[i]).wait()


def rows_call(dims, FF, meta, vec, inner_bias, x_all, ctx, cots, wis, bds):
    F, C, T, ns, span, D = dims
    R = ns * span
    tile = lambda n: pl.BlockSpec((1, R, n), lambda i: (i, 0, 0))
    widths = [(D, F32), (D, BF), (D, BF), (FF, BF), (D, BF), (FF, BF), (D, BF)]
    out_shape = (
        [jax.ShapeDtypeStruct((R, D), BF)] * C
        + [jax.ShapeDtypeStruct((C, R, n), kind) for n, kind in widths]
        + [jax.ShapeDtypeStruct((8, D), F32), jax.ShapeDtypeStruct((1, FF), F32)]
    )
    n_w = F * T
    outs = pl.pallas_call(
        functools.partial(rows_kernel, dims, FF),
        name="rows",
        grid=(C,),
        out_shape=out_shape,
        in_specs=[SMEM, const_spec((8, D)), const_spec((1, FF)), tile(D), tile(D)]
        + [ANY] * (C + 2 * n_w),
        out_specs=[ANY] * C
        + [tile(n) for n, _ in widths]
        + [const_spec((8, D)), const_spec((1, FF))],
        scratch_shapes=[
            pltpu.VMEM((C, R, D), BF),
            pltpu.VMEM((C, R, D), BF),
            pltpu.VMEM((D, FF), BF),
            pltpu.VMEM((D, D), BF),
            pltpu.VMEM((D, FF), BF),
            pltpu.VMEM((R, FF), F32),
            pltpu.SemaphoreType.DMA((3 * n_w + C,)),
            pltpu.SemaphoreType.DMA((C,)),
        ],
        compiler_params=pltpu.CompilerParams(vmem_limit_bytes=VMEM_LIMIT),
        cost_estimate=cost(4 * C * R * D * (2 * FF + D), 50e6, C * R * FF),
    )(meta, vec, inner_bias, x_all, ctx, *cots, *wis, *bds)
    return outs[:C], outs[C:]


def back_kernel(dims, qkv, ctx, dctx, e_ref, linv, out, ds_s):
    F, C, T, ns, span, D = dims
    step = pl.program_id(0)
    NP, L, half = D // 128, C * span, D // T
    s = step // NP
    pair = step % NP
    q_col = head_columns(pair, half)
    k_col = pl.multiple_of(q_col + half, 128)
    v_col = pl.multiple_of(q_col + 2 * half, 128)
    c_col = pl.multiple_of(pair * 128, 128)
    q = qkv[:, s, :, pl.ds(q_col, 128)].reshape(L, 128)
    k = qkv[:, s, :, pl.ds(k_col, 128)].reshape(L, 128)
    v = qkv[:, s, :, pl.ds(v_col, 128)].reshape(L, 128)
    grad = dctx[:, s, :, pl.ds(c_col, 128)].reshape(L, 128).astype(F32) * linv[0]
    grad_low = grad.astype(BF)
    product = grad_low.astype(F32) * ctx[:, s, :, pl.ds(c_col, 128)].reshape(L, 128).astype(F32)
    low = lax.broadcasted_iota(jnp.int32, (L, 128), 1) < HD
    zero = jnp.zeros((), BF)
    qs, ks, gs = [], [], []
    for h in range(2):
        mine = low if h == 0 else jnp.logical_not(low)
        row_dot = jnp.sum(jnp.where(mine, product, 0.0), axis=-1, keepdims=True)
        probs_grad = dot_nt(grad_low, jnp.where(mine, v, zero))
        e = e_ref[0, h * L : (h + 1) * L, :].astype(F32)
        ds_s[h * L : (h + 1) * L, :] = (e * (probs_grad - row_dot)).astype(BF)
        qs.append(jnp.where(mine, q, zero))
        ks.append(jnp.where(mine, k, zero))
        gs.append(jnp.where(mine, grad_low, zero))
    scale = 1.0 / math.sqrt(HD)
    dq = (dot_nn(ds_s[:L, :], ks[0]) + dot_nn(ds_s[L:, :], ks[1])) * scale
    dk = dot_tn(ds_s[...], jnp.concatenate(qs, axis=0)) * scale
    dv = dot_tn(e_ref[0], jnp.concatenate(gs, axis=0))
    out[:, s, :, pl.ds(q_col, 128)] = dq.astype(BF).reshape(C, span, 128)
    out[:, s, :, pl.ds(k_col, 128)] = dk.astype(BF).reshape(C, span, 128)
    out[:, s, :, pl.ds(v_col, 128)] = dv.astype(BF).reshape(C, span, 128)


def back_call(dims, qkv, ctx, dctx, e, linv):
    F, C, T, ns, span, D = dims
    NP, L = D // 128, C * span
    return pl.pallas_call(
        functools.partial(back_kernel, dims),
        name="back",
        grid=(ns * NP,),
        out_shape=jax.ShapeDtypeStruct(qkv.shape, BF),
        in_specs=[
            const_spec(qkv.shape),
            const_spec(ctx.shape),
            const_spec(dctx.shape),
            pl.BlockSpec((1, 2 * L, L), lambda i: (i, 0, 0)),
            pl.BlockSpec((1, L, 128), lambda i: (i, 0, 0)),
        ],
        out_specs=const_spec(qkv.shape),
        scratch_shapes=[pltpu.VMEM((2 * L, L), BF)],
        compiler_params=pltpu.CompilerParams(vmem_limit_bytes=VMEM_LIMIT),
        cost_estimate=cost(ns * NP * 16 * L * L * 128, 30e6, 0),
    )(qkv, ctx, dctx, e, linv)


def input_kernel(C, dqkv, w, first, *refs):
    outs, (sums, buf, sems) = refs[:C], refs[C:]
    k = pl.program_id(0)
    d = dqkv[0]

    @pl.when(k == 0)
    def _():
        sums[...] = jnp.zeros_like(sums)

    sums[...] += jnp.sum(d.astype(F32), axis=0, keepdims=True)
    buf[k] = (dot_nt(d, w[...]) + first[0]).astype(BF)
    for i in range(C):
        @pl.when(k == i)
        def _():
            pltpu.make_async_copy(buf.at[i], outs[i], sems.at[i]).start()

    @pl.when(k == C - 1)
    def _():
        for i in range(C):
            pltpu.make_async_copy(buf.at[i], outs[i], sems.at[i]).wait()


def input_call(dqkv, w, first):
    C, R, W = dqkv.shape
    D = w.shape[0]
    outs = pl.pallas_call(
        functools.partial(input_kernel, C),
        name="input_grad",
        grid=(C,),
        out_shape=[jax.ShapeDtypeStruct((R, D), BF)] * C + [jax.ShapeDtypeStruct((1, W), F32)],
        in_specs=[
            pl.BlockSpec((1, R, W), lambda i: (i, 0, 0)),
            const_spec(w.shape),
            pl.BlockSpec((1, R, D), lambda i: (i, 0, 0)),
        ],
        out_specs=[ANY] * C + [const_spec((1, W))],
        scratch_shapes=[pltpu.VMEM((C, R, D), BF), pltpu.SemaphoreType.DMA((C,))],
        compiler_params=pltpu.CompilerParams(vmem_limit_bytes=VMEM_LIMIT),
        cost_estimate=cost(2 * C * R * D * W, 15e6, 0),
    )(dqkv, w, first)
    return outs[:C], outs[C]


def weight_kernel(F, meta, left, right, keep, send, left_t, tile):
    D = left.shape[1]
    Dl = D // F

    @pl.when((pl.program_id(0) == 0) & (pl.program_id(1) == 0))
    def _():
        left_t[...] = left[...].T

    tile[...] = dot_nn(left_t[...], right[...]).astype(BF)
    f = meta[0]
    for high in range(F // 2):
        for bit, out in ((0, keep), (1, send)):
            row = pl.multiple_of((f ^ (2 * high + bit)) * Dl, 16)
            out[high, 0] = tile[pl.ds(row, Dl), :]


def weight_call(dims, meta, left, right):
    F, C, T, ns, span, D = dims
    rows, width = right.shape
    cols = 384
    per = width // T // cols
    out = jax.ShapeDtypeStruct((F // 2, T, D // F, width // T), BF)
    out_spec = pl.BlockSpec((F // 2, 1, D // F, cols), lambda a, b: (0, a, 0, b))
    return pl.pallas_call(
        functools.partial(weight_kernel, F),
        name="weight_grad",
        grid=(T, per),
        out_shape=[out, out],
        in_specs=[
            SMEM,
            const_spec(left.shape),
            pl.BlockSpec((rows, cols), lambda a, b: (0, a * per + b)),
        ],
        out_specs=[out_spec, out_spec],
        scratch_shapes=[pltpu.VMEM((D, rows), BF), pltpu.VMEM((D, cols), BF)],
        compiler_params=pltpu.CompilerParams(vmem_limit_bytes=VMEM_LIMIT),
        cost_estimate=cost(2 * rows * D * width, 2 * (rows * (D + width) + D * width), 0),
    )(meta, left, right)


def xor_pairs(count, mask):
    return [(i, i ^ mask) for i in range(count)]


def added(a, b):
    return (a.astype(F32) + b.astype(F32)).astype(BF)


def per_device(
    tokens_in, seq_lengths, query_weight, query_bias, key_weight, value_weight, value_bias,
    output_weight, output_bias, attn_gain, attn_shift, inner_weight, inner_bias, outer_weight,
    outer_bias, ffn_gain, ffn_shift, cotangent,
):
    F, C, T = (lax.axis_size(a) for a in ("fsdp", "ctx", "tp"))
    f, c, t = (lax.axis_index(a) for a in ("fsdp", "ctx", "tp"))
    S, span, D = tokens_in.shape
    ns = S // (C * T)
    Dl, half = D // F, D // T
    fhalf = inner_weight.shape[1]
    FF = fhalf * T
    H = query_bias.shape[0] * T
    R = ns * span
    dims = (F, C, T, ns, span, D)

    def to_sequences(array):
        out = []
        for k in range(C):
            piece = lax.dynamic_slice_in_dim(array, ((c ^ k) * T + t) * ns, ns, 0).reshape(R, D)
            out.append(lax.ppermute(piece, "ctx", xor_pairs(C, k)) if k else piece)
        return out

    def to_slots(pieces, kind):
        out = lax.full((S, span, D), 0, kind)
        for k in range(C):
            piece = lax.ppermute(pieces[k], "ctx", xor_pairs(C, k)) if k else pieces[k]
            for dt in range(T):
                got = lax.ppermute(piece, "tp", xor_pairs(T, dt)) if dt else piece
                out = lax.dynamic_update_slice_in_dim(
                    out, got.reshape(ns, span, D).astype(kind), ((c ^ k) * T + (t ^ dt)) * ns, 0
                )
        return out

    def gathered(shard):
        held = {}
        for high in range(0, F, 2):
            for dt in range(T):
                if high == 0 and dt == 0:
                    held[0, 0] = shard
                else:
                    pairs = [
                        (i * T + j, (i ^ high) * T + (j ^ dt)) for i in range(F) for j in range(T)
                    ]
                    held[high, dt] = lax.ppermute(shard, ("fsdp", "tp"), pairs)
        for high in range(0, F, 2):
            for dt in range(T):
                held[high + 1, dt] = lax.ppermute(held[high, dt], "fsdp", xor_pairs(F, 1))
        return [held[df, dt] for df in range(F) for dt in range(T)]

    def by_half(array):
        return array[jnp.arange(T) ^ t]

    x_pieces = to_sequences(tokens_in)
    qkv_pieces = gathered(jnp.concatenate([query_weight, key_weight, value_weight], axis=1))
    small = jnp.concatenate(
        [output_bias, attn_gain, attn_shift, outer_bias, ffn_gain, ffn_shift]
        + [query_bias.reshape(-1), value_bias.reshape(-1), inner_bias.reshape(-1)]
    )
    small = lax.all_gather(small, ("fsdp", "tp"), axis=0, tiled=False).reshape(F, T, -1)
    vec = small[:, 0, : 6 * Dl].reshape(F, 6, Dl).transpose(1, 0, 2).reshape(6, D).astype(F32)
    vec = jnp.concatenate([vec, jnp.zeros((2, D), F32)], axis=0)
    n_qb = query_bias.size

    def unit_rows(start, shape):
        block = small[:, :, start : start + math.prod(shape)].reshape(F, T, *shape)
        return by_half(block.transpose(1, 2, 0, 3).reshape(T, -1).astype(F32))

    q_off = unit_rows(6 * Dl, query_bias.shape)
    v_off = unit_rows(6 * Dl + n_qb, value_bias.shape)
    inner_off = unit_rows(6 * Dl + 2 * n_qb, inner_bias.shape).reshape(1, FF)
    qkv_off = jnp.stack([q_off, jnp.zeros_like(q_off), v_off], axis=1).reshape(1, 3 * D)
    inner_pieces = gathered(inner_weight)
    outer_pieces = gathered(jnp.concatenate([output_weight.T, outer_weight.T], axis=1))
    cot_pieces = to_sequences(cotangent)
    lengths = lax.dynamic_slice_in_dim(seq_lengths, (c * T + t) * ns, ns, 0)
    meta = jnp.concatenate([jnp.stack([f, c]).astype(jnp.int32), lengths])

    x_all, qkv_w, qkv, e, linv, ctx = front_call(dims, meta, qkv_off, x_pieces, qkv_pieces)
    los, (first, dctx, nl, act, og, ig, ag, sums, inner_sums) = rows_call(
        dims, FF, meta, vec, inner_off, x_all, ctx.reshape(C, R, D), cot_pieces,
        inner_pieces, outer_pieces,
    )
    layer_out = to_slots(los, BF)

    def reduced(left, right):
        left, right = left.reshape(C * R, -1), right.reshape(C * R, -1)
        keep, send = weight_call(dims, meta, left, right)
        total = added(keep, lax.ppermute(send, "fsdp", xor_pairs(F, 1)))
        while total.shape[0] > 1:
            h = total.shape[0] // 2
            total = added(total[:h], lax.ppermute(total[h:], "fsdp", xor_pairs(F, 2 * h)))
        total = total[0]
        while total.shape[0] > 1:
            h = total.shape[0] // 2
            total = added(total[:h], lax.ppermute(total[h:], "tp", xor_pairs(T, h)))
        total = total[0]
        bits = [1 << b for b in range(C.bit_length() - 1)]
        for bit in bits:
            h = total.shape[0] // 2
            mine = (c // bit) % 2
            away = lax.ppermute(
                lax.dynamic_slice_in_dim(total, (1 - mine) * h, h, 0), "ctx", xor_pairs(C, bit)
            )
            total = added(lax.dynamic_slice_in_dim(total, mine * h, h, 0), away)
        for bit in reversed(bits):
            away = lax.ppermute(total, "ctx", xor_pairs(C, bit))
            upper = (c // bit) % 2 == 1
            total = jnp.concatenate(
                [jnp.where(upper, away, total), jnp.where(upper, total, away)], axis=0
            )
        return total

    outer_t = reduced(og, act)
    inner_g = reduced(nl, ig)
    output_t = reduced(ag, ctx)
    dqkv = back_call(dims, qkv, ctx, dctx.reshape(ctx.shape), e, linv)
    ins, qkv_sums = input_call(dqkv.reshape(C, R, 3 * D), qkv_w, first)
    input_grad = to_slots(ins, F32)
    qkv_g = reduced(x_all, dqkv)

    def all_sum(array):
        for axis, count in (("fsdp", F), ("tp", T), ("ctx", C)):
            for b in range(count.bit_length() - 1):
                array = array + lax.ppermute(array, axis, xor_pairs(count, 1 << b))
        return array

    early = all_sum(jnp.concatenate([sums[:6].reshape(-1), by_half(inner_sums.reshape(T, -1)).reshape(-1)]))
    qkv_parts = by_half(qkv_sums.reshape(T, 3, half))
    late = all_sum(jnp.concatenate([qkv_parts[:, 0].reshape(-1), qkv_parts[:, 2].reshape(-1)]))
    vec_sums = lax.dynamic_slice_in_dim(early[: 6 * D].reshape(6, D), f * Dl, Dl, 1)

    def shard_of(array, shape):
        whole = array.reshape(shape[0] * T, shape[1] * F)
        return lax.dynamic_slice(whole, (t * shape[0], f * shape[1]), shape)

    return (
        layer_out,
        input_grad,
        qkv_g[:, :half].astype(F32),
        shard_of(late[:D], query_bias.shape),
        qkv_g[:, half : 2 * half].astype(F32),
        qkv_g[:, 2 * half :].astype(F32),
        shard_of(late[D:], value_bias.shape),
        output_t.T.astype(F32),
        vec_sums[0],
        vec_sums[1],
        vec_sums[2],
        inner_g.astype(F32),
        shard_of(early[6 * D :], inner_bias.shape),
        outer_t.T.astype(F32),
        vec_sums[3],
        vec_sums[4],
        vec_sums[5],
    )


def solution(mesh):
    rows3, flat = P("fsdp", "ctx", None), P("fsdp")
    wide, tall = P("fsdp", "tp"), P("tp", "fsdp")
    params = (wide, tall, wide, wide, tall, tall, flat, flat, flat, wide, tall, tall, flat, flat, flat)
    return jax.shard_map(
        per_device,
        mesh=mesh,
        in_specs=(rows3, P("fsdp")) + params + (rows3,),
        out_specs=(rows3, rows3) + params,
        check_vma=False,
    )
```

```python
import functools
import math

import jax
import jax.numpy as jnp
from jax import lax
from jax.experimental import pallas as pl
from jax.experimental.pallas import tpu as pltpu
from jax.sharding import PartitionSpec as P

HD = 64
BF = jnp.bfloat16
F32 = jnp.float32
ANY = pl.BlockSpec(memory_space=pl.ANY)
SMEM = pl.BlockSpec(memory_space=pltpu.SMEM)
EXTRA = 16
VMEM_LIMIT = 60 * 1024 * 1024


def dot_nn(a, b):
    return lax.dot_general(a, b, (((1,), (0,)), ((), ())), preferred_element_type=F32)


def dot_nt(a, b):
    return lax.dot_general(a, b, (((1,), (1,)), ((), ())), preferred_element_type=F32)


def dot_tn(a, b):
    return lax.dot_general(a, b, (((0,), (0,)), ((), ())), preferred_element_type=F32)


def const_spec(shape):
    zeros = (0,) * len(shape)
    return pl.BlockSpec(shape, lambda *_: zeros)


def cost(flops, moved, exps=0):
    return pl.CostEstimate(flops=int(flops), bytes_accessed=int(moved), transcendentals=int(exps))


def head_columns(pair, half_cols):
    per = half_cols // 128
    return pl.multiple_of(pair // per * (3 * half_cols) + pair % per * 128, 128)


def order_of(F, T, across):
    chip = [("fsdp", 1 << b) for b in range(1, F.bit_length() - 1)]
    pair = [("tp", 1 << b) for b in range(T.bit_length() - 1)]
    return chip + pair if across else pair + chip


def stacks(F, T, across):
    held, out = [(0, 0)], []
    steps = order_of(F, T, across)
    for n, (axis, bit) in enumerate(steps):
        got = [(df ^ bit, dt) if axis == "fsdp" else (df, dt ^ bit) for df, dt in held]
        if n == len(steps) - 1:
            out += [held, got]
        held = held + got
    return out + [[(df ^ 1, dt) for df, dt in part] for part in out]


def pieces_of(refs, F, T, across):
    return {
        at: ref.at[i] for ref, part in zip(refs, stacks(F, T, across)) for i, at in enumerate(part)
    }


def front_kernel(dims, meta, *refs):
    F, C, T, ns, span, D = dims
    n_w = F * T
    n_a = len(stacks(F, T, False))
    xs, low_refs, high_refs = refs[:C], refs[C : C + n_a], refs[C + n_a : C + 2 * n_a]
    x_out, w_out, qkv, e_out, linv_out, ctx, small, bias, sems = refs[C + 2 * n_a :]
    step = pl.program_id(0)
    NP = D // 128
    L = C * span
    Dl, half = D // F, D // T
    f = meta[0]
    c = meta[1]

    @pl.when(step == 0)
    def _():
        copies = [pltpu.make_async_copy(xs[k], x_out.at[k], sems.at[k]) for k in range(C)]
        qk = pieces_of(low_refs, F, T, False)
        vo = pieces_of(high_refs, F, T, True)
        for df in range(F):
            for dt in range(T):
                n = df * T + dt
                rows = pl.ds(pl.multiple_of((f ^ df) * Dl, 16), Dl)
                start = dt * 3 * half
                copies += [
                    pltpu.make_async_copy(
                        qk[df, dt].at[pl.ds(0, Dl)], w_out.at[rows, pl.ds(start, 2 * half)],
                        sems.at[C + n]),
                    pltpu.make_async_copy(
                        vo[df, dt].at[pl.ds(0, Dl), pl.ds(0, half)],
                        w_out.at[rows, pl.ds(start + 2 * half, half)], sems.at[C + n_w + n]),
                    pltpu.make_async_copy(
                        qk[df, dt].at[pl.ds(Dl, EXTRA), pl.ds(0, half)], small.at[n],
                        sems.at[C + 2 * n_w + n]),
                ]
        for copy in copies:
            copy.start()
        for copy in copies:
            copy.wait()
        bias[...] = jnp.zeros_like(bias)
        for dt in range(T):
            part = sum(small[df * T + dt, :2, :].astype(F32) for df in range(F))
            bias[:, dt * 3 * half : dt * 3 * half + half] = part[0:1]
            bias[:, (dt * 3 + 2) * half : (dt * 3 + 3) * half] = part[1:2]

        def project(j, carry):
            cols = pl.ds(pl.multiple_of(j * 384, 128), 384)
            y = dot_nn(x_out[...].reshape(L * ns, D), w_out[:, cols]) + bias[:, cols]
            qkv[:, :, :, cols] = y.astype(BF).reshape(C, ns, span, 384)
            return carry

        lax.fori_loop(0, 3 * D // 384, project, 0)

    s = step // NP
    pair = step % NP
    q_col = head_columns(pair, half)
    q = qkv[:, s, :, pl.ds(q_col, 128)].reshape(L, 128)
    k = qkv[:, s, :, pl.ds(pl.multiple_of(q_col + half, 128), 128)].reshape(L, 128)
    v = qkv[:, s, :, pl.ds(pl.multiple_of(q_col + 2 * half, 128), 128)].reshape(L, 128)
    low = lax.broadcasted_iota(jnp.int32, (L, 128), 1) < HD
    zero = jnp.zeros((), BF)
    one = jnp.ones((L, 128), BF)
    lane = lax.broadcasted_iota(jnp.int32, (1, L), 1)
    pos = ((lane // span) ^ c) * span + lane % span
    mask = jnp.where(pos < meta[2 + s], 0.0, -1e30)
    values = []
    for h in range(2):
        mine = low if h == 0 else jnp.logical_not(low)
        scores = dot_nt(q, jnp.where(mine, k, zero)) * (math.log2(math.e) / math.sqrt(HD)) + mask
        top = jnp.max(scores, axis=-1, keepdims=True)
        e_out[0, h * L : (h + 1) * L, :] = jnp.exp2(scores - top).astype(BF)
        values.append(
            jnp.concatenate([jnp.where(mine, v, zero), jnp.where(mine, one, zero)], axis=1)
        )
    acc = dot_nn(e_out[0, :L, :], values[0]) + dot_nn(e_out[0, L:, :], values[1])
    linv = 1.0 / acc[:, 128:]
    linv_out[0] = linv
    ctx[:, s, :, pl.ds(pl.multiple_of(pair * 128, 128), 128)] = (
        (acc[:, :128] * linv).astype(BF).reshape(C, span, 128)
    )


def front_call(dims, meta, xs, lows, highs):
    F, C, T, ns, span, D = dims
    NP, L = D // 128, C * span
    rows = ns * span
    shapes = [
        jax.ShapeDtypeStruct((C, rows, D), BF),
        jax.ShapeDtypeStruct((D, 3 * D), BF),
        jax.ShapeDtypeStruct((C, ns, span, 3 * D), BF),
        jax.ShapeDtypeStruct((ns * NP, 2 * L, L), BF),
        jax.ShapeDtypeStruct((ns * NP, L, 128), F32),
        jax.ShapeDtypeStruct((C, ns, span, D), BF),
    ]
    return pl.pallas_call(
        functools.partial(front_kernel, dims),
        name="front",
        grid=(ns * NP,),
        out_shape=shapes,
        in_specs=[SMEM] + [ANY] * (C + len(lows) + len(highs)),
        out_specs=[
            const_spec(shapes[0].shape),
            const_spec(shapes[1].shape),
            const_spec(shapes[2].shape),
            pl.BlockSpec((1, 2 * L, L), lambda i: (i, 0, 0)),
            pl.BlockSpec((1, L, 128), lambda i: (i, 0, 0)),
            const_spec(shapes[5].shape),
        ],
        scratch_shapes=[
            pltpu.VMEM((F * T, EXTRA, D // T), BF),
            pltpu.VMEM((1, 3 * D), F32),
            pltpu.SemaphoreType.DMA((C + 3 * F * T,)),
        ],
        compiler_params=pltpu.CompilerParams(vmem_limit_bytes=VMEM_LIMIT),
        cost_estimate=cost(2 * L * ns * D * 3 * D, 40e6, ns * 12 * L * L),
    )(meta, *xs, *lows, *highs)


def normalised(values):
    centre = values - jnp.mean(values, axis=-1, keepdims=True)
    spread = jnp.mean(centre * centre, axis=-1, keepdims=True)
    rstd = lax.rsqrt(spread + 1e-12)
    return centre * rstd, rstd


def norm_back(grad, gain, xhat, rstd):
    scaled = grad * gain
    first = jnp.mean(scaled, axis=-1, keepdims=True)
    second = jnp.mean(scaled * xhat, axis=-1, keepdims=True)
    return rstd * (scaled - first - xhat * second)


def rows_kernel(dims, FF, meta, x_ref, ctx_ref, *refs):
    F, C, T, ns, span, D = dims
    n_w = F * T
    n_a = len(stacks(F, T, False))
    cots = refs[:C]
    qk, vo, inner, outer = (
        pieces_of(refs[C + i * n_a : C + (i + 1) * n_a], F, T, i % 2 == 1) for i in range(4)
    )
    refs = refs[C + 4 * n_a :]
    los = refs[:C]
    (
        first_out, dctx_out, nl_out, act_out, og_out, ig_out, ag_out, sums,
        cot_s, lo_s, wi, wo, wout, gp_s, small, vec, inner_bias, sems, out_sems,
    ) = refs[C:]
    k = pl.program_id(0)
    R = ns * span
    Dl, half, fhalf = D // F, D // T, FF // T
    f = meta[0]
    c = meta[1]

    def weight_copies():
        copies = []
        for df in range(F):
            row = pl.multiple_of((f ^ df) * Dl, 16)
            for dt in range(T):
                n = df * T + dt
                rows = pl.ds(row, Dl)
                copies.append((
                    pltpu.make_async_copy(
                        vo[df, dt].at[pl.ds(0, Dl), pl.ds(half, half)],
                        wo.at[rows, pl.ds(dt * half, half)], sems.at[n]),
                    pltpu.make_async_copy(
                        inner[df, dt],
                        wi.at[rows, pl.ds(dt * fhalf, fhalf)], sems.at[n_w + n]),
                    pltpu.make_async_copy(
                        outer[df, dt],
                        wout.at[rows, pl.ds(dt * fhalf, fhalf)], sems.at[2 * n_w + n]),
                ) + tuple(
                    pltpu.make_async_copy(
                        (qk if part == 0 else vo)[df, dt].at[pl.ds(Dl, EXTRA)],
                        small.at[n, :, pl.ds(part * D, D)], sems.at[(3 + part) * n_w + n])
                    for part in range(2)
                ))
        return copies

    def cot_copies():
        return [
            pltpu.make_async_copy(cots[i], cot_s.at[i], sems.at[5 * n_w + i]) for i in range(C)
        ]

    @pl.when(k == 0)
    def _():
        copies = weight_copies()
        for which in range(5):
            for group in copies:
                group[which].start()
        for copy in cot_copies():
            copy.start()
        sums[...] = jnp.zeros_like(sums)
        for which in range(5):
            for group in copies:
                group[which].wait()
        for copy in cot_copies():
            copy.wait()
        for dt in range(T):
            part = sum(small[df * T + dt, :EXTRA, :].astype(F32) for df in range(F))
            inner_bias[:, dt * fhalf : (dt + 1) * fhalf] = part[2:3]
            if dt == 0:
                vec[...] = part[3:9, :D]

    def add_sum(row, value):
        sums[row : row + 1, :] += jnp.sum(value, axis=0, keepdims=True)

    out_bias, gain1, shift1 = vec[0:1, :], vec[1:2, :], vec[2:3, :]
    outer_bias, gain2, shift2 = vec[3:4, :], vec[4:5, :], vec[5:6, :]
    ctx_low = ctx_ref[0]
    before = x_ref[0].astype(F32) + dot_nt(ctx_low, wo[...]) + out_bias
    xhat1, rstd1 = normalised(before)
    normed = xhat1 * gain1 + shift1
    nl = normed.astype(BF)
    nl_out[0] = nl
    root = math.sqrt(2.0 / math.pi)
    chunk = 768
    for j in range(FF // chunk):
        cols = slice(j * chunk, (j + 1) * chunk)
        pre = dot_nn(nl, wi[:, cols]) + inner_bias[:, cols]
        square = pre * pre
        th = jnp.tanh(pre * (root + (root * 0.044715) * square))
        hp = 0.5 + 0.5 * th
        act_out[0, :, cols] = (pre * hp).astype(BF)
        gp_s[:, cols] = hp + (0.5 * pre) * (1.0 - th * th) * (
            root + (3.0 * root * 0.044715) * square
        )
    before2 = normed + dot_nt(act_out[0], wout[...]) + outer_bias
    xhat2, rstd2 = normalised(before2)
    row = lax.broadcasted_iota(jnp.int32, (R, 1), 0)
    position = (c ^ k) * span + row % span
    length = jnp.full((R, 1), meta[2], jnp.int32)
    for s in range(1, ns):
        length = jnp.where(row >= s * span, meta[2 + s], length)
    live = (position < length).astype(F32)
    lo_s[k] = (live * (xhat2 * gain2 + shift2)).astype(BF)
    for i in range(C):
        @pl.when(k == i)
        def _():
            pltpu.make_async_copy(lo_s.at[i], los[i], out_sems.at[i]).start()
    grad = cot_s[k].astype(F32) * live
    add_sum(4, grad * xhat2)
    add_sum(5, grad)
    second = norm_back(grad, gain2, xhat2, rstd2)
    og = second.astype(BF)
    og_out[0] = og
    add_sum(3, og.astype(F32))
    for j in range(FF // chunk):
        cols = slice(j * chunk, (j + 1) * chunk)
        ig = (dot_nn(og, wout[:, cols]) * gp_s[:, cols]).astype(BF)
        ig_out[0, :, cols] = ig
    ngrad = dot_nt(ig_out[0], wi[...]) + second
    add_sum(1, ngrad * xhat1)
    add_sum(2, ngrad)
    first = norm_back(ngrad, gain1, xhat1, rstd1)
    first_out[0] = first
    ag = first.astype(BF)
    ag_out[0] = ag
    add_sum(0, ag.astype(F32))
    dctx_out[0] = dot_nn(ag, wo[...]).astype(BF)

    @pl.when(k == C - 1)
    def _():
        for i in range(C):
            pltpu.make_async_copy(lo_s.at[i], los[i], out_sems.at[i]).wait()


def rows_call(dims, FF, meta, x_all, ctx, cots, weights):
    F, C, T, ns, span, D = dims
    R = ns * span
    tile = lambda n: pl.BlockSpec((1, R, n), lambda i: (i, 0, 0))
    widths = [(D, F32), (D, BF), (D, BF), (FF, BF), (D, BF), (FF, BF), (D, BF)]
    out_shape = (
        [jax.ShapeDtypeStruct((R, D), BF)] * C
        + [jax.ShapeDtypeStruct((C, R, n), kind) for n, kind in widths]
        + [jax.ShapeDtypeStruct((EXTRA, D), F32)]
    )
    n_w = F * T
    outs = pl.pallas_call(
        functools.partial(rows_kernel, dims, FF),
        name="rows",
        grid=(C,),
        out_shape=out_shape,
        in_specs=[SMEM, tile(D), tile(D)]
        + [ANY] * (C + len(weights)),
        out_specs=[ANY] * C
        + [tile(n) for n, _ in widths]
        + [const_spec((EXTRA, D))],
        scratch_shapes=[
            pltpu.VMEM((C, R, D), BF),
            pltpu.VMEM((C, R, D), BF),
            pltpu.VMEM((D, FF), BF),
            pltpu.VMEM((D, D), BF),
            pltpu.VMEM((D, FF), BF),
            pltpu.VMEM((R, FF), F32),
            pltpu.VMEM((n_w, EXTRA, FF // T), BF),
            pltpu.VMEM((6, D), F32),
            pltpu.VMEM((1, FF), F32),
            pltpu.SemaphoreType.DMA((5 * n_w + C,)),
            pltpu.SemaphoreType.DMA((C,)),
        ],
        compiler_params=pltpu.CompilerParams(vmem_limit_bytes=VMEM_LIMIT),
        cost_estimate=cost(4 * C * R * D * (2 * FF + D), 50e6, C * R * FF),
    )(meta, x_all, ctx, *cots, *weights)
    return outs[:C], outs[C:]


def back_kernel(dims, qkv, ctx, dctx, e_ref, linv, out, ds_s):
    F, C, T, ns, span, D = dims
    step = pl.program_id(0)
    NP, L, half = D // 128, C * span, D // T
    s = step // NP
    pair = step % NP
    q_col = head_columns(pair, half)
    k_col = pl.multiple_of(q_col + half, 128)
    v_col = pl.multiple_of(q_col + 2 * half, 128)
    c_col = pl.multiple_of(pair * 128, 128)
    q = qkv[:, s, :, pl.ds(q_col, 128)].reshape(L, 128)
    k = qkv[:, s, :, pl.ds(k_col, 128)].reshape(L, 128)
    v = qkv[:, s, :, pl.ds(v_col, 128)].reshape(L, 128)
    grad = dctx[:, s, :, pl.ds(c_col, 128)].reshape(L, 128).astype(F32) * linv[0]
    grad_low = grad.astype(BF)
    product = grad_low.astype(F32) * ctx[:, s, :, pl.ds(c_col, 128)].reshape(L, 128).astype(F32)
    low = lax.broadcasted_iota(jnp.int32, (L, 128), 1) < HD
    zero = jnp.zeros((), BF)
    qs, ks, gs = [], [], []
    for h in range(2):
        mine = low if h == 0 else jnp.logical_not(low)
        row_dot = jnp.sum(jnp.where(mine, product, 0.0), axis=-1, keepdims=True)
        probs_grad = dot_nt(grad_low, jnp.where(mine, v, zero))
        e = e_ref[0, h * L : (h + 1) * L, :].astype(F32)
        ds_s[h * L : (h + 1) * L, :] = (e * (probs_grad - row_dot)).astype(BF)
        qs.append(jnp.where(mine, q, zero))
        ks.append(jnp.where(mine, k, zero))
        gs.append(jnp.where(mine, grad_low, zero))
    scale = 1.0 / math.sqrt(HD)
    dq = (dot_nn(ds_s[:L, :], ks[0]) + dot_nn(ds_s[L:, :], ks[1])) * scale
    dk = dot_tn(ds_s[...], jnp.concatenate(qs, axis=0)) * scale
    dv = dot_tn(e_ref[0], jnp.concatenate(gs, axis=0))
    out[:, s, :, pl.ds(q_col, 128)] = dq.astype(BF).reshape(C, span, 128)
    out[:, s, :, pl.ds(k_col, 128)] = dk.astype(BF).reshape(C, span, 128)
    out[:, s, :, pl.ds(v_col, 128)] = dv.astype(BF).reshape(C, span, 128)


def back_call(dims, qkv, ctx, dctx, e, linv):
    F, C, T, ns, span, D = dims
    NP, L = D // 128, C * span
    return pl.pallas_call(
        functools.partial(back_kernel, dims),
        name="back",
        grid=(ns * NP,),
        out_shape=jax.ShapeDtypeStruct(qkv.shape, BF),
        in_specs=[
            const_spec(qkv.shape),
            const_spec(ctx.shape),
            const_spec(dctx.shape),
            pl.BlockSpec((1, 2 * L, L), lambda i: (i, 0, 0)),
            pl.BlockSpec((1, L, 128), lambda i: (i, 0, 0)),
        ],
        out_specs=const_spec(qkv.shape),
        scratch_shapes=[pltpu.VMEM((2 * L, L), BF)],
        compiler_params=pltpu.CompilerParams(vmem_limit_bytes=VMEM_LIMIT),
        cost_estimate=cost(ns * NP * 16 * L * L * 128, 30e6, 0),
    )(qkv, ctx, dctx, e, linv)


def input_kernel(C, dqkv, w, first, *refs):
    outs, (buf, sems) = refs[:C], refs[C:]
    k = pl.program_id(0)
    buf[k] = (dot_nt(dqkv[0], w[...]) + first[0]).astype(BF)
    for i in range(C):
        @pl.when(k == i)
        def _():
            pltpu.make_async_copy(buf.at[i], outs[i], sems.at[i]).start()

    @pl.when(k == C - 1)
    def _():
        for i in range(C):
            pltpu.make_async_copy(buf.at[i], outs[i], sems.at[i]).wait()


def input_call(dqkv, w, first):
    C, R, W = dqkv.shape
    D = w.shape[0]
    return pl.pallas_call(
        functools.partial(input_kernel, C),
        name="input_grad",
        grid=(C,),
        out_shape=[jax.ShapeDtypeStruct((R, D), BF)] * C,
        in_specs=[
            pl.BlockSpec((1, R, W), lambda i: (i, 0, 0)),
            const_spec(w.shape),
            pl.BlockSpec((1, R, D), lambda i: (i, 0, 0)),
        ],
        out_specs=[ANY] * C,
        scratch_shapes=[pltpu.VMEM((C, R, D), BF), pltpu.SemaphoreType.DMA((C,))],
        compiler_params=pltpu.CompilerParams(vmem_limit_bytes=VMEM_LIMIT),
        cost_estimate=cost(2 * C * R * D * W, 15e6, 0),
    )(dqkv, w, first)


COLS = 384


def weight_kernel(F, pers, with_sums, meta, *refs):
    n = len(pers)
    lefts, rights = refs[:n], refs[n : 2 * n]
    refs = refs[2 * n :]
    sums, refs = (refs[0], refs[1:]) if with_sums else (None, refs)
    keep, send, tile = refs[:3]
    turned = refs[3:]
    D = lefts[0].shape[1]
    Dl = D // F
    b = pl.program_id(1)

    @pl.when((pl.program_id(0) == 0) & (b == 0))
    def _():
        for left, left_t in zip(lefts, turned):
            left_t[:D, :] = left[...].T
            left_t[D:, :] = jnp.ones((EXTRA, left.shape[0]), BF)

    start = 0
    for right, left_t, per in zip(rights, turned, pers):
        @pl.when((b >= start) & (b < start + per))
        def _():
            tile[...] = dot_nn(left_t[...], right[...]).astype(BF)
        start += per
    if with_sums:
        for j in range(D // COLS):
            @pl.when(b == j)
            def _():
                tile[D:, :] = sums[:, j * COLS : (j + 1) * COLS].astype(BF)
    f = meta[0]
    for high in range(F // 2):
        for bit, out in ((0, keep), (1, send)):
            row = pl.multiple_of((f ^ (2 * high + bit)) * Dl, 16)
            out[high, 0, :Dl] = tile[pl.ds(row, Dl), :]
            out[high, 0, Dl:] = tile[D:, :]


def weight_call(dims, meta, pairs, sums=None):
    F, C, T, ns, span, D = dims
    rows = C * ns * span
    pairs = [(left.reshape(rows, -1), right.reshape(rows, -1)) for left, right in pairs]
    pers = [right.shape[1] // T // COLS for _, right in pairs]
    width = sum(pers) * COLS
    out = jax.ShapeDtypeStruct((F // 2, T, D // F + EXTRA, width), BF)
    out_spec = pl.BlockSpec((F // 2, 1, D // F + EXTRA, COLS), lambda a, b: (0, a, 0, b))
    right_specs, start = [], 0
    for per in pers:
        right_specs.append(
            pl.BlockSpec(
                (rows, COLS),
                lambda a, b, per=per, start=start: (0, a * per + jnp.clip(b - start, 0, per - 1)),
            )
        )
        start += per
    return pl.pallas_call(
        functools.partial(weight_kernel, F, pers, sums is not None),
        name="weight_grad",
        grid=(T, sum(pers)),
        out_shape=[out, out],
        in_specs=[SMEM]
        + [const_spec(left.shape) for left, _ in pairs]
        + right_specs
        + ([] if sums is None else [const_spec(sums.shape)]),
        out_specs=[out_spec, out_spec],
        scratch_shapes=[pltpu.VMEM((D + EXTRA, COLS), BF)]
        + [pltpu.VMEM((D + EXTRA, rows), BF) for _ in pairs],
        compiler_params=pltpu.CompilerParams(vmem_limit_bytes=VMEM_LIMIT),
        cost_estimate=cost(
            2 * rows * D * width * T, 2 * (rows * (D + width * T) + D * width * T), 0
        ),
    )(
        meta,
        *[left for left, _ in pairs],
        *[right for _, right in pairs],
        *([] if sums is None else [sums]),
    )


def xor_pairs(count, mask):
    return [(i, i ^ mask) for i in range(count)]


def after(value, others):
    return lax.optimization_barrier((value, *others))[0]


def added(a, b):
    return (a.astype(F32) + b.astype(F32)).astype(BF)


def per_device(
    tokens_in, seq_lengths, query_weight, query_bias, key_weight, value_weight, value_bias,
    output_weight, output_bias, attn_gain, attn_shift, inner_weight, inner_bias, outer_weight,
    outer_bias, ffn_gain, ffn_shift, cotangent,
):
    F, C, T = (lax.axis_size(a) for a in ("fsdp", "ctx", "tp"))
    f, c, t = (lax.axis_index(a) for a in ("fsdp", "ctx", "tp"))
    S, span, D = tokens_in.shape
    ns = S // (C * T)
    Dl, half = D // F, D // T
    fhalf = inner_weight.shape[1]
    FF = fhalf * T
    R = ns * span
    dims = (F, C, T, ns, span, D)

    def to_sequences(array):
        out = []
        for k in range(C):
            piece = lax.dynamic_slice_in_dim(array, ((c ^ k) * T + t) * ns, ns, 0).reshape(R, D)
            out.append(lax.ppermute(piece, "ctx", xor_pairs(C, k)) if k else piece)
        return out

    def ctx_moved(piece, k):
        return lax.ppermute(piece, "ctx", xor_pairs(C, k)) if k else piece

    def tp_moved(piece):
        return [piece] + [lax.ppermute(piece, "tp", xor_pairs(T, dt)) for dt in range(1, T)]

    def to_slots(pieces, kind):
        out = lax.full((S, span, D), 0, kind)
        for k in range(C):
            for dt, got in enumerate(pieces[k]):
                out = lax.dynamic_update_slice_in_dim(
                    out, got.reshape(ns, span, D).astype(kind), ((c ^ k) * T + (t ^ dt)) * ns, 0
                )
        return out

    def swapped(array, axis, bit):
        return lax.ppermute(array, axis, xor_pairs(lax.axis_size(axis), bit))

    def chip_start(shard, across):
        held = shard[None]
        for axis, bit in order_of(F, T, across)[:-1]:
            held = jnp.concatenate([held, swapped(held, axis, bit)], axis=0)
        return held

    def chip_end(held, across):
        axis, bit = order_of(F, T, across)[-1]
        return swapped(held, axis, bit)

    def both_cores(held, got):
        return [held, got, swapped(held, "fsdp", 1), swapped(got, "fsdp", 1)]

    def spread(array, width):
        rows, part = array.shape
        owner = lax.broadcasted_iota(jnp.int32, (rows, part * F), 1) // part
        return jnp.where(owner == f, jnp.tile(array, (1, F)), jnp.zeros((), BF)).reshape(-1, width)

    x_pieces = to_sequences(tokens_in)
    vectors = jnp.stack([output_bias, attn_gain, attn_shift, outer_bias, ffn_gain, ffn_shift])
    small = [
        spread(query_bias, half), spread(value_bias, half), spread(inner_bias, fhalf),
        spread(vectors, D),
    ]
    small = jnp.concatenate([jnp.pad(a, ((0, 0), (0, fhalf - a.shape[1]))) for a in small])
    small = jnp.pad(small, ((0, EXTRA - small.shape[0]), (0, 0)))
    low = jnp.concatenate([query_weight, key_weight], axis=1)
    high = jnp.concatenate([value_weight, output_weight.T], axis=1)
    low = chip_start(jnp.concatenate([low, small[:, :D]], axis=0), False)
    high = chip_start(jnp.concatenate([high, small[:, D:]], axis=0), True)
    low = after(low, [x_pieces[k] for k in range(1, C, 2)])
    lows = both_cores(low, chip_end(low, False))
    highs = both_cores(high, chip_end(high, True))
    inner = chip_start(after(inner_weight, [lows[1], highs[1]]), False)
    outer = chip_start(after(outer_weight.T, [lows[1], highs[1]]), True)
    inner_got, outer_got = chip_end(inner, False), chip_end(outer, True)
    cot_pieces = to_sequences(after(cotangent, [*x_pieces, *lows, *highs]))
    lengths = lax.dynamic_slice_in_dim(seq_lengths, (c * T + t) * ns, ns, 0)
    meta = jnp.concatenate([jnp.stack([f, c]).astype(jnp.int32), lengths])

    x_all, qkv_w, qkv, e, linv, ctx = front_call(
        dims, after(meta, [inner, outer]), x_pieces, lows, highs
    )
    inners = both_cores(after(inner, [ctx]), inner_got)
    outers = both_cores(after(outer, [ctx]), outer_got)
    los, (first, dctx, nl, act, og, ig, ag, sums) = rows_call(
        dims, FF, meta, x_all, ctx.reshape(C, R, D), cot_pieces, lows + highs + inners + outers,
    )

    def core_sum(keep, send):
        return added(keep, lax.ppermute(send, "fsdp", xor_pairs(F, 1)))

    def y_sum(total):
        while total.shape[0] > 1:
            h = total.shape[0] // 2
            total = added(total[:h], lax.ppermute(total[h:], "fsdp", xor_pairs(F, 2 * h)))
        return total[0]

    def x_sum(total):
        while total.shape[0] > 1:
            h = total.shape[0] // 2
            total = added(total[:h], lax.ppermute(total[h:], "tp", xor_pairs(T, h)))
        return total[0]

    def ctx_scatter(total):
        part = total.shape[1] // C
        mine = 0.0
        for k in range(C):
            block = lax.dynamic_slice_in_dim(total, (c ^ k) * part, part, 1)
            mine += ctx_moved(block, k).astype(F32)
        return mine.astype(BF)

    def ctx_gather(mine, like):
        part = mine.shape[1]
        out = like
        for k in range(C):
            out = lax.dynamic_update_slice_in_dim(out, ctx_moved(mine, k), (c ^ k) * part, 1)
        return out.astype(F32)

    lo = {k: ctx_moved(los[k], k) for k in range(C)}
    lo_both = [tp_moved(lo[k]) for k in range(C)]
    outer_parts = weight_call(dims, meta, [(og, act)], sums)
    nl = after(nl, [lo[1], *lo_both[0]])
    inner_parts = weight_call(dims, meta, [(nl, ig)])
    outer_core = core_sum(*outer_parts)
    dctx = after(dctx, [outer_core, lo[3], *lo_both[1], *inner_parts])
    dqkv = back_call(dims, qkv, ctx, dctx.reshape(ctx.shape), e, linv)
    inner_core = core_sum(*inner_parts)
    outer_y = y_sum(outer_core)
    ag = after(ag, [inner_core, outer_y, lo[2], *lo_both[3], dqkv])
    qkv_parts = weight_call(dims, meta, [(x_all, dqkv), (ag, ctx)])
    outer_x = x_sum(outer_y)
    inner_y = y_sum(inner_core)
    first = after(first, [outer_x, *lo_both[2], *qkv_parts])
    ins = input_call(dqkv.reshape(C, R, 3 * D), qkv_w, first)
    qkv_core = core_sum(*qkv_parts)
    outer_part = ctx_scatter(outer_x)
    layer_out = to_slots(lo_both, BF)
    input_grad = to_slots([tp_moved(ctx_moved(ins[k], k)) for k in range(C)], F32)
    inner_x = x_sum(inner_y)
    qkv_x = x_sum(y_sum(qkv_core))
    outer_g = ctx_gather(outer_part, outer_x)
    inner_g = ctx_gather(ctx_scatter(inner_x), inner_x)
    qkv_g = ctx_gather(ctx_scatter(qkv_x), qkv_x)

    def own(row, shape):
        whole = row.reshape(shape[0], shape[1] * F)
        return lax.dynamic_slice_in_dim(whole, f * shape[1], shape[1], 1)

    vec_sums = lax.dynamic_slice_in_dim(outer_g[Dl : Dl + 6, :D], f * Dl, Dl, 1)

    return (
        layer_out,
        input_grad,
        qkv_g[:Dl, :half],
        own(qkv_g[Dl, :half], query_bias.shape),
        qkv_g[:Dl, half : 2 * half],
        qkv_g[:Dl, 2 * half : 3 * half],
        own(qkv_g[Dl, 2 * half : 3 * half], value_bias.shape),
        qkv_g[:Dl, 3 * half :].T,
        vec_sums[0],
        vec_sums[1],
        vec_sums[2],
        inner_g[:Dl],
        own(inner_g[Dl], inner_bias.shape),
        outer_g[:Dl].T,
        vec_sums[3],
        vec_sums[4],
        vec_sums[5],
    )


def solution(mesh):
    rows3, flat = P("fsdp", "ctx", None), P("fsdp")
    wide, tall = P("fsdp", "tp"), P("tp", "fsdp")
    params = (wide, tall, wide, wide, tall, tall, flat, flat, flat, wide, tall, tall, flat, flat, flat)
    return jax.shard_map(
        per_device,
        mesh=mesh,
        in_specs=(rows3, P("fsdp")) + params + (rows3,),
        out_specs=(rows3, rows3) + params,
        check_vma=False,
    )
```

```python
import functools
import math

import jax
import jax.numpy as jnp
from jax import lax
from jax.experimental import pallas as pl
from jax.experimental.pallas import tpu as pltpu
from jax.sharding import PartitionSpec as P

HD = 64
BF = jnp.bfloat16
F32 = jnp.float32
ANY = pl.BlockSpec(memory_space=pl.ANY)
SMEM = pl.BlockSpec(memory_space=pltpu.SMEM)
EXTRA = 16
VMEM_LIMIT = 60 * 1024 * 1024


def dot_nn(a, b):
    return lax.dot_general(a, b, (((1,), (0,)), ((), ())), preferred_element_type=F32)


def dot_nt(a, b):
    return lax.dot_general(a, b, (((1,), (1,)), ((), ())), preferred_element_type=F32)


def dot_tn(a, b):
    return lax.dot_general(a, b, (((0,), (0,)), ((), ())), preferred_element_type=F32)


def const_spec(shape):
    zeros = (0,) * len(shape)
    return pl.BlockSpec(shape, lambda *_: zeros)


def cost(flops, moved, exps=0):
    return pl.CostEstimate(flops=int(flops), bytes_accessed=int(moved), transcendentals=int(exps))


def head_columns(pair, half_cols):
    per = half_cols // 128
    return pl.multiple_of(pair // per * (3 * half_cols) + pair % per * 128, 128)


def order_of(F, T, across):
    chip = [("fsdp", 1 << b) for b in range(1, F.bit_length() - 1)]
    pair = [("tp", 1 << b) for b in range(T.bit_length() - 1)]
    return chip + pair if across else pair + chip


def stacks(F, T, across):
    held, out = [(0, 0)], []
    steps = order_of(F, T, across)
    for n, (axis, bit) in enumerate(steps):
        got = [(df ^ bit, dt) if axis == "fsdp" else (df, dt ^ bit) for df, dt in held]
        if n == len(steps) - 1:
            out += [held, got]
        held = held + got
    return out + [[(df ^ 1, dt) for df, dt in part] for part in out]


def pieces_of(refs, F, T, across):
    return {
        at: ref.at[i] for ref, part in zip(refs, stacks(F, T, across)) for i, at in enumerate(part)
    }


def front_kernel(dims, meta, *refs):
    F, C, T, ns, span, D = dims
    n_w = F * T
    n_a = len(stacks(F, T, False))
    xs, low_refs, high_refs = refs[:C], refs[C : C + n_a], refs[C + n_a : C + 2 * n_a]
    x_out, w_out, qkv, e_out, linv_out, ctx, small, bias, sems = refs[C + 2 * n_a :]
    step = pl.program_id(0)
    NP = D // 128
    L = C * span
    Dl, half = D // F, D // T
    f = meta[0]
    c = meta[1]

    @pl.when(step == 0)
    def _():
        copies = [pltpu.make_async_copy(xs[k], x_out.at[k], sems.at[k]) for k in range(C)]
        qk = pieces_of(low_refs, F, T, False)
        vo = pieces_of(high_refs, F, T, True)
        for df in range(F):
            for dt in range(T):
                n = df * T + dt
                rows = pl.ds(pl.multiple_of((f ^ df) * Dl, 16), Dl)
                start = dt * 3 * half
                copies += [
                    pltpu.make_async_copy(
                        qk[df, dt].at[pl.ds(0, Dl)], w_out.at[rows, pl.ds(start, 2 * half)],
                        sems.at[C + n]),
                    pltpu.make_async_copy(
                        vo[df, dt].at[pl.ds(0, Dl), pl.ds(0, half)],
                        w_out.at[rows, pl.ds(start + 2 * half, half)], sems.at[C + n_w + n]),
                    pltpu.make_async_copy(
                        qk[df, dt].at[pl.ds(Dl, EXTRA), pl.ds(0, half)], small.at[n],
                        sems.at[C + 2 * n_w + n]),
                ]
        for copy in copies:
            copy.start()
        for copy in copies:
            copy.wait()
        bias[...] = jnp.zeros_like(bias)
        for dt in range(T):
            part = sum(small[df * T + dt, :2, :].astype(F32) for df in range(F))
            bias[:, dt * 3 * half : dt * 3 * half + half] = part[0:1]
            bias[:, (dt * 3 + 2) * half : (dt * 3 + 3) * half] = part[1:2]

        def project(j, carry):
            cols = pl.ds(pl.multiple_of(j * 384, 128), 384)
            y = dot_nn(x_out[...].reshape(L * ns, D), w_out[:, cols]) + bias[:, cols]
            qkv[:, :, :, cols] = y.astype(BF).reshape(C, ns, span, 384)
            return carry

        lax.fori_loop(0, 3 * D // 384, project, 0)

    s = step // NP
    pair = step % NP
    q_col = head_columns(pair, half)
    q = qkv[:, s, :, pl.ds(q_col, 128)].reshape(L, 128)
    k = qkv[:, s, :, pl.ds(pl.multiple_of(q_col + half, 128), 128)].reshape(L, 128)
    v = qkv[:, s, :, pl.ds(pl.multiple_of(q_col + 2 * half, 128), 128)].reshape(L, 128)
    low = lax.broadcasted_iota(jnp.int32, (L, 128), 1) < HD
    zero = jnp.zeros((), BF)
    one = jnp.ones((L, 128), BF)
    lane = lax.broadcasted_iota(jnp.int32, (1, L), 1)
    pos = ((lane // span) ^ c) * span + lane % span
    mask = jnp.where(pos < meta[2 + s], 0.0, -1e30)
    values = []
    for h in range(2):
        mine = low if h == 0 else jnp.logical_not(low)
        scores = dot_nt(q, jnp.where(mine, k, zero)) * (math.log2(math.e) / math.sqrt(HD)) + mask
        top = jnp.max(scores, axis=-1, keepdims=True)
        e_out[0, h * L : (h + 1) * L, :] = jnp.exp2(scores - top).astype(BF)
        values.append(
            jnp.concatenate([jnp.where(mine, v, zero), jnp.where(mine, one, zero)], axis=1)
        )
    acc = dot_nn(e_out[0, :L, :], values[0]) + dot_nn(e_out[0, L:, :], values[1])
    linv = 1.0 / acc[:, 128:]
    linv_out[0] = linv
    ctx[:, s, :, pl.ds(pl.multiple_of(pair * 128, 128), 128)] = (
        (acc[:, :128] * linv).astype(BF).reshape(C, span, 128)
    )


def front_call(dims, meta, xs, lows, highs):
    F, C, T, ns, span, D = dims
    NP, L = D // 128, C * span
    rows = ns * span
    shapes = [
        jax.ShapeDtypeStruct((C, rows, D), BF),
        jax.ShapeDtypeStruct((D, 3 * D), BF),
        jax.ShapeDtypeStruct((C, ns, span, 3 * D), BF),
        jax.ShapeDtypeStruct((ns * NP, 2 * L, L), BF),
        jax.ShapeDtypeStruct((ns * NP, L, 128), F32),
        jax.ShapeDtypeStruct((C, ns, span, D), BF),
    ]
    return pl.pallas_call(
        functools.partial(front_kernel, dims),
        name="front",
        grid=(ns * NP,),
        out_shape=shapes,
        in_specs=[SMEM] + [ANY] * (C + len(lows) + len(highs)),
        out_specs=[
            const_spec(shapes[0].shape),
            const_spec(shapes[1].shape),
            const_spec(shapes[2].shape),
            pl.BlockSpec((1, 2 * L, L), lambda i: (i, 0, 0)),
            pl.BlockSpec((1, L, 128), lambda i: (i, 0, 0)),
            const_spec(shapes[5].shape),
        ],
        scratch_shapes=[
            pltpu.VMEM((F * T, EXTRA, D // T), BF),
            pltpu.VMEM((1, 3 * D), F32),
            pltpu.SemaphoreType.DMA((C + 3 * F * T,)),
        ],
        compiler_params=pltpu.CompilerParams(vmem_limit_bytes=VMEM_LIMIT),
        cost_estimate=cost(2 * L * ns * D * 3 * D, 40e6, ns * 12 * L * L),
    )(meta, *xs, *lows, *highs)


def normalised(values):
    centre = values - jnp.mean(values, axis=-1, keepdims=True)
    spread = jnp.mean(centre * centre, axis=-1, keepdims=True)
    rstd = lax.rsqrt(spread + 1e-12)
    return centre * rstd, rstd


def norm_back(grad, gain, xhat, rstd):
    scaled = grad * gain
    first = jnp.mean(scaled, axis=-1, keepdims=True)
    second = jnp.mean(scaled * xhat, axis=-1, keepdims=True)
    return rstd * (scaled - first - xhat * second)


def rows_kernel(dims, FF, meta, x_ref, ctx_ref, *refs):
    F, C, T, ns, span, D = dims
    n_w = F * T
    n_a = len(stacks(F, T, False))
    cots = refs[:C]
    qk, vo, inner, outer = (
        pieces_of(refs[C + i * n_a : C + (i + 1) * n_a], F, T, i % 2 == 1) for i in range(4)
    )
    refs = refs[C + 4 * n_a :]
    los = refs[:C]
    (
        first_out, dctx_out, nl_out, act_out, og_out, ig_out, ag_out, sums,
        cot_s, lo_s, wi, wo, wout, gp_s, small, vec, inner_bias, sems, out_sems,
    ) = refs[C:]
    k = pl.program_id(0)
    R = ns * span
    Dl, half, fhalf = D // F, D // T, FF // T
    f = meta[0]
    c = meta[1]

    def weight_copies():
        copies = []
        for df in range(F):
            row = pl.multiple_of((f ^ df) * Dl, 16)
            for dt in range(T):
                n = df * T + dt
                rows = pl.ds(row, Dl)
                copies.append((
                    pltpu.make_async_copy(
                        vo[df, dt].at[pl.ds(0, Dl), pl.ds(half, half)],
                        wo.at[rows, pl.ds(dt * half, half)], sems.at[n]),
                    pltpu.make_async_copy(
                        inner[df, dt],
                        wi.at[rows, pl.ds(dt * fhalf, fhalf)], sems.at[n_w + n]),
                    pltpu.make_async_copy(
                        outer[df, dt],
                        wout.at[rows, pl.ds(dt * fhalf, fhalf)], sems.at[2 * n_w + n]),
                ) + tuple(
                    pltpu.make_async_copy(
                        (qk if part == 0 else vo)[df, dt].at[pl.ds(Dl, EXTRA)],
                        small.at[n, :, pl.ds(part * D, D)], sems.at[(3 + part) * n_w + n])
                    for part in range(2)
                ))
        return copies

    def cot_copies():
        return [
            pltpu.make_async_copy(cots[i], cot_s.at[i], sems.at[5 * n_w + i]) for i in range(C)
        ]

    @pl.when(k == 0)
    def _():
        copies = weight_copies()
        for which in range(5):
            for group in copies:
                group[which].start()
        for copy in cot_copies():
            copy.start()
        sums[...] = jnp.zeros_like(sums)
        for which in range(5):
            for group in copies:
                group[which].wait()
        for copy in cot_copies():
            copy.wait()
        for dt in range(T):
            part = sum(small[df * T + dt, :EXTRA, :].astype(F32) for df in range(F))
            inner_bias[:, dt * fhalf : (dt + 1) * fhalf] = part[2:3]
            if dt == 0:
                vec[...] = part[3:9, :D]

    def add_sum(row, value):
        sums[row : row + 1, :] += jnp.sum(value, axis=0, keepdims=True)

    out_bias, gain1, shift1 = vec[0:1, :], vec[1:2, :], vec[2:3, :]
    outer_bias, gain2, shift2 = vec[3:4, :], vec[4:5, :], vec[5:6, :]
    ctx_low = ctx_ref[0]
    before = x_ref[0].astype(F32) + dot_nt(ctx_low, wo[...]) + out_bias
    xhat1, rstd1 = normalised(before)
    normed = xhat1 * gain1 + shift1
    nl = normed.astype(BF)
    nl_out[0] = nl
    root = math.sqrt(2.0 / math.pi)
    chunk = 768
    for j in range(FF // chunk):
        cols = slice(j * chunk, (j + 1) * chunk)
        pre = dot_nn(nl, wi[:, cols]) + inner_bias[:, cols]
        square = pre * pre
        th = jnp.tanh(pre * (root + (root * 0.044715) * square))
        hp = 0.5 + 0.5 * th
        act_out[0, :, cols] = (pre * hp).astype(BF)
        gp_s[:, cols] = hp + (0.5 * pre) * (1.0 - th * th) * (
            root + (3.0 * root * 0.044715) * square
        )
    before2 = normed + dot_nt(act_out[0], wout[...]) + outer_bias
    xhat2, rstd2 = normalised(before2)
    row = lax.broadcasted_iota(jnp.int32, (R, 1), 0)
    position = (c ^ k) * span + row % span
    length = jnp.full((R, 1), meta[2], jnp.int32)
    for s in range(1, ns):
        length = jnp.where(row >= s * span, meta[2 + s], length)
    live = (position < length).astype(F32)
    lo_s[k] = (live * (xhat2 * gain2 + shift2)).astype(BF)
    for i in range(C):
        @pl.when(k == i)
        def _():
            pltpu.make_async_copy(lo_s.at[i], los[i], out_sems.at[i]).start()
    grad = cot_s[k].astype(F32) * live
    add_sum(4, grad * xhat2)
    add_sum(5, grad)
    second = norm_back(grad, gain2, xhat2, rstd2)
    og = second.astype(BF)
    og_out[0] = og
    add_sum(3, og.astype(F32))
    for j in range(FF // chunk):
        cols = slice(j * chunk, (j + 1) * chunk)
        ig = (dot_nn(og, wout[:, cols]) * gp_s[:, cols]).astype(BF)
        ig_out[0, :, cols] = ig
    ngrad = dot_nt(ig_out[0], wi[...]) + second
    add_sum(1, ngrad * xhat1)
    add_sum(2, ngrad)
    first = norm_back(ngrad, gain1, xhat1, rstd1)
    first_out[0] = first
    ag = first.astype(BF)
    ag_out[0] = ag
    add_sum(0, ag.astype(F32))
    dctx_out[0] = dot_nn(ag, wo[...]).astype(BF)

    @pl.when(k == C - 1)
    def _():
        for i in range(C):
            pltpu.make_async_copy(lo_s.at[i], los[i], out_sems.at[i]).wait()


def rows_call(dims, FF, meta, x_all, ctx, cots, weights):
    F, C, T, ns, span, D = dims
    R = ns * span
    tile = lambda n: pl.BlockSpec((1, R, n), lambda i: (i, 0, 0))
    widths = [(D, F32), (D, BF), (D, BF), (FF, BF), (D, BF), (FF, BF), (D, BF)]
    out_shape = (
        [jax.ShapeDtypeStruct((R, D), BF)] * C
        + [jax.ShapeDtypeStruct((C, R, n), kind) for n, kind in widths]
        + [jax.ShapeDtypeStruct((EXTRA, D), F32)]
    )
    n_w = F * T
    outs = pl.pallas_call(
        functools.partial(rows_kernel, dims, FF),
        name="rows",
        grid=(C,),
        out_shape=out_shape,
        in_specs=[SMEM, tile(D), tile(D)]
        + [ANY] * (C + len(weights)),
        out_specs=[ANY] * C
        + [tile(n) for n, _ in widths]
        + [const_spec((EXTRA, D))],
        scratch_shapes=[
            pltpu.VMEM((C, R, D), BF),
            pltpu.VMEM((C, R, D), BF),
            pltpu.VMEM((D, FF), BF),
            pltpu.VMEM((D, D), BF),
            pltpu.VMEM((D, FF), BF),
            pltpu.VMEM((R, FF), F32),
            pltpu.VMEM((n_w, EXTRA, FF // T), BF),
            pltpu.VMEM((6, D), F32),
            pltpu.VMEM((1, FF), F32),
            pltpu.SemaphoreType.DMA((5 * n_w + C,)),
            pltpu.SemaphoreType.DMA((C,)),
        ],
        compiler_params=pltpu.CompilerParams(vmem_limit_bytes=VMEM_LIMIT),
        cost_estimate=cost(4 * C * R * D * (2 * FF + D), 50e6, C * R * FF),
    )(meta, x_all, ctx, *cots, *weights)
    return outs[:C], outs[C:]


def back_kernel(dims, qkv, ctx, dctx, e_ref, linv, out, ds_s):
    F, C, T, ns, span, D = dims
    step = pl.program_id(0)
    NP, L, half = D // 128, C * span, D // T
    s = step // NP
    pair = step % NP
    q_col = head_columns(pair, half)
    k_col = pl.multiple_of(q_col + half, 128)
    v_col = pl.multiple_of(q_col + 2 * half, 128)
    c_col = pl.multiple_of(pair * 128, 128)
    q = qkv[:, s, :, pl.ds(q_col, 128)].reshape(L, 128)
    k = qkv[:, s, :, pl.ds(k_col, 128)].reshape(L, 128)
    v = qkv[:, s, :, pl.ds(v_col, 128)].reshape(L, 128)
    grad = dctx[:, s, :, pl.ds(c_col, 128)].reshape(L, 128).astype(F32) * linv[0]
    grad_low = grad.astype(BF)
    product = grad_low.astype(F32) * ctx[:, s, :, pl.ds(c_col, 128)].reshape(L, 128).astype(F32)
    low = lax.broadcasted_iota(jnp.int32, (L, 128), 1) < HD
    zero = jnp.zeros((), BF)
    qs, ks, gs = [], [], []
    for h in range(2):
        mine = low if h == 0 else jnp.logical_not(low)
        row_dot = jnp.sum(jnp.where(mine, product, 0.0), axis=-1, keepdims=True)
        probs_grad = dot_nt(grad_low, jnp.where(mine, v, zero))
        e = e_ref[0, h * L : (h + 1) * L, :].astype(F32)
        ds_s[h * L : (h + 1) * L, :] = (e * (probs_grad - row_dot)).astype(BF)
        qs.append(jnp.where(mine, q, zero))
        ks.append(jnp.where(mine, k, zero))
        gs.append(jnp.where(mine, grad_low, zero))
    scale = 1.0 / math.sqrt(HD)
    dq = (dot_nn(ds_s[:L, :], ks[0]) + dot_nn(ds_s[L:, :], ks[1])) * scale
    dk = dot_tn(ds_s[...], jnp.concatenate(qs, axis=0)) * scale
    dv = dot_tn(e_ref[0], jnp.concatenate(gs, axis=0))
    out[:, s, :, pl.ds(q_col, 128)] = dq.astype(BF).reshape(C, span, 128)
    out[:, s, :, pl.ds(k_col, 128)] = dk.astype(BF).reshape(C, span, 128)
    out[:, s, :, pl.ds(v_col, 128)] = dv.astype(BF).reshape(C, span, 128)


def back_call(dims, qkv, ctx, dctx, e, linv):
    F, C, T, ns, span, D = dims
    NP, L = D // 128, C * span
    return pl.pallas_call(
        functools.partial(back_kernel, dims),
        name="back",
        grid=(ns * NP,),
        out_shape=jax.ShapeDtypeStruct(qkv.shape, BF),
        in_specs=[
            const_spec(qkv.shape),
            const_spec(ctx.shape),
            const_spec(dctx.shape),
            pl.BlockSpec((1, 2 * L, L), lambda i: (i, 0, 0)),
            pl.BlockSpec((1, L, 128), lambda i: (i, 0, 0)),
        ],
        out_specs=const_spec(qkv.shape),
        scratch_shapes=[pltpu.VMEM((2 * L, L), BF)],
        compiler_params=pltpu.CompilerParams(vmem_limit_bytes=VMEM_LIMIT),
        cost_estimate=cost(ns * NP * 16 * L * L * 128, 30e6, 0),
    )(qkv, ctx, dctx, e, linv)


def input_kernel(C, dqkv, w, first, *refs):
    outs, (buf, sems) = refs[:C], refs[C:]
    k = pl.program_id(0)
    buf[k] = (dot_nt(dqkv[0], w[...]) + first[0]).astype(BF)
    for i in range(C):
        @pl.when(k == i)
        def _():
            pltpu.make_async_copy(buf.at[i], outs[i], sems.at[i]).start()

    @pl.when(k == C - 1)
    def _():
        for i in range(C):
            pltpu.make_async_copy(buf.at[i], outs[i], sems.at[i]).wait()


def input_call(dqkv, w, first):
    C, R, W = dqkv.shape
    D = w.shape[0]
    return pl.pallas_call(
        functools.partial(input_kernel, C),
        name="input_grad",
        grid=(C,),
        out_shape=[jax.ShapeDtypeStruct((R, D), BF)] * C,
        in_specs=[
            pl.BlockSpec((1, R, W), lambda i: (i, 0, 0)),
            const_spec(w.shape),
            pl.BlockSpec((1, R, D), lambda i: (i, 0, 0)),
        ],
        out_specs=[ANY] * C,
        scratch_shapes=[pltpu.VMEM((C, R, D), BF), pltpu.SemaphoreType.DMA((C,))],
        compiler_params=pltpu.CompilerParams(vmem_limit_bytes=VMEM_LIMIT),
        cost_estimate=cost(2 * C * R * D * W, 15e6, 0),
    )(dqkv, w, first)


COLS = 384


def weight_kernel(F, pers, with_sums, meta, *refs):
    n = len(pers)
    lefts, rights = refs[:n], refs[n : 2 * n]
    refs = refs[2 * n :]
    sums, refs = (refs[0], refs[1:]) if with_sums else (None, refs)
    keep, send, tile = refs[:3]
    turned = refs[3:]
    D = lefts[0].shape[1]
    Dl = D // F
    b = pl.program_id(1)

    @pl.when((pl.program_id(0) == 0) & (b == 0))
    def _():
        for left, left_t in zip(lefts, turned):
            left_t[:D, :] = left[...].T
            left_t[D:, :] = jnp.ones((EXTRA, left.shape[0]), BF)

    start = 0
    for right, left_t, per in zip(rights, turned, pers):
        @pl.when((b >= start) & (b < start + per))
        def _():
            tile[...] = dot_nn(left_t[...], right[...]).astype(BF)
        start += per
    if with_sums:
        for j in range(D // COLS):
            @pl.when(b == j)
            def _():
                tile[D:, :] = sums[:, j * COLS : (j + 1) * COLS].astype(BF)
    f = meta[0]
    for high in range(F // 2):
        for bit, out in ((0, keep), (1, send)):
            row = pl.multiple_of((f ^ (2 * high + bit)) * Dl, 16)
            out[high, 0, :Dl] = tile[pl.ds(row, Dl), :]
            out[high, 0, Dl:] = tile[D:, :]


def weight_call(dims, meta, pairs, sums=None):
    F, C, T, ns, span, D = dims
    rows = C * ns * span
    pairs = [(left.reshape(rows, -1), right.reshape(rows, -1)) for left, right in pairs]
    pers = [right.shape[1] // T // COLS for _, right in pairs]
    width = sum(pers) * COLS
    out = jax.ShapeDtypeStruct((F // 2, T, D // F + EXTRA, width), BF)
    out_spec = pl.BlockSpec((F // 2, 1, D // F + EXTRA, COLS), lambda a, b: (0, a, 0, b))
    right_specs, start = [], 0
    for per in pers:
        right_specs.append(
            pl.BlockSpec(
                (rows, COLS),
                lambda a, b, per=per, start=start: (0, a * per + jnp.clip(b - start, 0, per - 1)),
            )
        )
        start += per
    return pl.pallas_call(
        functools.partial(weight_kernel, F, pers, sums is not None),
        name="weight_grad",
        grid=(T, sum(pers)),
        out_shape=[out, out],
        in_specs=[SMEM]
        + [const_spec(left.shape) for left, _ in pairs]
        + right_specs
        + ([] if sums is None else [const_spec(sums.shape)]),
        out_specs=[out_spec, out_spec],
        scratch_shapes=[pltpu.VMEM((D + EXTRA, COLS), BF)]
        + [pltpu.VMEM((D + EXTRA, rows), BF) for _ in pairs],
        compiler_params=pltpu.CompilerParams(vmem_limit_bytes=VMEM_LIMIT),
        cost_estimate=cost(
            2 * rows * D * width * T, 2 * (rows * (D + width * T) + D * width * T), 0
        ),
    )(
        meta,
        *[left for left, _ in pairs],
        *[right for _, right in pairs],
        *([] if sums is None else [sums]),
    )


def xor_pairs(count, mask):
    return [(i, i ^ mask) for i in range(count)]


def after(value, others):
    return lax.optimization_barrier((value, *others))[0]


def added(a, b):
    return (a.astype(F32) + b.astype(F32)).astype(BF)


def per_device(
    tokens_in, seq_lengths, query_weight, query_bias, key_weight, value_weight, value_bias,
    output_weight, output_bias, attn_gain, attn_shift, inner_weight, inner_bias, outer_weight,
    outer_bias, ffn_gain, ffn_shift, cotangent,
):
    F, C, T = (lax.axis_size(a) for a in ("fsdp", "ctx", "tp"))
    f, c, t = (lax.axis_index(a) for a in ("fsdp", "ctx", "tp"))
    S, span, D = tokens_in.shape
    ns = S // (C * T)
    Dl, half = D // F, D // T
    fhalf = inner_weight.shape[1]
    FF = fhalf * T
    R = ns * span
    dims = (F, C, T, ns, span, D)

    def to_sequences(array, chained):
        out, before = {}, []
        for k in sorted(range(C), key=lambda k: (k > 0, k % 2 == 0, k)):
            piece = lax.dynamic_slice_in_dim(array, ((c ^ k) * T + t) * ns, ns, 0).reshape(R, D)
            if k:
                piece = lax.ppermute(after(piece, before), "ctx", xor_pairs(C, k))
                before = [piece] if chained else []
            out[k] = piece
        return [out[k] for k in range(C)]

    def ctx_moved(piece, k):
        return lax.ppermute(piece, "ctx", xor_pairs(C, k)) if k else piece

    def tp_moved(piece):
        return [piece] + [lax.ppermute(piece, "tp", xor_pairs(T, dt)) for dt in range(1, T)]

    def to_slots(pieces, kind):
        out = lax.full((S, span, D), 0, kind)
        for k in range(C):
            for dt, got in enumerate(pieces[k]):
                out = lax.dynamic_update_slice_in_dim(
                    out, got.reshape(ns, span, D).astype(kind), ((c ^ k) * T + (t ^ dt)) * ns, 0
                )
        return out

    def swapped(array, axis, bit):
        return lax.ppermute(array, axis, xor_pairs(lax.axis_size(axis), bit))

    def chip_start(shard, across):
        held = shard[None]
        for axis, bit in order_of(F, T, across)[:-1]:
            held = jnp.concatenate([held, swapped(held, axis, bit)], axis=0)
        return held

    def chip_end(held, across):
        axis, bit = order_of(F, T, across)[-1]
        return swapped(held, axis, bit)

    def both_cores(held, got, others=()):
        near = swapped(after(held, others), "fsdp", 1)
        return [held, got, near, swapped(got, "fsdp", 1)]

    def spread(array, width):
        rows, part = array.shape
        owner = lax.broadcasted_iota(jnp.int32, (rows, part * F), 1) // part
        return jnp.where(owner == f, jnp.tile(array, (1, F)), jnp.zeros((), BF)).reshape(-1, width)

    x_pieces = to_sequences(tokens_in, True)
    vectors = jnp.stack([output_bias, attn_gain, attn_shift, outer_bias, ffn_gain, ffn_shift])
    small = [
        spread(query_bias, half), spread(value_bias, half), spread(inner_bias, fhalf),
        spread(vectors, D),
    ]
    small = jnp.concatenate([jnp.pad(a, ((0, 0), (0, fhalf - a.shape[1]))) for a in small])
    small = jnp.pad(small, ((0, EXTRA - small.shape[0]), (0, 0)))
    low = jnp.concatenate([query_weight, key_weight], axis=1)
    high = jnp.concatenate([value_weight, output_weight.T], axis=1)
    low = chip_start(jnp.concatenate([low, small[:, :D]], axis=0), False)
    high = chip_start(jnp.concatenate([high, small[:, D:]], axis=0), True)
    lows = both_cores(low, chip_end(after(low, x_pieces[1:2]), False))
    highs = both_cores(high, chip_end(after(high, x_pieces[1:2]), True))
    halfway = [lows[1], highs[1], *x_pieces[3:4]]
    inner = chip_start(after(inner_weight, halfway), False)
    outer = chip_start(after(outer_weight.T, halfway), True)
    inner_got = chip_end(after(inner, x_pieces[2:3]), False)
    outer_got = chip_end(after(outer, x_pieces[2:3]), True)
    cot_pieces = to_sequences(after(cotangent, [*x_pieces, *lows, *highs]), False)
    lengths = lax.dynamic_slice_in_dim(seq_lengths, (c * T + t) * ns, ns, 0)
    meta = jnp.concatenate([jnp.stack([f, c]).astype(jnp.int32), lengths])

    x_all, qkv_w, qkv, e, linv, ctx = front_call(
        dims, after(meta, [inner, outer]), x_pieces, lows, highs
    )
    inners = both_cores(inner, inner_got, [ctx, *cot_pieces])
    outers = both_cores(outer, outer_got, [ctx, *cot_pieces])
    los, (first, dctx, nl, act, og, inner_low, ag, sums) = rows_call(
        dims, FF, meta, x_all, ctx.reshape(C, R, D), cot_pieces, lows + highs + inners + outers,
    )

    def core_sum(keep, send):
        return added(keep, lax.ppermute(send, "fsdp", xor_pairs(F, 1)))

    def chip_sum(total, axis, dim):
        while total.shape[dim] > 1:
            h = total.shape[dim] // 2
            stay, go = jnp.split(total, 2, axis=dim)
            total = added(stay, swapped(go, axis, 2 * h if axis == "fsdp" else h))
        return total

    def y_sum(total):
        return chip_sum(total, "fsdp", 0)

    def x_sum(total):
        return chip_sum(total, "tp", 1)

    def ctx_scatter(total):
        part = total.shape[1] // C
        mine = 0.0
        for k in range(C):
            block = lax.dynamic_slice_in_dim(total, (c ^ k) * part, part, 1)
            mine += ctx_moved(block, k).astype(F32)
        return mine.astype(BF)

    def ctx_gather(mine, like):
        part = mine.shape[1]
        out = like
        for k in range(C):
            out = lax.dynamic_update_slice_in_dim(out, ctx_moved(mine, k), (c ^ k) * part, 1)
        return out.astype(F32)

    lo = {k: ctx_moved(los[k], k) for k in range(C)}
    lo_both = [tp_moved(lo[k]) for k in range(C)]
    dqkv = back_call(dims, qkv, ctx, dctx.reshape(ctx.shape), e, linv)
    first = after(first, [lo[1], lo[3], *lo_both[0]])
    ins = input_call(dqkv.reshape(C, R, 3 * D), qkv_w, first)
    ig = {k: ctx_moved(ins[k], k) for k in range(C)}
    ig_both = [tp_moved(ig[k]) for k in range(C)]
    og = after(og, [lo[2], *lo_both[1], *ins])
    outer_parts = weight_call(dims, meta, [(og, act)], sums)
    nl = after(nl, [ig[1], ig[3], *lo_both[3], *outer_parts])
    inner_parts = weight_call(dims, meta, [(nl, inner_low)])
    outer_core = core_sum(*outer_parts)
    ag = after(ag, [outer_core, *lo_both[2], *ig_both[0], *inner_parts])
    qkv_parts = weight_call(dims, meta, [(x_all, dqkv), (ag, ctx)])
    inner_core = core_sum(*inner_parts)
    outer_y = y_sum(outer_core)
    inner_half = x_sum(inner_core)
    keep, send = qkv_parts
    qkv_core = core_sum(after(keep, [inner_half, ig[2], *ig_both[1]]), send)
    layer_out = to_slots(lo_both, BF)
    input_grad = to_slots(ig_both, F32)
    inner_x = y_sum(inner_half)[0, 0]
    qkv_x = x_sum(y_sum(qkv_core))[0, 0]
    outer_x = x_sum(outer_y)[0, 0]
    outer_part = ctx_scatter(outer_x)
    outer_g = ctx_gather(outer_part, outer_x)
    inner_g = ctx_gather(ctx_scatter(inner_x), inner_x)
    qkv_g = ctx_gather(ctx_scatter(qkv_x), qkv_x)

    def own(row, shape):
        whole = row.reshape(shape[0], shape[1] * F)
        return lax.dynamic_slice_in_dim(whole, f * shape[1], shape[1], 1)

    vec_sums = lax.dynamic_slice_in_dim(outer_g[Dl : Dl + 6, :D], f * Dl, Dl, 1)

    return (
        layer_out,
        input_grad,
        qkv_g[:Dl, :half],
        own(qkv_g[Dl, :half], query_bias.shape),
        qkv_g[:Dl, half : 2 * half],
        qkv_g[:Dl, 2 * half : 3 * half],
        own(qkv_g[Dl, 2 * half : 3 * half], value_bias.shape),
        qkv_g[:Dl, 3 * half :].T,
        vec_sums[0],
        vec_sums[1],
        vec_sums[2],
        inner_g[:Dl],
        own(inner_g[Dl], inner_bias.shape),
        outer_g[:Dl].T,
        vec_sums[3],
        vec_sums[4],
        vec_sums[5],
    )


def solution(mesh):
    rows3, flat = P("fsdp", "ctx", None), P("fsdp")
    wide, tall = P("fsdp", "tp"), P("tp", "fsdp")
    params = (wide, tall, wide, wide, tall, tall, flat, flat, flat, wide, tall, tall, flat, flat, flat)
    return jax.shard_map(
        per_device,
        mesh=mesh,
        in_specs=(rows3, P("fsdp")) + params + (rows3,),
        out_specs=(rows3, rows3) + params,
        check_vma=False,
    )
```

```python
import functools
import math

import jax
import jax.numpy as jnp
from jax import lax
from jax.experimental import pallas as pl
from jax.experimental.pallas import tpu as pltpu
from jax.sharding import PartitionSpec as P

HD = 64
BF = jnp.bfloat16
F32 = jnp.float32
ANY = pl.BlockSpec(memory_space=pl.ANY)
SMEM = pl.BlockSpec(memory_space=pltpu.SMEM)
EXTRA = 16
VMEM_LIMIT = 60 * 1024 * 1024


def dot_nn(a, b):
    return lax.dot_general(a, b, (((1,), (0,)), ((), ())), preferred_element_type=F32)


def dot_nt(a, b):
    return lax.dot_general(a, b, (((1,), (1,)), ((), ())), preferred_element_type=F32)


def dot_tn(a, b):
    return lax.dot_general(a, b, (((0,), (0,)), ((), ())), preferred_element_type=F32)


def const_spec(shape):
    zeros = (0,) * len(shape)
    return pl.BlockSpec(shape, lambda *_: zeros)


def cost(flops, moved, exps=0):
    return pl.CostEstimate(flops=int(flops), bytes_accessed=int(moved), transcendentals=int(exps))


def head_columns(pair, half_cols):
    per = half_cols // 128
    return pl.multiple_of(pair // per * (3 * half_cols) + pair % per * 128, 128)


def order_of(F, T, across):
    chip = [("fsdp", 1 << b) for b in range(1, F.bit_length() - 1)]
    pair = [("tp", 1 << b) for b in range(T.bit_length() - 1)]
    return chip + pair if across else pair + chip


def stacks(F, T, across):
    held, out = [(0, 0)], []
    steps = order_of(F, T, across)
    for n, (axis, bit) in enumerate(steps):
        got = [(df ^ bit, dt) if axis == "fsdp" else (df, dt ^ bit) for df, dt in held]
        if n == len(steps) - 1:
            out += [held, got]
        held = held + got
    return out + [[(df ^ 1, dt) for df, dt in part] for part in out]


def pieces_of(refs, F, T, across):
    return {
        at: ref.at[i] for ref, part in zip(refs, stacks(F, T, across)) for i, at in enumerate(part)
    }


def front_kernel(dims, meta, *refs):
    F, C, T, ns, span, D = dims
    n_w = F * T
    n_a = len(stacks(F, T, False))
    xs, low_refs, high_refs = refs[:C], refs[C : C + n_a], refs[C + n_a : C + 2 * n_a]
    x_out, w_out, qkv, e_out, linv_out, ctx, small, bias, sems = refs[C + 2 * n_a :]
    step = pl.program_id(0)
    NP = D // 128
    L = C * span
    Dl, half = D // F, D // T
    f = meta[0]
    c = meta[1]

    @pl.when(step == 0)
    def _():
        copies = [pltpu.make_async_copy(xs[k], x_out.at[k], sems.at[k]) for k in range(C)]
        qk = pieces_of(low_refs, F, T, False)
        vo = pieces_of(high_refs, F, T, True)
        for df in range(F):
            for dt in range(T):
                n = df * T + dt
                rows = pl.ds(pl.multiple_of((f ^ df) * Dl, 16), Dl)
                start = dt * 3 * half
                copies += [
                    pltpu.make_async_copy(
                        qk[df, dt].at[pl.ds(0, Dl)], w_out.at[rows, pl.ds(start, 2 * half)],
                        sems.at[C + n]),
                    pltpu.make_async_copy(
                        vo[df, dt].at[pl.ds(0, Dl), pl.ds(0, half)],
                        w_out.at[rows, pl.ds(start + 2 * half, half)], sems.at[C + n_w + n]),
                    pltpu.make_async_copy(
                        qk[df, dt].at[pl.ds(Dl, EXTRA), pl.ds(0, half)], small.at[n],
                        sems.at[C + 2 * n_w + n]),
                ]
        for copy in copies:
            copy.start()
        for copy in copies:
            copy.wait()
        bias[...] = jnp.zeros_like(bias)
        for dt in range(T):
            part = sum(small[df * T + dt, :2, :].astype(F32) for df in range(F))
            bias[:, dt * 3 * half : dt * 3 * half + half] = part[0:1]
            bias[:, (dt * 3 + 2) * half : (dt * 3 + 3) * half] = part[1:2]

        def project(j, carry):
            cols = pl.ds(pl.multiple_of(j * 384, 128), 384)
            y = dot_nn(x_out[...].reshape(L * ns, D), w_out[:, cols]) + bias[:, cols]
            qkv[:, :, :, cols] = y.astype(BF).reshape(C, ns, span, 384)
            return carry

        lax.fori_loop(0, 3 * D // 384, project, 0)

    s = step // NP
    pair = step % NP
    q_col = head_columns(pair, half)
    q = qkv[:, s, :, pl.ds(q_col, 128)].reshape(L, 128)
    k = qkv[:, s, :, pl.ds(pl.multiple_of(q_col + half, 128), 128)].reshape(L, 128)
    v = qkv[:, s, :, pl.ds(pl.multiple_of(q_col + 2 * half, 128), 128)].reshape(L, 128)
    low = lax.broadcasted_iota(jnp.int32, (L, 128), 1) < HD
    zero = jnp.zeros((), BF)
    one = jnp.ones((L, 128), BF)
    lane = lax.broadcasted_iota(jnp.int32, (1, L), 1)
    pos = ((lane // span) ^ c) * span + lane % span
    mask = jnp.where(pos < meta[2 + s], 0.0, -1e30)
    values = []
    for h in range(2):
        mine = low if h == 0 else jnp.logical_not(low)
        scores = dot_nt(q, jnp.where(mine, k, zero)) * (math.log2(math.e) / math.sqrt(HD)) + mask
        top = jnp.max(scores, axis=-1, keepdims=True)
        e_out[0, h * L : (h + 1) * L, :] = jnp.exp2(scores - top).astype(BF)
        values.append(
            jnp.concatenate([jnp.where(mine, v, zero), jnp.where(mine, one, zero)], axis=1)
        )
    acc = dot_nn(e_out[0, :L, :], values[0]) + dot_nn(e_out[0, L:, :], values[1])
    linv = 1.0 / acc[:, 128:]
    linv_out[0] = linv
    ctx[:, s, :, pl.ds(pl.multiple_of(pair * 128, 128), 128)] = (
        (acc[:, :128] * linv).astype(BF).reshape(C, span, 128)
    )


def front_call(dims, meta, xs, lows, highs):
    F, C, T, ns, span, D = dims
    NP, L = D // 128, C * span
    rows = ns * span
    shapes = [
        jax.ShapeDtypeStruct((C, rows, D), BF),
        jax.ShapeDtypeStruct((D, 3 * D), BF),
        jax.ShapeDtypeStruct((C, ns, span, 3 * D), BF),
        jax.ShapeDtypeStruct((ns * NP, 2 * L, L), BF),
        jax.ShapeDtypeStruct((ns * NP, L, 128), F32),
        jax.ShapeDtypeStruct((C, ns, span, D), BF),
    ]
    return pl.pallas_call(
        functools.partial(front_kernel, dims),
        name="front",
        grid=(ns * NP,),
        out_shape=shapes,
        in_specs=[SMEM] + [ANY] * (C + len(lows) + len(highs)),
        out_specs=[
            const_spec(shapes[0].shape),
            const_spec(shapes[1].shape),
            const_spec(shapes[2].shape),
            pl.BlockSpec((1, 2 * L, L), lambda i: (i, 0, 0)),
            pl.BlockSpec((1, L, 128), lambda i: (i, 0, 0)),
            const_spec(shapes[5].shape),
        ],
        scratch_shapes=[
            pltpu.VMEM((F * T, EXTRA, D // T), BF),
            pltpu.VMEM((1, 3 * D), F32),
            pltpu.SemaphoreType.DMA((C + 3 * F * T,)),
        ],
        compiler_params=pltpu.CompilerParams(vmem_limit_bytes=VMEM_LIMIT),
        cost_estimate=cost(2 * L * ns * D * 3 * D, 40e6, ns * 12 * L * L),
    )(meta, *xs, *lows, *highs)


def normalised(values):
    centre = values - jnp.mean(values, axis=-1, keepdims=True)
    spread = jnp.mean(centre * centre, axis=-1, keepdims=True)
    rstd = lax.rsqrt(spread + 1e-12)
    return centre * rstd, rstd


def norm_back(grad, gain, xhat, rstd):
    scaled = grad * gain
    first = jnp.mean(scaled, axis=-1, keepdims=True)
    second = jnp.mean(scaled * xhat, axis=-1, keepdims=True)
    return rstd * (scaled - first - xhat * second)


def rows_kernel(dims, FF, meta, x_ref, ctx_ref, *refs):
    F, C, T, ns, span, D = dims
    n_w = F * T
    n_a = len(stacks(F, T, False))
    cots = refs[:C]
    qk, vo, inner, outer = (
        pieces_of(refs[C + i * n_a : C + (i + 1) * n_a], F, T, i % 2 == 1) for i in range(4)
    )
    refs = refs[C + 4 * n_a :]
    los = refs[:C]
    (
        first_out, dctx_out, nl_out, act_out, og_out, ig_out, ag_out, sums,
        cot_s, lo_s, wi, wo, wout, gp_s, small, vec, inner_bias, sems, out_sems,
    ) = refs[C:]
    k = pl.program_id(0)
    R = ns * span
    Dl, half, fhalf = D // F, D // T, FF // T
    f = meta[0]
    c = meta[1]

    def weight_copies():
        copies = []
        for df in range(F):
            row = pl.multiple_of((f ^ df) * Dl, 16)
            for dt in range(T):
                n = df * T + dt
                rows = pl.ds(row, Dl)
                copies.append((
                    pltpu.make_async_copy(
                        vo[df, dt].at[pl.ds(0, Dl), pl.ds(half, half)],
                        wo.at[rows, pl.ds(dt * half, half)], sems.at[n]),
                    pltpu.make_async_copy(
                        inner[df, dt],
                        wi.at[rows, pl.ds(dt * fhalf, fhalf)], sems.at[n_w + n]),
                    pltpu.make_async_copy(
                        outer[df, dt],
                        wout.at[rows, pl.ds(dt * fhalf, fhalf)], sems.at[2 * n_w + n]),
                ) + tuple(
                    pltpu.make_async_copy(
                        (qk if part == 0 else vo)[df, dt].at[pl.ds(Dl, EXTRA)],
                        small.at[n, :, pl.ds(part * D, D)], sems.at[(3 + part) * n_w + n])
                    for part in range(2)
                ))
        return copies

    def cot_copies():
        return [
            pltpu.make_async_copy(cots[i], cot_s.at[i], sems.at[5 * n_w + i]) for i in range(C)
        ]

    @pl.when(k == 0)
    def _():
        copies = weight_copies()
        for which in range(5):
            for group in copies:
                group[which].start()
        for copy in cot_copies():
            copy.start()
        sums[...] = jnp.zeros_like(sums)
        for which in range(5):
            for group in copies:
                group[which].wait()
        for copy in cot_copies():
            copy.wait()
        for dt in range(T):
            part = sum(small[df * T + dt, :EXTRA, :].astype(F32) for df in range(F))
            inner_bias[:, dt * fhalf : (dt + 1) * fhalf] = part[2:3]
            if dt == 0:
                vec[...] = part[3:9, :D]

    def add_sum(row, value):
        sums[row : row + 1, :] += jnp.sum(value, axis=0, keepdims=True)

    out_bias, gain1, shift1 = vec[0:1, :], vec[1:2, :], vec[2:3, :]
    outer_bias, gain2, shift2 = vec[3:4, :], vec[4:5, :], vec[5:6, :]
    ctx_low = ctx_ref[0]
    before = x_ref[0].astype(F32) + dot_nt(ctx_low, wo[...]) + out_bias
    xhat1, rstd1 = normalised(before)
    normed = xhat1 * gain1 + shift1
    nl = normed.astype(BF)
    nl_out[0] = nl
    root = math.sqrt(2.0 / math.pi)
    chunk = 768
    for j in range(FF // chunk):
        cols = slice(j * chunk, (j + 1) * chunk)
        pre = dot_nn(nl, wi[:, cols]) + inner_bias[:, cols]
        square = pre * pre
        th = jnp.tanh(pre * (root + (root * 0.044715) * square))
        hp = 0.5 + 0.5 * th
        act_out[0, :, cols] = (pre * hp).astype(BF)
        gp_s[:, cols] = hp + (0.5 * pre) * (1.0 - th * th) * (
            root + (3.0 * root * 0.044715) * square
        )
    before2 = normed + dot_nt(act_out[0], wout[...]) + outer_bias
    xhat2, rstd2 = normalised(before2)
    row = lax.broadcasted_iota(jnp.int32, (R, 1), 0)
    position = (c ^ k) * span + row % span
    length = jnp.full((R, 1), meta[2], jnp.int32)
    for s in range(1, ns):
        length = jnp.where(row >= s * span, meta[2 + s], length)
    live = (position < length).astype(F32)
    lo_s[k] = (live * (xhat2 * gain2 + shift2)).astype(BF)
    for i in range(C):
        @pl.when(k == i)
        def _():
            pltpu.make_async_copy(lo_s.at[i], los[i], out_sems.at[i]).start()
    grad = cot_s[k].astype(F32) * live
    add_sum(4, grad * xhat2)
    add_sum(5, grad)
    second = norm_back(grad, gain2, xhat2, rstd2)
    og = second.astype(BF)
    og_out[0] = og
    add_sum(3, og.astype(F32))
    for j in range(FF // chunk):
        cols = slice(j * chunk, (j + 1) * chunk)
        ig = (dot_nn(og, wout[:, cols]) * gp_s[:, cols]).astype(BF)
        ig_out[0, :, cols] = ig
    ngrad = dot_nt(ig_out[0], wi[...]) + second
    add_sum(1, ngrad * xhat1)
    add_sum(2, ngrad)
    first = norm_back(ngrad, gain1, xhat1, rstd1)
    first_out[0] = first
    ag = first.astype(BF)
    ag_out[0] = ag
    add_sum(0, ag.astype(F32))
    dctx_out[0] = dot_nn(ag, wo[...]).astype(BF)

    @pl.when(k == C - 1)
    def _():
        for i in range(C):
            pltpu.make_async_copy(lo_s.at[i], los[i], out_sems.at[i]).wait()


def rows_call(dims, FF, meta, x_all, ctx, cots, weights):
    F, C, T, ns, span, D = dims
    R = ns * span
    tile = lambda n: pl.BlockSpec((1, R, n), lambda i: (i, 0, 0))
    widths = [(D, F32), (D, BF), (D, BF), (FF, BF), (D, BF), (FF, BF), (D, BF)]
    out_shape = (
        [jax.ShapeDtypeStruct((R, D), BF)] * C
        + [jax.ShapeDtypeStruct((C, R, n), kind) for n, kind in widths]
        + [jax.ShapeDtypeStruct((EXTRA, D), F32)]
    )
    n_w = F * T
    outs = pl.pallas_call(
        functools.partial(rows_kernel, dims, FF),
        name="rows",
        grid=(C,),
        out_shape=out_shape,
        in_specs=[SMEM, tile(D), tile(D)]
        + [ANY] * (C + len(weights)),
        out_specs=[ANY] * C
        + [tile(n) for n, _ in widths]
        + [const_spec((EXTRA, D))],
        scratch_shapes=[
            pltpu.VMEM((C, R, D), BF),
            pltpu.VMEM((C, R, D), BF),
            pltpu.VMEM((D, FF), BF),
            pltpu.VMEM((D, D), BF),
            pltpu.VMEM((D, FF), BF),
            pltpu.VMEM((R, FF), F32),
            pltpu.VMEM((n_w, EXTRA, FF // T), BF),
            pltpu.VMEM((6, D), F32),
            pltpu.VMEM((1, FF), F32),
            pltpu.SemaphoreType.DMA((5 * n_w + C,)),
            pltpu.SemaphoreType.DMA((C,)),
        ],
        compiler_params=pltpu.CompilerParams(vmem_limit_bytes=VMEM_LIMIT),
        cost_estimate=cost(4 * C * R * D * (2 * FF + D), 50e6, C * R * FF),
    )(meta, x_all, ctx, *cots, *weights)
    return outs[:C], outs[C:]


def back_kernel(dims, qkv, ctx, dctx, e_ref, linv, out, ds_s):
    F, C, T, ns, span, D = dims
    step = pl.program_id(0)
    NP, L, half = D // 128, C * span, D // T
    s = step // NP
    pair = step % NP
    q_col = head_columns(pair, half)
    k_col = pl.multiple_of(q_col + half, 128)
    v_col = pl.multiple_of(q_col + 2 * half, 128)
    c_col = pl.multiple_of(pair * 128, 128)
    q = qkv[:, s, :, pl.ds(q_col, 128)].reshape(L, 128)
    k = qkv[:, s, :, pl.ds(k_col, 128)].reshape(L, 128)
    v = qkv[:, s, :, pl.ds(v_col, 128)].reshape(L, 128)
    grad = dctx[:, s, :, pl.ds(c_col, 128)].reshape(L, 128).astype(F32) * linv[0]
    grad_low = grad.astype(BF)
    product = grad_low.astype(F32) * ctx[:, s, :, pl.ds(c_col, 128)].reshape(L, 128).astype(F32)
    low = lax.broadcasted_iota(jnp.int32, (L, 128), 1) < HD
    zero = jnp.zeros((), BF)
    qs, ks, gs = [], [], []
    for h in range(2):
        mine = low if h == 0 else jnp.logical_not(low)
        row_dot = jnp.sum(jnp.where(mine, product, 0.0), axis=-1, keepdims=True)
        probs_grad = dot_nt(grad_low, jnp.where(mine, v, zero))
        e = e_ref[0, h * L : (h + 1) * L, :].astype(F32)
        ds_s[h * L : (h + 1) * L, :] = (e * (probs_grad - row_dot)).astype(BF)
        qs.append(jnp.where(mine, q, zero))
        ks.append(jnp.where(mine, k, zero))
        gs.append(jnp.where(mine, grad_low, zero))
    scale = 1.0 / math.sqrt(HD)
    dq = (dot_nn(ds_s[:L, :], ks[0]) + dot_nn(ds_s[L:, :], ks[1])) * scale
    dk = dot_tn(ds_s[...], jnp.concatenate(qs, axis=0)) * scale
    dv = dot_tn(e_ref[0], jnp.concatenate(gs, axis=0))
    out[:, s, :, pl.ds(q_col, 128)] = dq.astype(BF).reshape(C, span, 128)
    out[:, s, :, pl.ds(k_col, 128)] = dk.astype(BF).reshape(C, span, 128)
    out[:, s, :, pl.ds(v_col, 128)] = dv.astype(BF).reshape(C, span, 128)


def back_call(dims, qkv, ctx, dctx, e, linv):
    F, C, T, ns, span, D = dims
    NP, L = D // 128, C * span
    return pl.pallas_call(
        functools.partial(back_kernel, dims),
        name="back",
        grid=(ns * NP,),
        out_shape=jax.ShapeDtypeStruct(qkv.shape, BF),
        in_specs=[
            const_spec(qkv.shape),
            const_spec(ctx.shape),
            const_spec(dctx.shape),
            pl.BlockSpec((1, 2 * L, L), lambda i: (i, 0, 0)),
            pl.BlockSpec((1, L, 128), lambda i: (i, 0, 0)),
        ],
        out_specs=const_spec(qkv.shape),
        scratch_shapes=[pltpu.VMEM((2 * L, L), BF)],
        compiler_params=pltpu.CompilerParams(vmem_limit_bytes=VMEM_LIMIT),
        cost_estimate=cost(ns * NP * 16 * L * L * 128, 30e6, 0),
    )(qkv, ctx, dctx, e, linv)


def input_kernel(C, dqkv, w, first, *refs):
    outs, (buf, sems) = refs[:C], refs[C:]
    k = pl.program_id(0)
    buf[k] = (dot_nt(dqkv[0], w[...]) + first[0]).astype(BF)
    for i in range(C):
        @pl.when(k == i)
        def _():
            pltpu.make_async_copy(buf.at[i], outs[i], sems.at[i]).start()

    @pl.when(k == C - 1)
    def _():
        for i in range(C):
            pltpu.make_async_copy(buf.at[i], outs[i], sems.at[i]).wait()


def input_call(dqkv, w, first):
    C, R, W = dqkv.shape
    D = w.shape[0]
    return pl.pallas_call(
        functools.partial(input_kernel, C),
        name="input_grad",
        grid=(C,),
        out_shape=[jax.ShapeDtypeStruct((R, D), BF)] * C,
        in_specs=[
            pl.BlockSpec((1, R, W), lambda i: (i, 0, 0)),
            const_spec(w.shape),
            pl.BlockSpec((1, R, D), lambda i: (i, 0, 0)),
        ],
        out_specs=[ANY] * C,
        scratch_shapes=[pltpu.VMEM((C, R, D), BF), pltpu.SemaphoreType.DMA((C,))],
        compiler_params=pltpu.CompilerParams(vmem_limit_bytes=VMEM_LIMIT),
        cost_estimate=cost(2 * C * R * D * W, 15e6, 0),
    )(dqkv, w, first)


COLS = 384


def weight_kernel(F, pers, with_sums, meta, *refs):
    n = len(pers)
    lefts, rights = refs[:n], refs[n : 2 * n]
    refs = refs[2 * n :]
    sums, refs = (refs[0], refs[1:]) if with_sums else (None, refs)
    keep, send, tile = refs[:3]
    turned = refs[3:]
    D = lefts[0].shape[1]
    Dl = D // F
    b = pl.program_id(1)

    @pl.when((pl.program_id(0) == 0) & (b == 0))
    def _():
        for left, left_t in zip(lefts, turned):
            left_t[:D, :] = left[...].T
            left_t[D:, :] = jnp.ones((EXTRA, left.shape[0]), BF)

    start = 0
    for right, left_t, per in zip(rights, turned, pers):
        @pl.when((b >= start) & (b < start + per))
        def _():
            tile[...] = dot_nn(left_t[...], right[...]).astype(BF)
        start += per
    if with_sums:
        for j in range(D // COLS):
            @pl.when(b == j)
            def _():
                tile[D:, :] = sums[:, j * COLS : (j + 1) * COLS].astype(BF)
    f = meta[0]
    for high in range(F // 2):
        for bit, out in ((0, keep), (1, send)):
            row = pl.multiple_of((f ^ (2 * high + bit)) * Dl, 16)
            out[high, 0, :Dl] = tile[pl.ds(row, Dl), :]
            out[high, 0, Dl:] = tile[D:, :]


def weight_call(dims, meta, pairs, sums=None):
    F, C, T, ns, span, D = dims
    rows = C * ns * span
    pairs = [(left.reshape(rows, -1), right.reshape(rows, -1)) for left, right in pairs]
    pers = [right.shape[1] // T // COLS for _, right in pairs]
    width = sum(pers) * COLS
    out = jax.ShapeDtypeStruct((F // 2, T, D // F + EXTRA, width), BF)
    out_spec = pl.BlockSpec((F // 2, 1, D // F + EXTRA, COLS), lambda a, b: (0, a, 0, b))
    right_specs, start = [], 0
    for per in pers:
        right_specs.append(
            pl.BlockSpec(
                (rows, COLS),
                lambda a, b, per=per, start=start: (0, a * per + jnp.clip(b - start, 0, per - 1)),
            )
        )
        start += per
    return pl.pallas_call(
        functools.partial(weight_kernel, F, pers, sums is not None),
        name="weight_grad",
        grid=(T, sum(pers)),
        out_shape=[out, out],
        in_specs=[SMEM]
        + [const_spec(left.shape) for left, _ in pairs]
        + right_specs
        + ([] if sums is None else [const_spec(sums.shape)]),
        out_specs=[out_spec, out_spec],
        scratch_shapes=[pltpu.VMEM((D + EXTRA, COLS), BF)]
        + [pltpu.VMEM((D + EXTRA, rows), BF) for _ in pairs],
        compiler_params=pltpu.CompilerParams(vmem_limit_bytes=VMEM_LIMIT),
        cost_estimate=cost(
            2 * rows * D * width * T, 2 * (rows * (D + width * T) + D * width * T), 0
        ),
    )(
        meta,
        *[left for left, _ in pairs],
        *[right for _, right in pairs],
        *([] if sums is None else [sums]),
    )


def xor_pairs(count, mask):
    return [(i, i ^ mask) for i in range(count)]


def after(value, others):
    return lax.optimization_barrier((value, *others))[0]


def added(a, b):
    return (a.astype(F32) + b.astype(F32)).astype(BF)


def per_device(
    tokens_in, seq_lengths, query_weight, query_bias, key_weight, value_weight, value_bias,
    output_weight, output_bias, attn_gain, attn_shift, inner_weight, inner_bias, outer_weight,
    outer_bias, ffn_gain, ffn_shift, cotangent,
):
    F, C, T = (lax.axis_size(a) for a in ("fsdp", "ctx", "tp"))
    f, c, t = (lax.axis_index(a) for a in ("fsdp", "ctx", "tp"))
    S, span, D = tokens_in.shape
    ns = S // (C * T)
    Dl, half = D // F, D // T
    fhalf = inner_weight.shape[1]
    FF = fhalf * T
    R = ns * span
    dims = (F, C, T, ns, span, D)

    def sequence_pieces(array):
        return [
            lax.dynamic_slice_in_dim(array, ((c ^ k) * T + t) * ns, ns, 0).reshape(R, D)
            for k in range(C)
        ]

    def ctx_first(pieces):
        if C != 4:
            return [ctx_moved(piece, k) for k, piece in enumerate(pieces)][1:]
        h = R // 2
        up = jnp.concatenate([pieces[1], pieces[2][:h]], axis=0)
        down = jnp.concatenate([pieces[3], pieces[2][h:]], axis=0)
        return [ctx_moved(up, 1), ctx_moved(down, 3)]

    def ctx_second(own, got):
        if C != 4:
            return [own, *got], list(got)
        up, down = got
        raw = [ctx_moved(up[R:], 3), ctx_moved(down[R:], 1)]
        return [own, up[:R], jnp.concatenate(raw, axis=0), down[:R]], raw

    def ctx_moved(piece, k):
        return lax.ppermute(piece, "ctx", xor_pairs(C, k)) if k else piece

    def tp_moved(pieces):
        both = jnp.concatenate(pieces, axis=0)
        return [both] + [lax.ppermute(both, "tp", xor_pairs(T, dt)) for dt in range(1, T)]

    def to_slots(groups, kind):
        out = lax.full((S, span, D), 0, kind)
        pieces = {}
        for ks, group in groups:
            for dt, merged in enumerate(group):
                for i, k in enumerate(ks):
                    pieces[k, dt] = merged[i * R : (i + 1) * R]
        for k in range(C):
            for dt in range(T):
                got = pieces[k, dt]
                out = lax.dynamic_update_slice_in_dim(
                    out, got.reshape(ns, span, D).astype(kind), ((c ^ k) * T + (t ^ dt)) * ns, 0
                )
        return out

    def swapped(array, axis, bit):
        return lax.ppermute(array, axis, xor_pairs(lax.axis_size(axis), bit))

    def chip_start(shard, across):
        held = shard[None]
        for axis, bit in order_of(F, T, across)[:-1]:
            held = jnp.concatenate([held, swapped(held, axis, bit)], axis=0)
        return held

    def chip_end(held, across):
        axis, bit = order_of(F, T, across)[-1]
        return swapped(held, axis, bit)

    def both_cores(held, got, others=()):
        near = swapped(after(held, others), "fsdp", 1)
        return [held, got, near, swapped(got, "fsdp", 1)]

    def spread(array, width):
        rows, part = array.shape
        owner = lax.broadcasted_iota(jnp.int32, (rows, part * F), 1) // part
        return jnp.where(owner == f, jnp.tile(array, (1, F)), jnp.zeros((), BF)).reshape(-1, width)

    x_pieces = sequence_pieces(tokens_in)
    x_got = ctx_first(x_pieces)
    vectors = jnp.stack([output_bias, attn_gain, attn_shift, outer_bias, ffn_gain, ffn_shift])
    small = [
        spread(query_bias, half), spread(value_bias, half), spread(inner_bias, fhalf),
        spread(vectors, D),
    ]
    small = jnp.concatenate([jnp.pad(a, ((0, 0), (0, fhalf - a.shape[1]))) for a in small])
    small = jnp.pad(small, ((0, EXTRA - small.shape[0]), (0, 0)))
    low = jnp.concatenate([query_weight, key_weight], axis=1)
    high = jnp.concatenate([value_weight, output_weight.T], axis=1)
    low = chip_start(jnp.concatenate([low, small[:, :D]], axis=0), False)
    high = chip_start(jnp.concatenate([high, small[:, D:]], axis=0), True)
    lows = both_cores(low, chip_end(low, False))
    highs = both_cores(high, chip_end(high, True))
    halfway = [lows[1], highs[1], *x_got]
    x_pieces, x_raw = ctx_second(x_pieces[0], x_got)
    inner = chip_start(after(inner_weight, halfway), False)
    outer = chip_start(after(outer_weight.T, halfway), True)
    inner_got = chip_end(after(inner, x_raw), False)
    outer_got = chip_end(after(outer, x_raw), True)
    cot_pieces = sequence_pieces(after(cotangent, [*x_raw, *lows, *highs]))
    cot_got = ctx_first(cot_pieces)
    lengths = lax.dynamic_slice_in_dim(seq_lengths, (c * T + t) * ns, ns, 0)
    meta = jnp.concatenate([jnp.stack([f, c]).astype(jnp.int32), lengths])

    x_all, qkv_w, qkv, e, linv, ctx = front_call(
        dims, after(meta, [inner, outer]), x_pieces, lows, highs
    )
    inners = both_cores(inner, inner_got, [ctx, *cot_got])
    outers = both_cores(outer, outer_got, [ctx, *cot_got])
    cot_pieces, _ = ctx_second(cot_pieces[0], cot_got)
    los, (first, dctx, nl, act, og, inner_low, ag, sums) = rows_call(
        dims, FF, meta, x_all, ctx.reshape(C, R, D), cot_pieces, lows + highs + inners + outers,
    )

    def core_sum(keep, send):
        return added(keep, lax.ppermute(send, "fsdp", xor_pairs(F, 1)))

    def chip_sum(total, axis, dim):
        while total.shape[dim] > 1:
            h = total.shape[dim] // 2
            stay, go = jnp.split(total, 2, axis=dim)
            total = added(stay, swapped(go, axis, 2 * h if axis == "fsdp" else h))
        return total

    def y_sum(total):
        return chip_sum(total, "fsdp", 0)

    def x_sum(total):
        return chip_sum(total, "tp", 1)

    def ctx_scatter(total):
        part = total.shape[1] // C
        mine = 0.0
        for k in range(C):
            block = lax.dynamic_slice_in_dim(total, (c ^ k) * part, part, 1)
            mine += ctx_moved(block, k).astype(F32)
        return mine.astype(BF)

    def ctx_gather(mine, like):
        part = mine.shape[1]
        out = like
        for k in range(C):
            out = lax.dynamic_update_slice_in_dim(out, ctx_moved(mine, k), (c ^ k) * part, 1)
        return out.astype(F32)

    outer_parts = weight_call(dims, meta, [(og, act)], sums)
    inner_parts = weight_call(dims, meta, [(after(nl, outer_parts), inner_low)])
    outer_core = core_sum(*outer_parts)
    dctx = after(dctx, [outer_core, *inner_parts])
    dqkv = back_call(dims, qkv, ctx, dctx.reshape(ctx.shape), e, linv)
    lo_got = ctx_first(los)
    own_lo = tp_moved(los[:1])
    inner_core = core_sum(*inner_parts)
    outer_y = y_sum(outer_core)
    first = after(first, [inner_core, outer_y, *lo_got, *own_lo])
    ins = input_call(dqkv.reshape(C, R, 3 * D), qkv_w, first)
    los, lo_raw = ctx_second(los[0], [after(got, [dqkv]) for got in lo_got])
    outer_x = x_sum(outer_y)
    inner_y = y_sum(after(inner_core, [outer_y]))
    ag = after(ag, [*lo_raw, *ins])
    qkv_parts = weight_call(dims, meta, [(x_all, dqkv), (ag, ctx)])
    ig_got = ctx_first(ins)
    far_lo = tp_moved(los[1:])
    keep, send = qkv_parts
    qkv_core = core_sum(keep, after(send, [outer_x, inner_y, *ig_got]))
    ig, ig_raw = ctx_second(ins[0], ig_got)
    outer_x = after(outer_x[0, 0], [qkv_core, *ig_raw])
    outer_part = ctx_scatter(outer_x)
    qkv_y = after(y_sum(qkv_core), [outer_part, *ig_raw])
    ig_both = tp_moved(after(tuple(ig[:2]), [outer_part]) + tuple(ig[2:]))
    inner_x = after(x_sum(after(inner_y, [outer_part]))[0, 0], [qkv_y])
    inner_part = ctx_scatter(inner_x)
    outer_g = ctx_gather(after(outer_part, [qkv_y]), outer_x)
    qkv_x = after(x_sum(qkv_y)[0, 0], [outer_g, inner_part])
    own_lo, far_lo = (after(tuple(part), [qkv_core]) for part in (own_lo, far_lo))
    layer_out = to_slots([([0], own_lo), (list(range(1, C)), far_lo)], BF)
    input_grad = to_slots([(list(range(C)), after(tuple(ig_both), [qkv_x]))], F32)
    inner_g = ctx_gather(inner_part, inner_x)
    qkv_g = ctx_gather(ctx_scatter(qkv_x), qkv_x)

    def own(row, shape):
        whole = row.reshape(shape[0], shape[1] * F)
        return lax.dynamic_slice_in_dim(whole, f * shape[1], shape[1], 1)

    vec_sums = lax.dynamic_slice_in_dim(outer_g[Dl : Dl + 6, :D], f * Dl, Dl, 1)

    return (
        layer_out,
        input_grad,
        qkv_g[:Dl, :half],
        own(qkv_g[Dl, :half], query_bias.shape),
        qkv_g[:Dl, half : 2 * half],
        qkv_g[:Dl, 2 * half : 3 * half],
        own(qkv_g[Dl, 2 * half : 3 * half], value_bias.shape),
        qkv_g[:Dl, 3 * half :].T,
        vec_sums[0],
        vec_sums[1],
        vec_sums[2],
        inner_g[:Dl],
        own(inner_g[Dl], inner_bias.shape),
        outer_g[:Dl].T,
        vec_sums[3],
        vec_sums[4],
        vec_sums[5],
    )


def solution(mesh):
    rows3, flat = P("fsdp", "ctx", None), P("fsdp")
    wide, tall = P("fsdp", "tp"), P("tp", "fsdp")
    params = (wide, tall, wide, wide, tall, tall, flat, flat, flat, wide, tall, tall, flat, flat, flat)
    return jax.shard_map(
        per_device,
        mesh=mesh,
        in_specs=(rows3, P("fsdp")) + params + (rows3,),
        out_specs=(rows3, rows3) + params,
        check_vma=False,
    )
```

```python
import functools
import math

import jax
import jax.numpy as jnp
from jax import lax
from jax.experimental import pallas as pl
from jax.experimental.pallas import tpu as pltpu
from jax.sharding import PartitionSpec as P

HD = 64
BF = jnp.bfloat16
F32 = jnp.float32
ANY = pl.BlockSpec(memory_space=pl.ANY)
SMEM = pl.BlockSpec(memory_space=pltpu.SMEM)
EXTRA = 16
VMEM_LIMIT = 60 * 1024 * 1024


def dot_nn(a, b):
    return lax.dot_general(a, b, (((1,), (0,)), ((), ())), preferred_element_type=F32)


def dot_nt(a, b):
    return lax.dot_general(a, b, (((1,), (1,)), ((), ())), preferred_element_type=F32)


def dot_tn(a, b):
    return lax.dot_general(a, b, (((0,), (0,)), ((), ())), preferred_element_type=F32)


def const_spec(shape):
    zeros = (0,) * len(shape)
    return pl.BlockSpec(shape, lambda *_: zeros)


def cost(flops, moved, exps=0):
    return pl.CostEstimate(flops=int(flops), bytes_accessed=int(moved), transcendentals=int(exps))


def head_columns(pair, half_cols):
    per = half_cols // 128
    return pl.multiple_of(pair // per * (3 * half_cols) + pair % per * 128, 128)


def order_of(F, T, across):
    chip = [("fsdp", 1 << b) for b in range(1, F.bit_length() - 1)]
    pair = [("tp", 1 << b) for b in range(T.bit_length() - 1)]
    return chip + pair if across else pair + chip


def stacks(F, T, across):
    held, out = [(0, 0)], []
    steps = order_of(F, T, across)
    for n, (axis, bit) in enumerate(steps):
        got = [(df ^ bit, dt) if axis == "fsdp" else (df, dt ^ bit) for df, dt in held]
        if n == len(steps) - 1:
            out += [held, got]
        held = held + got
    return out + [[(df ^ 1, dt) for df, dt in part] for part in out]


def pieces_of(refs, F, T, across):
    return {
        at: ref.at[i] for ref, part in zip(refs, stacks(F, T, across)) for i, at in enumerate(part)
    }


def front_kernel(dims, meta, *refs):
    F, C, T, ns, span, D = dims
    n_w = F * T
    n_a = len(stacks(F, T, False))
    xs, low_refs, high_refs = refs[:C], refs[C : C + n_a], refs[C + n_a : C + 2 * n_a]
    x_out, w_out, qkv, e_out, linv_out, ctx, small, bias, sems = refs[C + 2 * n_a :]
    step = pl.program_id(0)
    NP = D // 128
    L = C * span
    Dl, half = D // F, D // T
    f = meta[0]
    c = meta[1]

    @pl.when(step == 0)
    def _():
        copies = [pltpu.make_async_copy(xs[k], x_out.at[k], sems.at[k]) for k in range(C)]
        qk = pieces_of(low_refs, F, T, False)
        vo = pieces_of(high_refs, F, T, True)
        for df in range(F):
            for dt in range(T):
                n = df * T + dt
                rows = pl.ds(pl.multiple_of((f ^ df) * Dl, 16), Dl)
                start = dt * 3 * half
                copies += [
                    pltpu.make_async_copy(
                        qk[df, dt].at[pl.ds(0, Dl)], w_out.at[rows, pl.ds(start, 2 * half)],
                        sems.at[C + n]),
                    pltpu.make_async_copy(
                        vo[df, dt].at[pl.ds(0, Dl), pl.ds(0, half)],
                        w_out.at[rows, pl.ds(start + 2 * half, half)], sems.at[C + n_w + n]),
                    pltpu.make_async_copy(
                        qk[df, dt].at[pl.ds(Dl, EXTRA), pl.ds(0, half)], small.at[n],
                        sems.at[C + 2 * n_w + n]),
                ]
        for copy in copies:
            copy.start()
        for copy in copies:
            copy.wait()
        bias[...] = jnp.zeros_like(bias)
        for dt in range(T):
            part = sum(small[df * T + dt, :2, :].astype(F32) for df in range(F))
            bias[:, dt * 3 * half : dt * 3 * half + half] = part[0:1]
            bias[:, (dt * 3 + 2) * half : (dt * 3 + 3) * half] = part[1:2]

        def project(j, carry):
            cols = pl.ds(pl.multiple_of(j * 384, 128), 384)
            y = dot_nn(x_out[...].reshape(L * ns, D), w_out[:, cols]) + bias[:, cols]
            qkv[:, :, :, cols] = y.astype(BF).reshape(C, ns, span, 384)
            return carry

        lax.fori_loop(0, 3 * D // 384, project, 0)

    s = step // NP
    pair = step % NP
    q_col = head_columns(pair, half)
    q = qkv[:, s, :, pl.ds(q_col, 128)].reshape(L, 128)
    k = qkv[:, s, :, pl.ds(pl.multiple_of(q_col + half, 128), 128)].reshape(L, 128)
    v = qkv[:, s, :, pl.ds(pl.multiple_of(q_col + 2 * half, 128), 128)].reshape(L, 128)
    low = lax.broadcasted_iota(jnp.int32, (L, 128), 1) < HD
    zero = jnp.zeros((), BF)
    one = jnp.ones((L, 128), BF)
    lane = lax.broadcasted_iota(jnp.int32, (1, L), 1)
    pos = ((lane // span) ^ c) * span + lane % span
    mask = jnp.where(pos < meta[2 + s], 0.0, -1e30)
    values = []
    for h in range(2):
        mine = low if h == 0 else jnp.logical_not(low)
        scores = dot_nt(q, jnp.where(mine, k, zero)) * (math.log2(math.e) / math.sqrt(HD)) + mask
        top = jnp.max(scores, axis=-1, keepdims=True)
        e_out[0, h * L : (h + 1) * L, :] = jnp.exp2(scores - top).astype(BF)
        values.append(
            jnp.concatenate([jnp.where(mine, v, zero), jnp.where(mine, one, zero)], axis=1)
        )
    acc = dot_nn(e_out[0, :L, :], values[0]) + dot_nn(e_out[0, L:, :], values[1])
    linv = 1.0 / acc[:, 128:]
    linv_out[0] = linv
    ctx[:, s, :, pl.ds(pl.multiple_of(pair * 128, 128), 128)] = (
        (acc[:, :128] * linv).astype(BF).reshape(C, span, 128)
    )


def front_call(dims, meta, xs, lows, highs):
    F, C, T, ns, span, D = dims
    NP, L = D // 128, C * span
    rows = ns * span
    shapes = [
        jax.ShapeDtypeStruct((C, rows, D), BF),
        jax.ShapeDtypeStruct((D, 3 * D), BF),
        jax.ShapeDtypeStruct((C, ns, span, 3 * D), BF),
        jax.ShapeDtypeStruct((ns * NP, 2 * L, L), BF),
        jax.ShapeDtypeStruct((ns * NP, L, 128), F32),
        jax.ShapeDtypeStruct((C, ns, span, D), BF),
    ]
    return pl.pallas_call(
        functools.partial(front_kernel, dims),
        name="front",
        grid=(ns * NP,),
        out_shape=shapes,
        in_specs=[SMEM] + [ANY] * (C + len(lows) + len(highs)),
        out_specs=[
            const_spec(shapes[0].shape),
            const_spec(shapes[1].shape),
            const_spec(shapes[2].shape),
            pl.BlockSpec((1, 2 * L, L), lambda i: (i, 0, 0)),
            pl.BlockSpec((1, L, 128), lambda i: (i, 0, 0)),
            const_spec(shapes[5].shape),
        ],
        scratch_shapes=[
            pltpu.VMEM((F * T, EXTRA, D // T), BF),
            pltpu.VMEM((1, 3 * D), F32),
            pltpu.SemaphoreType.DMA((C + 3 * F * T,)),
        ],
        compiler_params=pltpu.CompilerParams(vmem_limit_bytes=VMEM_LIMIT),
        cost_estimate=cost(2 * L * ns * D * 3 * D, 40e6, ns * 12 * L * L),
    )(meta, *xs, *lows, *highs)


def normalised(values):
    centre = values - jnp.mean(values, axis=-1, keepdims=True)
    spread = jnp.mean(centre * centre, axis=-1, keepdims=True)
    rstd = lax.rsqrt(spread + 1e-12)
    return centre * rstd, rstd


def norm_back(grad, gain, xhat, rstd):
    scaled = grad * gain
    first = jnp.mean(scaled, axis=-1, keepdims=True)
    second = jnp.mean(scaled * xhat, axis=-1, keepdims=True)
    return rstd * (scaled - first - xhat * second)


def rows_kernel(dims, FF, meta, x_ref, ctx_ref, *refs):
    F, C, T, ns, span, D = dims
    n_w = F * T
    n_a = len(stacks(F, T, False))
    cots = refs[:C]
    qk, vo, inner, outer = (
        pieces_of(refs[C + i * n_a : C + (i + 1) * n_a], F, T, i % 2 == 1) for i in range(4)
    )
    refs = refs[C + 4 * n_a :]
    los = refs[:C]
    (
        first_out, dctx_out, nl_out, act_out, og_out, ig_out, ag_out, sums,
        cot_s, lo_s, wi, wo, wout, gp_s, small, vec, inner_bias, sems, out_sems,
    ) = refs[C:]
    k = pl.program_id(0)
    R = ns * span
    Dl, half, fhalf = D // F, D // T, FF // T
    f = meta[0]
    c = meta[1]

    def weight_copies():
        copies = []
        for df in range(F):
            row = pl.multiple_of((f ^ df) * Dl, 16)
            for dt in range(T):
                n = df * T + dt
                rows = pl.ds(row, Dl)
                copies.append((
                    pltpu.make_async_copy(
                        vo[df, dt].at[pl.ds(0, Dl), pl.ds(half, half)],
                        wo.at[rows, pl.ds(dt * half, half)], sems.at[n]),
                    pltpu.make_async_copy(
                        inner[df, dt],
                        wi.at[rows, pl.ds(dt * fhalf, fhalf)], sems.at[n_w + n]),
                    pltpu.make_async_copy(
                        outer[df, dt],
                        wout.at[rows, pl.ds(dt * fhalf, fhalf)], sems.at[2 * n_w + n]),
                ) + tuple(
                    pltpu.make_async_copy(
                        (qk if part == 0 else vo)[df, dt].at[pl.ds(Dl, EXTRA)],
                        small.at[n, :, pl.ds(part * D, D)], sems.at[(3 + part) * n_w + n])
                    for part in range(2)
                ))
        return copies

    def cot_copies():
        return [
            pltpu.make_async_copy(cots[i], cot_s.at[i], sems.at[5 * n_w + i]) for i in range(C)
        ]

    @pl.when(k == 0)
    def _():
        copies = weight_copies()
        for which in range(5):
            for group in copies:
                group[which].start()
        for copy in cot_copies():
            copy.start()
        sums[...] = jnp.zeros_like(sums)
        for which in range(5):
            for group in copies:
                group[which].wait()
        for copy in cot_copies():
            copy.wait()
        for dt in range(T):
            part = sum(small[df * T + dt, :EXTRA, :].astype(F32) for df in range(F))
            inner_bias[:, dt * fhalf : (dt + 1) * fhalf] = part[2:3]
            if dt == 0:
                vec[...] = part[3:9, :D]

    def add_sum(row, value):
        sums[row : row + 1, :] += jnp.sum(value, axis=0, keepdims=True)

    out_bias, gain1, shift1 = vec[0:1, :], vec[1:2, :], vec[2:3, :]
    outer_bias, gain2, shift2 = vec[3:4, :], vec[4:5, :], vec[5:6, :]
    ctx_low = ctx_ref[0]
    before = x_ref[0].astype(F32) + dot_nt(ctx_low, wo[...]) + out_bias
    xhat1, rstd1 = normalised(before)
    normed = xhat1 * gain1 + shift1
    nl = normed.astype(BF)
    nl_out[0] = nl
    root = math.sqrt(2.0 / math.pi)
    chunk = 768
    for j in range(FF // chunk):
        cols = slice(j * chunk, (j + 1) * chunk)
        pre = dot_nn(nl, wi[:, cols]) + inner_bias[:, cols]
        square = pre * pre
        th = jnp.tanh(pre * (root + (root * 0.044715) * square))
        hp = 0.5 + 0.5 * th
        act_out[0, :, cols] = (pre * hp).astype(BF)
        gp_s[:, cols] = hp + (0.5 * pre) * (1.0 - th * th) * (
            root + (3.0 * root * 0.044715) * square
        )
    before2 = normed + dot_nt(act_out[0], wout[...]) + outer_bias
    xhat2, rstd2 = normalised(before2)
    row = lax.broadcasted_iota(jnp.int32, (R, 1), 0)
    position = (c ^ k) * span + row % span
    length = jnp.full((R, 1), meta[2], jnp.int32)
    for s in range(1, ns):
        length = jnp.where(row >= s * span, meta[2 + s], length)
    live = (position < length).astype(F32)
    lo_s[k] = (live * (xhat2 * gain2 + shift2)).astype(BF)
    for i in range(C):
        @pl.when(k == i)
        def _():
            pltpu.make_async_copy(lo_s.at[i], los[i], out_sems.at[i]).start()
    grad = cot_s[k].astype(F32) * live
    add_sum(4, grad * xhat2)
    add_sum(5, grad)
    second = norm_back(grad, gain2, xhat2, rstd2)
    og = second.astype(BF)
    og_out[0] = og
    add_sum(3, og.astype(F32))
    for j in range(FF // chunk):
        cols = slice(j * chunk, (j + 1) * chunk)
        ig = (dot_nn(og, wout[:, cols]) * gp_s[:, cols]).astype(BF)
        ig_out[0, :, cols] = ig
    ngrad = dot_nt(ig_out[0], wi[...]) + second
    add_sum(1, ngrad * xhat1)
    add_sum(2, ngrad)
    first = norm_back(ngrad, gain1, xhat1, rstd1)
    first_out[0] = first
    ag = first.astype(BF)
    ag_out[0] = ag
    add_sum(0, ag.astype(F32))
    dctx_out[0] = dot_nn(ag, wo[...]).astype(BF)

    @pl.when(k == C - 1)
    def _():
        for i in range(C):
            pltpu.make_async_copy(lo_s.at[i], los[i], out_sems.at[i]).wait()


def rows_call(dims, FF, meta, x_all, ctx, cots, weights):
    F, C, T, ns, span, D = dims
    R = ns * span
    tile = lambda n: pl.BlockSpec((1, R, n), lambda i: (i, 0, 0))
    widths = [(D, F32), (D, BF), (D, BF), (FF, BF), (D, BF), (FF, BF), (D, BF)]
    out_shape = (
        [jax.ShapeDtypeStruct((R, D), BF)] * C
        + [jax.ShapeDtypeStruct((C, R, n), kind) for n, kind in widths]
        + [jax.ShapeDtypeStruct((EXTRA, D), F32)]
    )
    n_w = F * T
    outs = pl.pallas_call(
        functools.partial(rows_kernel, dims, FF),
        name="rows",
        grid=(C,),
        out_shape=out_shape,
        in_specs=[SMEM, tile(D), tile(D)]
        + [ANY] * (C + len(weights)),
        out_specs=[ANY] * C
        + [tile(n) for n, _ in widths]
        + [const_spec((EXTRA, D))],
        scratch_shapes=[
            pltpu.VMEM((C, R, D), BF),
            pltpu.VMEM((C, R, D), BF),
            pltpu.VMEM((D, FF), BF),
            pltpu.VMEM((D, D), BF),
            pltpu.VMEM((D, FF), BF),
            pltpu.VMEM((R, FF), F32),
            pltpu.VMEM((n_w, EXTRA, FF // T), BF),
            pltpu.VMEM((6, D), F32),
            pltpu.VMEM((1, FF), F32),
            pltpu.SemaphoreType.DMA((5 * n_w + C,)),
            pltpu.SemaphoreType.DMA((C,)),
        ],
        compiler_params=pltpu.CompilerParams(vmem_limit_bytes=VMEM_LIMIT),
        cost_estimate=cost(4 * C * R * D * (2 * FF + D), 50e6, C * R * FF),
    )(meta, x_all, ctx, *cots, *weights)
    return outs[:C], outs[C:]


def back_kernel(dims, qkv, ctx, dctx, e_ref, linv, out, ds_s):
    F, C, T, ns, span, D = dims
    step = pl.program_id(0)
    NP, L, half = D // 128, C * span, D // T
    s = step // NP
    pair = step % NP
    q_col = head_columns(pair, half)
    k_col = pl.multiple_of(q_col + half, 128)
    v_col = pl.multiple_of(q_col + 2 * half, 128)
    c_col = pl.multiple_of(pair * 128, 128)
    q = qkv[:, s, :, pl.ds(q_col, 128)].reshape(L, 128)
    k = qkv[:, s, :, pl.ds(k_col, 128)].reshape(L, 128)
    v = qkv[:, s, :, pl.ds(v_col, 128)].reshape(L, 128)
    grad = dctx[:, s, :, pl.ds(c_col, 128)].reshape(L, 128).astype(F32) * linv[0]
    grad_low = grad.astype(BF)
    product = grad_low.astype(F32) * ctx[:, s, :, pl.ds(c_col, 128)].reshape(L, 128).astype(F32)
    low = lax.broadcasted_iota(jnp.int32, (L, 128), 1) < HD
    zero = jnp.zeros((), BF)
    qs, ks, gs = [], [], []
    for h in range(2):
        mine = low if h == 0 else jnp.logical_not(low)
        row_dot = jnp.sum(jnp.where(mine, product, 0.0), axis=-1, keepdims=True)
        probs_grad = dot_nt(grad_low, jnp.where(mine, v, zero))
        e = e_ref[0, h * L : (h + 1) * L, :].astype(F32)
        ds_s[h * L : (h + 1) * L, :] = (e * (probs_grad - row_dot)).astype(BF)
        qs.append(jnp.where(mine, q, zero))
        ks.append(jnp.where(mine, k, zero))
        gs.append(jnp.where(mine, grad_low, zero))
    scale = 1.0 / math.sqrt(HD)
    dq = (dot_nn(ds_s[:L, :], ks[0]) + dot_nn(ds_s[L:, :], ks[1])) * scale
    dk = dot_tn(ds_s[...], jnp.concatenate(qs, axis=0)) * scale
    dv = dot_tn(e_ref[0], jnp.concatenate(gs, axis=0))
    out[:, s, :, pl.ds(q_col, 128)] = dq.astype(BF).reshape(C, span, 128)
    out[:, s, :, pl.ds(k_col, 128)] = dk.astype(BF).reshape(C, span, 128)
    out[:, s, :, pl.ds(v_col, 128)] = dv.astype(BF).reshape(C, span, 128)


def back_call(dims, qkv, ctx, dctx, e, linv):
    F, C, T, ns, span, D = dims
    NP, L = D // 128, C * span
    return pl.pallas_call(
        functools.partial(back_kernel, dims),
        name="back",
        grid=(ns * NP,),
        out_shape=jax.ShapeDtypeStruct(qkv.shape, BF),
        in_specs=[
            const_spec(qkv.shape),
            const_spec(ctx.shape),
            const_spec(dctx.shape),
            pl.BlockSpec((1, 2 * L, L), lambda i: (i, 0, 0)),
            pl.BlockSpec((1, L, 128), lambda i: (i, 0, 0)),
        ],
        out_specs=const_spec(qkv.shape),
        scratch_shapes=[pltpu.VMEM((2 * L, L), BF)],
        compiler_params=pltpu.CompilerParams(vmem_limit_bytes=VMEM_LIMIT),
        cost_estimate=cost(ns * NP * 16 * L * L * 128, 30e6, 0),
    )(qkv, ctx, dctx, e, linv)


def input_kernel(C, dqkv, w, first, *refs):
    outs, (buf, sems) = refs[:C], refs[C:]
    k = pl.program_id(0)
    buf[k] = (dot_nt(dqkv[0], w[...]) + first[0]).astype(BF)
    for i in range(C):
        @pl.when(k == i)
        def _():
            pltpu.make_async_copy(buf.at[i], outs[i], sems.at[i]).start()

    @pl.when(k == C - 1)
    def _():
        for i in range(C):
            pltpu.make_async_copy(buf.at[i], outs[i], sems.at[i]).wait()


def input_call(dqkv, w, first):
    C, R, W = dqkv.shape
    D = w.shape[0]
    return pl.pallas_call(
        functools.partial(input_kernel, C),
        name="input_grad",
        grid=(C,),
        out_shape=[jax.ShapeDtypeStruct((R, D), BF)] * C,
        in_specs=[
            pl.BlockSpec((1, R, W), lambda i: (i, 0, 0)),
            const_spec(w.shape),
            pl.BlockSpec((1, R, D), lambda i: (i, 0, 0)),
        ],
        out_specs=[ANY] * C,
        scratch_shapes=[pltpu.VMEM((C, R, D), BF), pltpu.SemaphoreType.DMA((C,))],
        compiler_params=pltpu.CompilerParams(vmem_limit_bytes=VMEM_LIMIT),
        cost_estimate=cost(2 * C * R * D * W, 15e6, 0),
    )(dqkv, w, first)


COLS = 384


def weight_kernel(F, pers, with_sums, meta, *refs):
    n = len(pers)
    lefts, rights = refs[:n], refs[n : 2 * n]
    refs = refs[2 * n :]
    sums, refs = (refs[0], refs[1:]) if with_sums else (None, refs)
    keep, send, tile = refs[:3]
    turned = refs[3:]
    D = lefts[0].shape[1]
    Dl = D // F
    b = pl.program_id(1)

    @pl.when((pl.program_id(0) == 0) & (b == 0))
    def _():
        for left, left_t in zip(lefts, turned):
            left_t[:D, :] = left[...].T
            left_t[D:, :] = jnp.ones((EXTRA, left.shape[0]), BF)

    start = 0
    for right, left_t, per in zip(rights, turned, pers):
        @pl.when((b >= start) & (b < start + per))
        def _():
            tile[...] = dot_nn(left_t[...], right[...]).astype(BF)
        start += per
    if with_sums:
        for j in range(D // COLS):
            @pl.when(b == j)
            def _():
                tile[D:, :] = sums[:, j * COLS : (j + 1) * COLS].astype(BF)
    f = meta[0]
    for high in range(F // 2):
        for bit, out in ((0, keep), (1, send)):
            row = pl.multiple_of((f ^ (2 * high + bit)) * Dl, 16)
            out[high, 0, :Dl] = tile[pl.ds(row, Dl), :]
            out[high, 0, Dl:] = tile[D:, :]


def weight_call(dims, meta, pairs, sums=None):
    F, C, T, ns, span, D = dims
    rows = C * ns * span
    pairs = [(left.reshape(rows, -1), right.reshape(rows, -1)) for left, right in pairs]
    pers = [right.shape[1] // T // COLS for _, right in pairs]
    width = sum(pers) * COLS
    out = jax.ShapeDtypeStruct((F // 2, T, D // F + EXTRA, width), BF)
    out_spec = pl.BlockSpec((F // 2, 1, D // F + EXTRA, COLS), lambda a, b: (0, a, 0, b))
    right_specs, start = [], 0
    for per in pers:
        right_specs.append(
            pl.BlockSpec(
                (rows, COLS),
                lambda a, b, per=per, start=start: (0, a * per + jnp.clip(b - start, 0, per - 1)),
            )
        )
        start += per
    return pl.pallas_call(
        functools.partial(weight_kernel, F, pers, sums is not None),
        name="weight_grad",
        grid=(T, sum(pers)),
        out_shape=[out, out],
        in_specs=[SMEM]
        + [const_spec(left.shape) for left, _ in pairs]
        + right_specs
        + ([] if sums is None else [const_spec(sums.shape)]),
        out_specs=[out_spec, out_spec],
        scratch_shapes=[pltpu.VMEM((D + EXTRA, COLS), BF)]
        + [pltpu.VMEM((D + EXTRA, rows), BF) for _ in pairs],
        compiler_params=pltpu.CompilerParams(vmem_limit_bytes=VMEM_LIMIT),
        cost_estimate=cost(
            2 * rows * D * width * T, 2 * (rows * (D + width * T) + D * width * T), 0
        ),
    )(
        meta,
        *[left for left, _ in pairs],
        *[right for _, right in pairs],
        *([] if sums is None else [sums]),
    )


def xor_pairs(count, mask):
    return [(i, i ^ mask) for i in range(count)]


def after(value, others):
    return lax.optimization_barrier((value, *others))[0]


def added(a, b):
    return (a.astype(F32) + b.astype(F32)).astype(BF)


def per_device(
    tokens_in, seq_lengths, query_weight, query_bias, key_weight, value_weight, value_bias,
    output_weight, output_bias, attn_gain, attn_shift, inner_weight, inner_bias, outer_weight,
    outer_bias, ffn_gain, ffn_shift, cotangent,
):
    F, C, T = (lax.axis_size(a) for a in ("fsdp", "ctx", "tp"))
    f, c, t = (lax.axis_index(a) for a in ("fsdp", "ctx", "tp"))
    S, span, D = tokens_in.shape
    ns = S // (C * T)
    Dl, half = D // F, D // T
    fhalf = inner_weight.shape[1]
    FF = fhalf * T
    R = ns * span
    dims = (F, C, T, ns, span, D)

    def sequence_pieces(array):
        return [
            lax.dynamic_slice_in_dim(array, ((c ^ k) * T + t) * ns, ns, 0).reshape(R, D)
            for k in range(C)
        ]

    def ctx_moved(piece, k):
        return lax.ppermute(piece, "ctx", xor_pairs(C, k)) if k else piece

    def tp_moved(pieces):
        both = jnp.concatenate(pieces, axis=0) if len(pieces) > 1 else pieces[0]
        return [both] + [lax.ppermute(both, "tp", xor_pairs(T, dt)) for dt in range(1, T)]

    def to_slots(groups, kind):
        out = lax.full((S, span, D), 0, kind)
        pieces = {}
        for ks, group in groups:
            for dt, merged in enumerate(group):
                for i, k in enumerate(ks):
                    pieces[k, dt] = merged[i * R : (i + 1) * R]
        for k in range(C):
            for dt in range(T):
                got = pieces[k, dt]
                out = lax.dynamic_update_slice_in_dim(
                    out, got.reshape(ns, span, D).astype(kind), ((c ^ k) * T + (t ^ dt)) * ns, 0
                )
        return out

    def swapped(array, axis, bit):
        return lax.ppermute(array, axis, xor_pairs(lax.axis_size(axis), bit))

    def chip_start(shard, across):
        held = shard[None]
        for axis, bit in order_of(F, T, across)[:-1]:
            held = jnp.concatenate([held, swapped(held, axis, bit)], axis=0)
        return held

    def chip_end(held, across):
        axis, bit = order_of(F, T, across)[-1]
        return swapped(held, axis, bit)

    def both_cores(held, got, others=()):
        near = swapped(after(held, others), "fsdp", 1)
        return [held, got, near, swapped(got, "fsdp", 1)]

    def spread(array, width):
        rows, part = array.shape
        owner = lax.broadcasted_iota(jnp.int32, (rows, part * F), 1) // part
        return jnp.where(owner == f, jnp.tile(array, (1, F)), jnp.zeros((), BF)).reshape(-1, width)

    x_pieces = sequence_pieces(tokens_in)
    near_x = ctx_moved(x_pieces[1], 1)
    x_pieces = x_pieces[:1] + [near_x] + [
        ctx_moved(after(x_pieces[k], [near_x]), k) for k in range(2, C)
    ]
    vectors = jnp.stack([output_bias, attn_gain, attn_shift, outer_bias, ffn_gain, ffn_shift])
    small = [
        spread(query_bias, half), spread(value_bias, half), spread(inner_bias, fhalf),
        spread(vectors, D),
    ]
    small = jnp.concatenate([jnp.pad(a, ((0, 0), (0, fhalf - a.shape[1]))) for a in small])
    small = jnp.pad(small, ((0, EXTRA - small.shape[0]), (0, 0)))
    low = jnp.concatenate([query_weight, key_weight], axis=1)
    high = jnp.concatenate([value_weight, output_weight.T], axis=1)
    low = chip_start(jnp.concatenate([low, small[:, :D]], axis=0), False)
    high = chip_start(jnp.concatenate([high, small[:, D:]], axis=0), True)
    lows = both_cores(low, chip_end(after(low, [near_x]), False))
    highs = both_cores(high, chip_end(after(high, [near_x]), True))
    halfway = [lows[1], highs[1], *x_pieces[2:]]
    inner = chip_start(after(inner_weight, halfway), False)
    outer = chip_start(after(outer_weight.T, halfway), True)
    inner_got = chip_end(inner, False)
    outer_got = chip_end(outer, True)
    cot_pieces = sequence_pieces(after(cotangent, [*x_pieces[1:], *lows, *highs]))
    cot_pieces = [ctx_moved(piece, k) for k, piece in enumerate(cot_pieces)]
    lengths = lax.dynamic_slice_in_dim(seq_lengths, (c * T + t) * ns, ns, 0)
    meta = jnp.concatenate([jnp.stack([f, c]).astype(jnp.int32), lengths])

    x_all, qkv_w, qkv, e, linv, ctx = front_call(
        dims, after(meta, [inner, outer]), x_pieces, lows, highs
    )
    inners = both_cores(inner, inner_got, [ctx, *cot_pieces[1:]])
    outers = both_cores(outer, outer_got, [ctx, *cot_pieces[1:]])
    los, (first, dctx, nl, act, og, inner_low, ag, sums) = rows_call(
        dims, FF, meta, x_all, ctx.reshape(C, R, D), cot_pieces, lows + highs + inners + outers,
    )

    def core_sum(keep, send):
        return added(keep, lax.ppermute(send, "fsdp", xor_pairs(F, 1)))

    def chip_sum(total, axis, dim):
        got = total
        while total.shape[dim] > 1:
            h = total.shape[dim] // 2
            stay, go = jnp.split(total, 2, axis=dim)
            got = swapped(go, axis, 2 * h if axis == "fsdp" else h)
            total = added(stay, got)
        return total, got

    def y_sum(total):
        return chip_sum(total, "fsdp", 0)

    def x_sum(total):
        return chip_sum(total, "tp", 1)

    def ctx_scatter(total):
        part = total.shape[1] // C
        mine = 0.0
        for k in range(C):
            block = lax.dynamic_slice_in_dim(total, (c ^ k) * part, part, 1)
            mine += ctx_moved(block, k).astype(F32)
        return mine.astype(BF)

    def ctx_gather(mine, like):
        part = mine.shape[1]
        out = like
        for k in range(C):
            out = lax.dynamic_update_slice_in_dim(out, ctx_moved(mine, k), (c ^ k) * part, 1)
        return out.astype(F32)

    outer_parts = weight_call(dims, meta, [(og, act)], sums)
    inner_parts = weight_call(dims, meta, [(after(nl, outer_parts), inner_low)])
    los = [ctx_moved(piece, k) for k, piece in enumerate(los)]
    keep, send = outer_parts
    outer_core = core_sum(keep, after(send, los[1:2]))
    keep, send = inner_parts
    inner_parts = keep, after(send, los[3:4])
    dctx = after(dctx, [outer_core, *inner_parts])
    dqkv = back_call(dims, qkv, ctx, dctx.reshape(ctx.shape), e, linv)
    inner_core = core_sum(*inner_parts)
    outer_y, outer_raw = y_sum(outer_core)
    even = range(2, C, 2)
    early = [0] + list(range(1, C, 2))
    early_lo = tp_moved([los[k] for k in early])
    first = after(first, [inner_core, outer_y, *los[1:], *early_lo[1:]])
    ins = input_call(dqkv.reshape(C, R, 3 * D), qkv_w, first)
    late_lo = tp_moved([after(los[k], [dqkv]) for k in even])
    outer_x, outer_raw = x_sum(outer_y)
    inner_y, inner_raw = y_sum(inner_core)
    ag = after(ag, ins)
    keep, send = weight_call(dims, meta, [(x_all, dqkv), (ag, ctx)])
    ig = [ctx_moved(piece, k) if k % 2 else piece for k, piece in enumerate(ins)]
    send = after(send, [outer_raw, inner_raw] + ig[1::2] + late_lo[1:])
    qkv_core = core_sum(keep, send)
    for k in even:
        ig[k] = ctx_moved(after(ins[k], ig[1::2]), k)
    outer_x = after(outer_x[0, 0], [qkv_core])
    outer_part = ctx_scatter(outer_x)
    early_ig = tp_moved(after(tuple(ig[k] for k in early), [qkv_core]))
    qkv_y, _ = y_sum(qkv_core)
    inner_x, _ = x_sum(after(inner_y, [outer_part]))
    outer_g = ctx_gather(after(outer_part, [qkv_y]), outer_x)
    inner_x = after(inner_x[0, 0], [ig[k] for k in even])
    inner_part = ctx_scatter(inner_x)
    qkv_x, _ = x_sum(qkv_y)
    qkv_x = qkv_x[0, 0]
    late_ig = tp_moved([after(ig[k], [qkv_x]) for k in even])
    early_lo, late_lo = (after(tuple(part), [qkv_core]) for part in (early_lo, late_lo))
    early_ig = after(tuple(early_ig), [qkv_x])
    layer_out = to_slots([(early, early_lo), (list(even), late_lo)], BF)
    input_grad = to_slots([(early, early_ig), (list(even), late_ig)], F32)
    inner_g = ctx_gather(inner_part, inner_x)
    qkv_g = ctx_gather(ctx_scatter(qkv_x), qkv_x)

    def own(row, shape):
        whole = row.reshape(shape[0], shape[1] * F)
        return lax.dynamic_slice_in_dim(whole, f * shape[1], shape[1], 1)

    vec_sums = lax.dynamic_slice_in_dim(outer_g[Dl : Dl + 6, :D], f * Dl, Dl, 1)

    return (
        layer_out,
        input_grad,
        qkv_g[:Dl, :half],
        own(qkv_g[Dl, :half], query_bias.shape),
        qkv_g[:Dl, half : 2 * half],
        qkv_g[:Dl, 2 * half : 3 * half],
        own(qkv_g[Dl, 2 * half : 3 * half], value_bias.shape),
        qkv_g[:Dl, 3 * half :].T,
        vec_sums[0],
        vec_sums[1],
        vec_sums[2],
        inner_g[:Dl],
        own(inner_g[Dl], inner_bias.shape),
        outer_g[:Dl].T,
        vec_sums[3],
        vec_sums[4],
        vec_sums[5],
    )


def solution(mesh):
    rows3, flat = P("fsdp", "ctx", None), P("fsdp")
    wide, tall = P("fsdp", "tp"), P("tp", "fsdp")
    params = (wide, tall, wide, wide, tall, tall, flat, flat, flat, wide, tall, tall, flat, flat, flat)
    return jax.shard_map(
        per_device,
        mesh=mesh,
        in_specs=(rows3, P("fsdp")) + params + (rows3,),
        out_specs=(rows3, rows3) + params,
        check_vma=False,
    )
```

```python
import functools
import math

import jax
import jax.numpy as jnp
from jax import lax
from jax.experimental import pallas as pl
from jax.experimental.pallas import tpu as pltpu
from jax.sharding import PartitionSpec as P

HD = 64
BF = jnp.bfloat16
F32 = jnp.float32
ANY = pl.BlockSpec(memory_space=pl.ANY)
SMEM = pl.BlockSpec(memory_space=pltpu.SMEM)
EXTRA = 16
VMEM_LIMIT = 60 * 1024 * 1024


def dot_nn(a, b):
    return lax.dot_general(a, b, (((1,), (0,)), ((), ())), preferred_element_type=F32)


def dot_nt(a, b):
    return lax.dot_general(a, b, (((1,), (1,)), ((), ())), preferred_element_type=F32)


def dot_tn(a, b):
    return lax.dot_general(a, b, (((0,), (0,)), ((), ())), preferred_element_type=F32)


def const_spec(shape):
    zeros = (0,) * len(shape)
    return pl.BlockSpec(shape, lambda *_: zeros)


def cost(flops, moved, exps=0):
    return pl.CostEstimate(flops=int(flops), bytes_accessed=int(moved), transcendentals=int(exps))


def head_columns(pair, half_cols):
    per = half_cols // 128
    return pl.multiple_of(pair // per * (3 * half_cols) + pair % per * 128, 128)


def order_of(F, T, across):
    chip = [("fsdp", 1 << b) for b in range(1, F.bit_length() - 1)]
    pair = [("tp", 1 << b) for b in range(T.bit_length() - 1)]
    return chip + pair if across else pair + chip


def stacks(F, T, across):
    held, out = [(0, 0)], []
    steps = order_of(F, T, across)
    for n, (axis, bit) in enumerate(steps):
        got = [(df ^ bit, dt) if axis == "fsdp" else (df, dt ^ bit) for df, dt in held]
        if n == len(steps) - 1:
            out += [held, got]
        held = held + got
    return out + [[(df ^ 1, dt) for df, dt in part] for part in out]


def pieces_of(refs, F, T, across):
    return {
        at: ref.at[i] for ref, part in zip(refs, stacks(F, T, across)) for i, at in enumerate(part)
    }


def front_kernel(dims, meta, *refs):
    F, C, T, ns, span, D = dims
    n_w = F * T
    n_a = len(stacks(F, T, False))
    xs, low_refs, high_refs = refs[:C], refs[C : C + n_a], refs[C + n_a : C + 2 * n_a]
    x_out, w_out, qkv, e_out, linv_out, ctx, small, bias, sems = refs[C + 2 * n_a :]
    step = pl.program_id(0)
    NP = D // 128
    L = C * span
    Dl, half = D // F, D // T
    f = meta[0]
    c = meta[1]

    @pl.when(step == 0)
    def _():
        copies = [pltpu.make_async_copy(xs[k], x_out.at[k], sems.at[k]) for k in range(C)]
        qk = pieces_of(low_refs, F, T, False)
        vo = pieces_of(high_refs, F, T, True)
        for df in range(F):
            for dt in range(T):
                n = df * T + dt
                rows = pl.ds(pl.multiple_of((f ^ df) * Dl, 16), Dl)
                start = dt * 3 * half
                copies += [
                    pltpu.make_async_copy(
                        qk[df, dt].at[pl.ds(0, Dl)], w_out.at[rows, pl.ds(start, 2 * half)],
                        sems.at[C + n]),
                    pltpu.make_async_copy(
                        vo[df, dt].at[pl.ds(0, Dl), pl.ds(0, half)],
                        w_out.at[rows, pl.ds(start + 2 * half, half)], sems.at[C + n_w + n]),
                    pltpu.make_async_copy(
                        qk[df, dt].at[pl.ds(Dl, EXTRA), pl.ds(0, half)], small.at[n],
                        sems.at[C + 2 * n_w + n]),
                ]
        for copy in copies:
            copy.start()
        for copy in copies:
            copy.wait()
        bias[...] = jnp.zeros_like(bias)
        for dt in range(T):
            part = sum(small[df * T + dt, :2, :].astype(F32) for df in range(F))
            bias[:, dt * 3 * half : dt * 3 * half + half] = part[0:1]
            bias[:, (dt * 3 + 2) * half : (dt * 3 + 3) * half] = part[1:2]

        def project(j, carry):
            cols = pl.ds(pl.multiple_of(j * 384, 128), 384)
            y = dot_nn(x_out[...].reshape(L * ns, D), w_out[:, cols]) + bias[:, cols]
            qkv[:, :, :, cols] = y.astype(BF).reshape(C, ns, span, 384)
            return carry

        lax.fori_loop(0, 3 * D // 384, project, 0)

    s = step // NP
    pair = step % NP
    q_col = head_columns(pair, half)
    q = qkv[:, s, :, pl.ds(q_col, 128)].reshape(L, 128)
    k = qkv[:, s, :, pl.ds(pl.multiple_of(q_col + half, 128), 128)].reshape(L, 128)
    v = qkv[:, s, :, pl.ds(pl.multiple_of(q_col + 2 * half, 128), 128)].reshape(L, 128)
    low = lax.broadcasted_iota(jnp.int32, (L, 128), 1) < HD
    zero = jnp.zeros((), BF)
    one = jnp.ones((L, 128), BF)
    lane = lax.broadcasted_iota(jnp.int32, (1, L), 1)
    pos = ((lane // span) ^ c) * span + lane % span
    mask = jnp.where(pos < meta[2 + s], 0.0, -1e30)
    values = []
    for h in range(2):
        mine = low if h == 0 else jnp.logical_not(low)
        scores = dot_nt(q, jnp.where(mine, k, zero)) * (math.log2(math.e) / math.sqrt(HD)) + mask
        top = jnp.max(scores, axis=-1, keepdims=True)
        e_out[0, h * L : (h + 1) * L, :] = jnp.exp2(scores - top).astype(BF)
        values.append(
            jnp.concatenate([jnp.where(mine, v, zero), jnp.where(mine, one, zero)], axis=1)
        )
    acc = dot_nn(e_out[0, :L, :], values[0]) + dot_nn(e_out[0, L:, :], values[1])
    linv = 1.0 / acc[:, 128:]
    linv_out[0] = linv
    ctx[:, s, :, pl.ds(pl.multiple_of(pair * 128, 128), 128)] = (
        (acc[:, :128] * linv).astype(BF).reshape(C, span, 128)
    )


def front_call(dims, meta, xs, lows, highs):
    F, C, T, ns, span, D = dims
    NP, L = D // 128, C * span
    rows = ns * span
    shapes = [
        jax.ShapeDtypeStruct((C, rows, D), BF),
        jax.ShapeDtypeStruct((D, 3 * D), BF),
        jax.ShapeDtypeStruct((C, ns, span, 3 * D), BF),
        jax.ShapeDtypeStruct((ns * NP, 2 * L, L), BF),
        jax.ShapeDtypeStruct((ns * NP, L, 128), F32),
        jax.ShapeDtypeStruct((C, ns, span, D), BF),
    ]
    return pl.pallas_call(
        functools.partial(front_kernel, dims),
        name="front",
        grid=(ns * NP,),
        out_shape=shapes,
        in_specs=[SMEM] + [ANY] * (C + len(lows) + len(highs)),
        out_specs=[
            const_spec(shapes[0].shape),
            const_spec(shapes[1].shape),
            const_spec(shapes[2].shape),
            pl.BlockSpec((1, 2 * L, L), lambda i: (i, 0, 0)),
            pl.BlockSpec((1, L, 128), lambda i: (i, 0, 0)),
            const_spec(shapes[5].shape),
        ],
        scratch_shapes=[
            pltpu.VMEM((F * T, EXTRA, D // T), BF),
            pltpu.VMEM((1, 3 * D), F32),
            pltpu.SemaphoreType.DMA((C + 3 * F * T,)),
        ],
        compiler_params=pltpu.CompilerParams(vmem_limit_bytes=VMEM_LIMIT),
        cost_estimate=cost(2 * L * ns * D * 3 * D, 40e6, ns * 12 * L * L),
    )(meta, *xs, *lows, *highs)


def normalised(values):
    centre = values - jnp.mean(values, axis=-1, keepdims=True)
    spread = jnp.mean(centre * centre, axis=-1, keepdims=True)
    rstd = lax.rsqrt(spread + 1e-12)
    return centre * rstd, rstd


def norm_back(grad, gain, xhat, rstd):
    scaled = grad * gain
    first = jnp.mean(scaled, axis=-1, keepdims=True)
    second = jnp.mean(scaled * xhat, axis=-1, keepdims=True)
    return rstd * (scaled - first - xhat * second)


def rows_kernel(dims, FF, meta, x_ref, ctx_ref, *refs):
    F, C, T, ns, span, D = dims
    n_w = F * T
    n_a = len(stacks(F, T, False))
    cots = refs[:C]
    qk, vo, inner, outer = (
        pieces_of(refs[C + i * n_a : C + (i + 1) * n_a], F, T, i % 2 == 1) for i in range(4)
    )
    refs = refs[C + 4 * n_a :]
    los = refs[:C]
    (
        first_out, dctx_out, nl_out, act_out, og_out, ig_out, ag_out, sums,
        cot_s, lo_s, wi, wo, wout, gp_s, small, vec, inner_bias, sems, out_sems,
    ) = refs[C:]
    k = pl.program_id(0)
    R = ns * span
    Dl, half, fhalf = D // F, D // T, FF // T
    f = meta[0]
    c = meta[1]

    def weight_copies():
        copies = []
        for df in range(F):
            row = pl.multiple_of((f ^ df) * Dl, 16)
            for dt in range(T):
                n = df * T + dt
                rows = pl.ds(row, Dl)
                copies.append((
                    pltpu.make_async_copy(
                        vo[df, dt].at[pl.ds(0, Dl), pl.ds(half, half)],
                        wo.at[rows, pl.ds(dt * half, half)], sems.at[n]),
                    pltpu.make_async_copy(
                        inner[df, dt],
                        wi.at[rows, pl.ds(dt * fhalf, fhalf)], sems.at[n_w + n]),
                    pltpu.make_async_copy(
                        outer[df, dt],
                        wout.at[rows, pl.ds(dt * fhalf, fhalf)], sems.at[2 * n_w + n]),
                ) + tuple(
                    pltpu.make_async_copy(
                        (qk if part == 0 else vo)[df, dt].at[pl.ds(Dl, EXTRA)],
                        small.at[n, :, pl.ds(part * D, D)], sems.at[(3 + part) * n_w + n])
                    for part in range(2)
                ))
        return copies

    def cot_copies():
        return [
            pltpu.make_async_copy(cots[i], cot_s.at[i], sems.at[5 * n_w + i]) for i in range(C)
        ]

    @pl.when(k == 0)
    def _():
        copies = weight_copies()
        for which in range(5):
            for group in copies:
                group[which].start()
        for copy in cot_copies():
            copy.start()
        sums[...] = jnp.zeros_like(sums)
        for which in range(5):
            for group in copies:
                group[which].wait()
        for copy in cot_copies():
            copy.wait()
        for dt in range(T):
            part = sum(small[df * T + dt, :EXTRA, :].astype(F32) for df in range(F))
            inner_bias[:, dt * fhalf : (dt + 1) * fhalf] = part[2:3]
            if dt == 0:
                vec[...] = part[3:9, :D]

    def add_sum(row, value):
        sums[row : row + 1, :] += jnp.sum(value, axis=0, keepdims=True)

    out_bias, gain1, shift1 = vec[0:1, :], vec[1:2, :], vec[2:3, :]
    outer_bias, gain2, shift2 = vec[3:4, :], vec[4:5, :], vec[5:6, :]
    ctx_low = ctx_ref[0]
    before = x_ref[0].astype(F32) + dot_nt(ctx_low, wo[...]) + out_bias
    xhat1, rstd1 = normalised(before)
    normed = xhat1 * gain1 + shift1
    nl = normed.astype(BF)
    nl_out[0] = nl
    root = math.sqrt(2.0 / math.pi)
    chunk = 768
    for j in range(FF // chunk):
        cols = slice(j * chunk, (j + 1) * chunk)
        pre = dot_nn(nl, wi[:, cols]) + inner_bias[:, cols]
        square = pre * pre
        th = jnp.tanh(pre * (root + (root * 0.044715) * square))
        hp = 0.5 + 0.5 * th
        act_out[0, :, cols] = (pre * hp).astype(BF)
        gp_s[:, cols] = hp + (0.5 * pre) * (1.0 - th * th) * (
            root + (3.0 * root * 0.044715) * square
        )
    before2 = normed + dot_nt(act_out[0], wout[...]) + outer_bias
    xhat2, rstd2 = normalised(before2)
    row = lax.broadcasted_iota(jnp.int32, (R, 1), 0)
    position = (c ^ k) * span + row % span
    length = jnp.full((R, 1), meta[2], jnp.int32)
    for s in range(1, ns):
        length = jnp.where(row >= s * span, meta[2 + s], length)
    live = (position < length).astype(F32)
    lo_s[k] = (live * (xhat2 * gain2 + shift2)).astype(BF)
    for i in range(C):
        @pl.when(k == i)
        def _():
            pltpu.make_async_copy(lo_s.at[i], los[i], out_sems.at[i]).start()
    grad = cot_s[k].astype(F32) * live
    add_sum(4, grad * xhat2)
    add_sum(5, grad)
    second = norm_back(grad, gain2, xhat2, rstd2)
    og = second.astype(BF)
    og_out[0] = og
    add_sum(3, og.astype(F32))
    for j in range(FF // chunk):
        cols = slice(j * chunk, (j + 1) * chunk)
        ig = (dot_nn(og, wout[:, cols]) * gp_s[:, cols]).astype(BF)
        ig_out[0, :, cols] = ig
    ngrad = dot_nt(ig_out[0], wi[...]) + second
    add_sum(1, ngrad * xhat1)
    add_sum(2, ngrad)
    first = norm_back(ngrad, gain1, xhat1, rstd1)
    first_out[0] = first
    ag = first.astype(BF)
    ag_out[0] = ag
    add_sum(0, ag.astype(F32))
    dctx_out[0] = dot_nn(ag, wo[...]).astype(BF)

    @pl.when(k == C - 1)
    def _():
        for i in range(C):
            pltpu.make_async_copy(lo_s.at[i], los[i], out_sems.at[i]).wait()


def rows_call(dims, FF, meta, x_all, ctx, cots, weights):
    F, C, T, ns, span, D = dims
    R = ns * span
    tile = lambda n: pl.BlockSpec((1, R, n), lambda i: (i, 0, 0))
    widths = [(D, F32), (D, BF), (D, BF), (FF, BF), (D, BF), (FF, BF), (D, BF)]
    out_shape = (
        [jax.ShapeDtypeStruct((R, D), BF)] * C
        + [jax.ShapeDtypeStruct((C, R, n), kind) for n, kind in widths]
        + [jax.ShapeDtypeStruct((EXTRA, D), F32)]
    )
    n_w = F * T
    outs = pl.pallas_call(
        functools.partial(rows_kernel, dims, FF),
        name="rows",
        grid=(C,),
        out_shape=out_shape,
        in_specs=[SMEM, tile(D), tile(D)]
        + [ANY] * (C + len(weights)),
        out_specs=[ANY] * C
        + [tile(n) for n, _ in widths]
        + [const_spec((EXTRA, D))],
        scratch_shapes=[
            pltpu.VMEM((C, R, D), BF),
            pltpu.VMEM((C, R, D), BF),
            pltpu.VMEM((D, FF), BF),
            pltpu.VMEM((D, D), BF),
            pltpu.VMEM((D, FF), BF),
            pltpu.VMEM((R, FF), F32),
            pltpu.VMEM((n_w, EXTRA, FF // T), BF),
            pltpu.VMEM((6, D), F32),
            pltpu.VMEM((1, FF), F32),
            pltpu.SemaphoreType.DMA((5 * n_w + C,)),
            pltpu.SemaphoreType.DMA((C,)),
        ],
        compiler_params=pltpu.CompilerParams(vmem_limit_bytes=VMEM_LIMIT),
        cost_estimate=cost(4 * C * R * D * (2 * FF + D), 50e6, C * R * FF),
    )(meta, x_all, ctx, *cots, *weights)
    return outs[:C], outs[C:]


def back_kernel(dims, qkv, ctx, dctx, e_ref, linv, out, ds_s):
    F, C, T, ns, span, D = dims
    step = pl.program_id(0)
    NP, L, half = D // 128, C * span, D // T
    s = step // NP
    pair = step % NP
    q_col = head_columns(pair, half)
    k_col = pl.multiple_of(q_col + half, 128)
    v_col = pl.multiple_of(q_col + 2 * half, 128)
    c_col = pl.multiple_of(pair * 128, 128)
    q = qkv[:, s, :, pl.ds(q_col, 128)].reshape(L, 128)
    k = qkv[:, s, :, pl.ds(k_col, 128)].reshape(L, 128)
    v = qkv[:, s, :, pl.ds(v_col, 128)].reshape(L, 128)
    grad = dctx[:, s, :, pl.ds(c_col, 128)].reshape(L, 128).astype(F32) * linv[0]
    grad_low = grad.astype(BF)
    product = grad_low.astype(F32) * ctx[:, s, :, pl.ds(c_col, 128)].reshape(L, 128).astype(F32)
    low = lax.broadcasted_iota(jnp.int32, (L, 128), 1) < HD
    zero = jnp.zeros((), BF)
    qs, ks, gs = [], [], []
    for h in range(2):
        mine = low if h == 0 else jnp.logical_not(low)
        row_dot = jnp.sum(jnp.where(mine, product, 0.0), axis=-1, keepdims=True)
        probs_grad = dot_nt(grad_low, jnp.where(mine, v, zero))
        e = e_ref[0, h * L : (h + 1) * L, :].astype(F32)
        ds_s[h * L : (h + 1) * L, :] = (e * (probs_grad - row_dot)).astype(BF)
        qs.append(jnp.where(mine, q, zero))
        ks.append(jnp.where(mine, k, zero))
        gs.append(jnp.where(mine, grad_low, zero))
    scale = 1.0 / math.sqrt(HD)
    dq = (dot_nn(ds_s[:L, :], ks[0]) + dot_nn(ds_s[L:, :], ks[1])) * scale
    dk = dot_tn(ds_s[...], jnp.concatenate(qs, axis=0)) * scale
    dv = dot_tn(e_ref[0], jnp.concatenate(gs, axis=0))
    out[:, s, :, pl.ds(q_col, 128)] = dq.astype(BF).reshape(C, span, 128)
    out[:, s, :, pl.ds(k_col, 128)] = dk.astype(BF).reshape(C, span, 128)
    out[:, s, :, pl.ds(v_col, 128)] = dv.astype(BF).reshape(C, span, 128)


def back_call(dims, qkv, ctx, dctx, e, linv):
    F, C, T, ns, span, D = dims
    NP, L = D // 128, C * span
    return pl.pallas_call(
        functools.partial(back_kernel, dims),
        name="back",
        grid=(ns * NP,),
        out_shape=jax.ShapeDtypeStruct(qkv.shape, BF),
        in_specs=[
            const_spec(qkv.shape),
            const_spec(ctx.shape),
            const_spec(dctx.shape),
            pl.BlockSpec((1, 2 * L, L), lambda i: (i, 0, 0)),
            pl.BlockSpec((1, L, 128), lambda i: (i, 0, 0)),
        ],
        out_specs=const_spec(qkv.shape),
        scratch_shapes=[pltpu.VMEM((2 * L, L), BF)],
        compiler_params=pltpu.CompilerParams(vmem_limit_bytes=VMEM_LIMIT),
        cost_estimate=cost(ns * NP * 16 * L * L * 128, 30e6, 0),
    )(qkv, ctx, dctx, e, linv)


def input_kernel(C, dqkv, w, first, *refs):
    outs, (buf, sems) = refs[:C], refs[C:]
    k = pl.program_id(0)
    buf[k] = (dot_nt(dqkv[0], w[...]) + first[0]).astype(BF)
    for i in range(C):
        @pl.when(k == i)
        def _():
            pltpu.make_async_copy(buf.at[i], outs[i], sems.at[i]).start()

    @pl.when(k == C - 1)
    def _():
        for i in range(C):
            pltpu.make_async_copy(buf.at[i], outs[i], sems.at[i]).wait()


def input_call(dqkv, w, first):
    C, R, W = dqkv.shape
    D = w.shape[0]
    return pl.pallas_call(
        functools.partial(input_kernel, C),
        name="input_grad",
        grid=(C,),
        out_shape=[jax.ShapeDtypeStruct((R, D), BF)] * C,
        in_specs=[
            pl.BlockSpec((1, R, W), lambda i: (i, 0, 0)),
            const_spec(w.shape),
            pl.BlockSpec((1, R, D), lambda i: (i, 0, 0)),
        ],
        out_specs=[ANY] * C,
        scratch_shapes=[pltpu.VMEM((C, R, D), BF), pltpu.SemaphoreType.DMA((C,))],
        compiler_params=pltpu.CompilerParams(vmem_limit_bytes=VMEM_LIMIT),
        cost_estimate=cost(2 * C * R * D * W, 15e6, 0),
    )(dqkv, w, first)


COLS = 384


def weight_kernel(F, pers, with_sums, meta, *refs):
    n = len(pers)
    lefts, rights = refs[:n], refs[n : 2 * n]
    refs = refs[2 * n :]
    sums, refs = (refs[0], refs[1:]) if with_sums else (None, refs)
    keep, send, tile = refs[:3]
    turned = refs[3:]
    D = lefts[0].shape[1]
    Dl = D // F
    b = pl.program_id(1)

    @pl.when((pl.program_id(0) == 0) & (b == 0))
    def _():
        for left, left_t in zip(lefts, turned):
            left_t[:D, :] = left[...].T
            left_t[D:, :] = jnp.ones((EXTRA, left.shape[0]), BF)

    start = 0
    for right, left_t, per in zip(rights, turned, pers):
        @pl.when((b >= start) & (b < start + per))
        def _():
            tile[...] = dot_nn(left_t[...], right[...]).astype(BF)
        start += per
    if with_sums:
        for j in range(D // COLS):
            @pl.when(b == j)
            def _():
                tile[D:, :] = sums[:, j * COLS : (j + 1) * COLS].astype(BF)
    f = meta[0]
    for high in range(F // 2):
        for bit, out in ((0, keep), (1, send)):
            row = pl.multiple_of((f ^ (2 * high + bit)) * Dl, 16)
            out[high, 0, :Dl] = tile[pl.ds(row, Dl), :]
            out[high, 0, Dl:] = tile[D:, :]


def weight_call(dims, meta, pairs, sums=None):
    F, C, T, ns, span, D = dims
    rows = C * ns * span
    pairs = [(left.reshape(rows, -1), right.reshape(rows, -1)) for left, right in pairs]
    pers = [right.shape[1] // T // COLS for _, right in pairs]
    width = sum(pers) * COLS
    out = jax.ShapeDtypeStruct((F // 2, T, D // F + EXTRA, width), BF)
    out_spec = pl.BlockSpec((F // 2, 1, D // F + EXTRA, COLS), lambda a, b: (0, a, 0, b))
    right_specs, start = [], 0
    for per in pers:
        right_specs.append(
            pl.BlockSpec(
                (rows, COLS),
                lambda a, b, per=per, start=start: (0, a * per + jnp.clip(b - start, 0, per - 1)),
            )
        )
        start += per
    return pl.pallas_call(
        functools.partial(weight_kernel, F, pers, sums is not None),
        name="weight_grad",
        grid=(T, sum(pers)),
        out_shape=[out, out],
        in_specs=[SMEM]
        + [const_spec(left.shape) for left, _ in pairs]
        + right_specs
        + ([] if sums is None else [const_spec(sums.shape)]),
        out_specs=[out_spec, out_spec],
        scratch_shapes=[pltpu.VMEM((D + EXTRA, COLS), BF)]
        + [pltpu.VMEM((D + EXTRA, rows), BF) for _ in pairs],
        compiler_params=pltpu.CompilerParams(vmem_limit_bytes=VMEM_LIMIT),
        cost_estimate=cost(
            2 * rows * D * width * T, 2 * (rows * (D + width * T) + D * width * T), 0
        ),
    )(
        meta,
        *[left for left, _ in pairs],
        *[right for _, right in pairs],
        *([] if sums is None else [sums]),
    )


def xor_pairs(count, mask):
    return [(i, i ^ mask) for i in range(count)]


def after(value, others):
    return lax.optimization_barrier((value, *others))[0]


def added(a, b):
    return (a.astype(F32) + b.astype(F32)).astype(BF)


def per_device(
    tokens_in, seq_lengths, query_weight, query_bias, key_weight, value_weight, value_bias,
    output_weight, output_bias, attn_gain, attn_shift, inner_weight, inner_bias, outer_weight,
    outer_bias, ffn_gain, ffn_shift, cotangent,
):
    F, C, T = (lax.axis_size(a) for a in ("fsdp", "ctx", "tp"))
    f, c, t = (lax.axis_index(a) for a in ("fsdp", "ctx", "tp"))
    S, span, D = tokens_in.shape
    ns = S // (C * T)
    Dl, half = D // F, D // T
    fhalf = inner_weight.shape[1]
    FF = fhalf * T
    R = ns * span
    dims = (F, C, T, ns, span, D)

    def sequence_pieces(array):
        return [
            lax.dynamic_slice_in_dim(array, ((c ^ k) * T + t) * ns, ns, 0).reshape(R, D)
            for k in range(C)
        ]

    def ctx_moved(piece, k):
        return lax.ppermute(piece, "ctx", xor_pairs(C, k)) if k else piece

    def tp_moved(pieces):
        both = jnp.concatenate(pieces, axis=0) if len(pieces) > 1 else pieces[0]
        return [both] + [lax.ppermute(both, "tp", xor_pairs(T, dt)) for dt in range(1, T)]

    def to_slots(groups, kind):
        out = lax.full((S, span, D), 0, kind)
        pieces = {}
        for ks, group in groups:
            for dt, merged in enumerate(group):
                for i, k in enumerate(ks):
                    pieces[k, dt] = merged[i * R : (i + 1) * R]
        for k in range(C):
            for dt in range(T):
                got = pieces[k, dt]
                out = lax.dynamic_update_slice_in_dim(
                    out, got.reshape(ns, span, D).astype(kind), ((c ^ k) * T + (t ^ dt)) * ns, 0
                )
        return out

    def swapped(array, axis, bit):
        return lax.ppermute(array, axis, xor_pairs(lax.axis_size(axis), bit))

    def chip_start(shard, across):
        held = shard[None]
        for axis, bit in order_of(F, T, across)[:-1]:
            held = jnp.concatenate([held, swapped(held, axis, bit)], axis=0)
        return held

    def chip_end(held, across):
        axis, bit = order_of(F, T, across)[-1]
        return swapped(held, axis, bit)

    def both_cores(held, got, others=()):
        near = swapped(after(held, others), "fsdp", 1)
        return [held, got, near, swapped(got, "fsdp", 1)]

    def spread(array, width):
        rows, part = array.shape
        owner = lax.broadcasted_iota(jnp.int32, (rows, part * F), 1) // part
        return jnp.where(owner == f, jnp.tile(array, (1, F)), jnp.zeros((), BF)).reshape(-1, width)

    x_pieces = sequence_pieces(tokens_in)
    near_x = ctx_moved(x_pieces[1], 1)
    before = [near_x]
    x_pieces[1] = near_x
    for k in [*range(3, C, 2), *range(2, C, 2)]:
        x_pieces[k] = ctx_moved(after(x_pieces[k], before), k)
        before = [x_pieces[k]]
    vectors = jnp.stack([output_bias, attn_gain, attn_shift, outer_bias, ffn_gain, ffn_shift])
    small = [
        spread(query_bias, half), spread(value_bias, half), spread(inner_bias, fhalf),
        spread(vectors, D),
    ]
    small = jnp.concatenate([jnp.pad(a, ((0, 0), (0, fhalf - a.shape[1]))) for a in small])
    small = jnp.pad(small, ((0, EXTRA - small.shape[0]), (0, 0)))
    low = jnp.concatenate([query_weight, key_weight], axis=1)
    high = jnp.concatenate([value_weight, output_weight.T], axis=1)
    low = chip_start(jnp.concatenate([low, small[:, :D]], axis=0), False)
    high = chip_start(jnp.concatenate([high, small[:, D:]], axis=0), True)
    lows = both_cores(low, chip_end(after(low, [near_x]), False))
    highs = both_cores(high, chip_end(after(high, [near_x]), True))
    halfway = [lows[1], highs[1], *x_pieces[3::2]]
    inner = chip_start(after(inner_weight, halfway), False)
    outer = chip_start(after(outer_weight.T, halfway), True)
    inner_got = chip_end(after(inner, x_pieces[2::2]), False)
    outer_got = chip_end(after(outer, x_pieces[2::2]), True)
    cot_pieces = sequence_pieces(after(cotangent, [*x_pieces[1:], *lows, *highs]))
    cot_pieces = [ctx_moved(piece, k) for k, piece in enumerate(cot_pieces)]
    lengths = lax.dynamic_slice_in_dim(seq_lengths, (c * T + t) * ns, ns, 0)
    meta = jnp.concatenate([jnp.stack([f, c]).astype(jnp.int32), lengths])

    x_all, qkv_w, qkv, e, linv, ctx = front_call(
        dims, after(meta, [inner, outer]), x_pieces, lows, highs
    )
    inners = both_cores(inner, inner_got, [ctx, *cot_pieces[1:]])
    outers = both_cores(outer, outer_got, [ctx, *cot_pieces[1:]])
    los, (first, dctx, nl, act, og, inner_low, ag, sums) = rows_call(
        dims, FF, meta, x_all, ctx.reshape(C, R, D), cot_pieces, lows + highs + inners + outers,
    )

    def core_sum(keep, send):
        return added(keep, lax.ppermute(send, "fsdp", xor_pairs(F, 1)))

    def chip_sum(total, axis, dim):
        got = total
        while total.shape[dim] > 1:
            h = total.shape[dim] // 2
            stay, go = jnp.split(total, 2, axis=dim)
            got = swapped(go, axis, 2 * h if axis == "fsdp" else h)
            total = added(stay, got)
        return total, got

    def y_sum(total):
        return chip_sum(total, "fsdp", 0)

    def x_sum(total):
        return chip_sum(total, "tp", 1)

    def ctx_scatter(total):
        part = total.shape[1] // C
        mine = 0.0
        for k in range(C):
            block = lax.dynamic_slice_in_dim(total, (c ^ k) * part, part, 1)
            mine += ctx_moved(block, k).astype(F32)
        return mine.astype(BF)

    def ctx_gather(mine, like):
        part = mine.shape[1]
        out = like
        for k in range(C):
            out = lax.dynamic_update_slice_in_dim(out, ctx_moved(mine, k), (c ^ k) * part, 1)
        return out.astype(F32)

    outer_parts = weight_call(dims, meta, [(og, act)], sums)
    inner_parts = weight_call(dims, meta, [(after(nl, outer_parts), inner_low)])
    los = [ctx_moved(piece, k) for k, piece in enumerate(los)]
    keep, send = outer_parts
    outer_core = core_sum(keep, after(send, los[1:2]))
    keep, send = inner_parts
    inner_parts = keep, after(send, los[3:4])
    dctx = after(dctx, [outer_core, *inner_parts])
    dqkv = back_call(dims, qkv, ctx, dctx.reshape(ctx.shape), e, linv)
    inner_core = core_sum(*inner_parts)
    outer_y, outer_raw = y_sum(outer_core)
    even = range(2, C, 2)
    early = [0] + list(range(1, C, 2))
    early_lo = tp_moved([los[k] for k in early])
    first = after(first, [inner_core, outer_y, *los[1:], *early_lo[1:]])
    ins = input_call(dqkv.reshape(C, R, 3 * D), qkv_w, first)
    late_lo = tp_moved([after(los[k], [dqkv]) for k in even])
    outer_x, outer_raw = x_sum(outer_y)
    inner_y, inner_raw = y_sum(inner_core)
    ag = after(ag, ins)
    keep, send = weight_call(dims, meta, [(x_all, dqkv), (ag, ctx)])
    ig = [ctx_moved(piece, k) if k % 2 else piece for k, piece in enumerate(ins)]
    send = after(send, [outer_raw, inner_raw] + ig[1::2] + late_lo[1:])
    qkv_core = core_sum(keep, send)
    for k in even:
        ig[k] = ctx_moved(after(ins[k], ig[1::2]), k)
    outer_x = after(outer_x[0, 0], [qkv_core] + [ig[k] for k in even])
    outer_part = ctx_scatter(outer_x)
    early_ig = tp_moved(after(tuple(ig[k] for k in early), [qkv_core]))
    qkv_y, _ = y_sum(qkv_core)
    inner_x, _ = x_sum(after(inner_y, [outer_part]))
    outer_g = ctx_gather(outer_part, outer_x)
    inner_x = after(inner_x[0, 0], [qkv_y] + [ig[k] for k in even])
    inner_part = ctx_scatter(inner_x)
    qkv_x, _ = x_sum(qkv_y)
    qkv_x = after(qkv_x[0, 0], [inner_part])
    qkv_part = ctx_scatter(qkv_x)
    late_ig = tp_moved([after(ig[k], [qkv_x]) for k in even])
    early_lo, late_lo = (after(tuple(part), [qkv_core]) for part in (early_lo, late_lo))
    early_ig = after(tuple(early_ig), [qkv_x])
    layer_out = to_slots([(early, early_lo), (list(even), late_lo)], BF)
    input_grad = to_slots([(early, early_ig), (list(even), late_ig)], F32)
    inner_g = ctx_gather(inner_part, inner_x)
    qkv_g = ctx_gather(qkv_part, qkv_x)

    def own(row, shape):
        whole = row.reshape(shape[0], shape[1] * F)
        return lax.dynamic_slice_in_dim(whole, f * shape[1], shape[1], 1)

    vec_sums = lax.dynamic_slice_in_dim(outer_g[Dl : Dl + 6, :D], f * Dl, Dl, 1)

    return (
        layer_out,
        input_grad,
        qkv_g[:Dl, :half],
        own(qkv_g[Dl, :half], query_bias.shape),
        qkv_g[:Dl, half : 2 * half],
        qkv_g[:Dl, 2 * half : 3 * half],
        own(qkv_g[Dl, 2 * half : 3 * half], value_bias.shape),
        qkv_g[:Dl, 3 * half :].T,
        vec_sums[0],
        vec_sums[1],
        vec_sums[2],
        inner_g[:Dl],
        own(inner_g[Dl], inner_bias.shape),
        outer_g[:Dl].T,
        vec_sums[3],
        vec_sums[4],
        vec_sums[5],
    )


def solution(mesh):
    rows3, flat = P("fsdp", "ctx", None), P("fsdp")
    wide, tall = P("fsdp", "tp"), P("tp", "fsdp")
    params = (wide, tall, wide, wide, tall, tall, flat, flat, flat, wide, tall, tall, flat, flat, flat)
    return jax.shard_map(
        per_device,
        mesh=mesh,
        in_specs=(rows3, P("fsdp")) + params + (rows3,),
        out_specs=(rows3, rows3) + params,
        check_vma=False,
    )
```

```python
import functools
import math

import jax
import jax.numpy as jnp
from jax import lax
from jax.experimental import pallas as pl
from jax.experimental.pallas import tpu as pltpu
from jax.sharding import PartitionSpec as P

HD = 64
BF = jnp.bfloat16
F32 = jnp.float32
ANY = pl.BlockSpec(memory_space=pl.ANY)
SMEM = pl.BlockSpec(memory_space=pltpu.SMEM)
EXTRA = 16
VMEM_LIMIT = 60 * 1024 * 1024


def dot_nn(a, b):
    return lax.dot_general(a, b, (((1,), (0,)), ((), ())), preferred_element_type=F32)


def dot_nt(a, b):
    return lax.dot_general(a, b, (((1,), (1,)), ((), ())), preferred_element_type=F32)


def dot_tn(a, b):
    return lax.dot_general(a, b, (((0,), (0,)), ((), ())), preferred_element_type=F32)


def const_spec(shape):
    zeros = (0,) * len(shape)
    return pl.BlockSpec(shape, lambda *_: zeros)


def cost(flops, moved, exps=0):
    return pl.CostEstimate(flops=int(flops), bytes_accessed=int(moved), transcendentals=int(exps))


def head_columns(pair, half_cols):
    per = half_cols // 128
    return pl.multiple_of(pair // per * (3 * half_cols) + pair % per * 128, 128)


def order_of(F, T, across):
    chip = [("fsdp", 1 << b) for b in range(1, F.bit_length() - 1)]
    pair = [("tp", 1 << b) for b in range(T.bit_length() - 1)]
    return chip + pair if across else pair + chip


def stacks(F, T, across):
    held, out = [(0, 0)], []
    steps = order_of(F, T, across)
    for n, (axis, bit) in enumerate(steps):
        got = [(df ^ bit, dt) if axis == "fsdp" else (df, dt ^ bit) for df, dt in held]
        if n == len(steps) - 1:
            out += [held, got]
        held = held + got
    return out + [[(df ^ 1, dt) for df, dt in part] for part in out]


def pieces_of(refs, F, T, across):
    return {
        at: ref.at[i] for ref, part in zip(refs, stacks(F, T, across)) for i, at in enumerate(part)
    }


def front_kernel(dims, meta, *refs):
    F, C, T, ns, span, D = dims
    n_w = F * T
    n_a = len(stacks(F, T, False))
    xs, low_refs, high_refs = refs[:C], refs[C : C + n_a], refs[C + n_a : C + 2 * n_a]
    x_out, w_out, qkv, e_out, linv_out, ctx, small, bias, sems = refs[C + 2 * n_a :]
    step = pl.program_id(0)
    NP = D // 128
    L = C * span
    Dl, half = D // F, D // T
    f = meta[0]
    c = meta[1]

    @pl.when(step == 0)
    def _():
        copies = [pltpu.make_async_copy(xs[k], x_out.at[k], sems.at[k]) for k in range(C)]
        qk = pieces_of(low_refs, F, T, False)
        vo = pieces_of(high_refs, F, T, True)
        for df in range(F):
            for dt in range(T):
                n = df * T + dt
                rows = pl.ds(pl.multiple_of((f ^ df) * Dl, 16), Dl)
                start = dt * 3 * half
                copies += [
                    pltpu.make_async_copy(
                        qk[df, dt].at[pl.ds(0, Dl)], w_out.at[rows, pl.ds(start, 2 * half)],
                        sems.at[C + n]),
                    pltpu.make_async_copy(
                        vo[df, dt].at[pl.ds(0, Dl), pl.ds(0, half)],
                        w_out.at[rows, pl.ds(start + 2 * half, half)], sems.at[C + n_w + n]),
                    pltpu.make_async_copy(
                        qk[df, dt].at[pl.ds(Dl, EXTRA), pl.ds(0, half)], small.at[n],
                        sems.at[C + 2 * n_w + n]),
                ]
        for copy in copies:
            copy.start()
        for copy in copies:
            copy.wait()
        bias[...] = jnp.zeros_like(bias)
        for dt in range(T):
            part = sum(small[df * T + dt, :2, :].astype(F32) for df in range(F))
            bias[:, dt * 3 * half : dt * 3 * half + half] = part[0:1]
            bias[:, (dt * 3 + 2) * half : (dt * 3 + 3) * half] = part[1:2]

        def project(j, carry):
            cols = pl.ds(pl.multiple_of(j * 384, 128), 384)
            y = dot_nn(x_out[...].reshape(L * ns, D), w_out[:, cols]) + bias[:, cols]
            qkv[:, :, :, cols] = y.astype(BF).reshape(C, ns, span, 384)
            return carry

        lax.fori_loop(0, 3 * D // 384, project, 0)

    s = step // NP
    pair = step % NP
    q_col = head_columns(pair, half)
    q = qkv[:, s, :, pl.ds(q_col, 128)].reshape(L, 128)
    k = qkv[:, s, :, pl.ds(pl.multiple_of(q_col + half, 128), 128)].reshape(L, 128)
    v = qkv[:, s, :, pl.ds(pl.multiple_of(q_col + 2 * half, 128), 128)].reshape(L, 128)
    low = lax.broadcasted_iota(jnp.int32, (L, 128), 1) < HD
    zero = jnp.zeros((), BF)
    one = jnp.ones((L, 128), BF)
    lane = lax.broadcasted_iota(jnp.int32, (1, L), 1)
    pos = ((lane // span) ^ c) * span + lane % span
    mask = jnp.where(pos < meta[2 + s], 0.0, -1e30)
    values = []
    for h in range(2):
        mine = low if h == 0 else jnp.logical_not(low)
        scores = dot_nt(q, jnp.where(mine, k, zero)) * (math.log2(math.e) / math.sqrt(HD)) + mask
        top = jnp.max(scores, axis=-1, keepdims=True)
        e_out[0, h * L : (h + 1) * L, :] = jnp.exp2(scores - top).astype(BF)
        values.append(
            jnp.concatenate([jnp.where(mine, v, zero), jnp.where(mine, one, zero)], axis=1)
        )
    acc = dot_nn(e_out[0, :L, :], values[0]) + dot_nn(e_out[0, L:, :], values[1])
    linv = 1.0 / acc[:, 128:]
    linv_out[0] = linv
    ctx[:, s, :, pl.ds(pl.multiple_of(pair * 128, 128), 128)] = (
        (acc[:, :128] * linv).astype(BF).reshape(C, span, 128)
    )


def front_call(dims, meta, xs, lows, highs):
    F, C, T, ns, span, D = dims
    NP, L = D // 128, C * span
    rows = ns * span
    shapes = [
        jax.ShapeDtypeStruct((C, rows, D), BF),
        jax.ShapeDtypeStruct((D, 3 * D), BF),
        jax.ShapeDtypeStruct((C, ns, span, 3 * D), BF),
        jax.ShapeDtypeStruct((ns * NP, 2 * L, L), BF),
        jax.ShapeDtypeStruct((ns * NP, L, 128), F32),
        jax.ShapeDtypeStruct((C, ns, span, D), BF),
    ]
    return pl.pallas_call(
        functools.partial(front_kernel, dims),
        name="front",
        grid=(ns * NP,),
        out_shape=shapes,
        in_specs=[SMEM] + [ANY] * (C + len(lows) + len(highs)),
        out_specs=[
            const_spec(shapes[0].shape),
            const_spec(shapes[1].shape),
            const_spec(shapes[2].shape),
            pl.BlockSpec((1, 2 * L, L), lambda i: (i, 0, 0)),
            pl.BlockSpec((1, L, 128), lambda i: (i, 0, 0)),
            const_spec(shapes[5].shape),
        ],
        scratch_shapes=[
            pltpu.VMEM((F * T, EXTRA, D // T), BF),
            pltpu.VMEM((1, 3 * D), F32),
            pltpu.SemaphoreType.DMA((C + 3 * F * T,)),
        ],
        compiler_params=pltpu.CompilerParams(vmem_limit_bytes=VMEM_LIMIT),
        cost_estimate=cost(2 * L * ns * D * 3 * D, 40e6, ns * 12 * L * L),
    )(meta, *xs, *lows, *highs)


def normalised(values):
    centre = values - jnp.mean(values, axis=-1, keepdims=True)
    spread = jnp.mean(centre * centre, axis=-1, keepdims=True)
    rstd = lax.rsqrt(spread + 1e-12)
    return centre * rstd, rstd


def norm_back(grad, gain, xhat, rstd):
    scaled = grad * gain
    first = jnp.mean(scaled, axis=-1, keepdims=True)
    second = jnp.mean(scaled * xhat, axis=-1, keepdims=True)
    return rstd * (scaled - first - xhat * second)


def rows_kernel(dims, FF, meta, x_ref, ctx_ref, *refs):
    F, C, T, ns, span, D = dims
    n_w = F * T
    n_a = len(stacks(F, T, False))
    cots = refs[:C]
    qk, vo, inner, outer = (
        pieces_of(refs[C + i * n_a : C + (i + 1) * n_a], F, T, i % 2 == 1) for i in range(4)
    )
    refs = refs[C + 4 * n_a :]
    los = refs[:C]
    (
        first_out, dctx_out, nl_out, act_out, og_out, ig_out, ag_out, sums,
        cot_s, lo_s, wi, wo, wout, gp_s, small, vec, inner_bias, sems, out_sems,
    ) = refs[C:]
    k = pl.program_id(0)
    R = ns * span
    Dl, half, fhalf = D // F, D // T, FF // T
    f = meta[0]
    c = meta[1]

    def weight_copies():
        copies = []
        for df in range(F):
            row = pl.multiple_of((f ^ df) * Dl, 16)
            for dt in range(T):
                n = df * T + dt
                rows = pl.ds(row, Dl)
                copies.append((
                    pltpu.make_async_copy(
                        vo[df, dt].at[pl.ds(0, Dl), pl.ds(half, half)],
                        wo.at[rows, pl.ds(dt * half, half)], sems.at[n]),
                    pltpu.make_async_copy(
                        inner[df, dt],
                        wi.at[rows, pl.ds(dt * fhalf, fhalf)], sems.at[n_w + n]),
                    pltpu.make_async_copy(
                        outer[df, dt],
                        wout.at[rows, pl.ds(dt * fhalf, fhalf)], sems.at[2 * n_w + n]),
                ) + tuple(
                    pltpu.make_async_copy(
                        (qk if part == 0 else vo)[df, dt].at[pl.ds(Dl, EXTRA)],
                        small.at[n, :, pl.ds(part * D, D)], sems.at[(3 + part) * n_w + n])
                    for part in range(2)
                ))
        return copies

    def cot_copies():
        return [
            pltpu.make_async_copy(cots[i], cot_s.at[i], sems.at[5 * n_w + i]) for i in range(C)
        ]

    @pl.when(k == 0)
    def _():
        copies = weight_copies()
        for which in range(5):
            for group in copies:
                group[which].start()
        for copy in cot_copies():
            copy.start()
        sums[...] = jnp.zeros_like(sums)
        for which in range(5):
            for group in copies:
                group[which].wait()
        for copy in cot_copies():
            copy.wait()
        for dt in range(T):
            part = sum(small[df * T + dt, :EXTRA, :].astype(F32) for df in range(F))
            inner_bias[:, dt * fhalf : (dt + 1) * fhalf] = part[2:3]
            if dt == 0:
                vec[...] = part[3:9, :D]

    def add_sum(row, value):
        sums[row : row + 1, :] += jnp.sum(value, axis=0, keepdims=True)

    out_bias, gain1, shift1 = vec[0:1, :], vec[1:2, :], vec[2:3, :]
    outer_bias, gain2, shift2 = vec[3:4, :], vec[4:5, :], vec[5:6, :]
    ctx_low = ctx_ref[0]
    before = x_ref[0].astype(F32) + dot_nt(ctx_low, wo[...]) + out_bias
    xhat1, rstd1 = normalised(before)
    normed = xhat1 * gain1 + shift1
    nl = normed.astype(BF)
    nl_out[0] = nl
    root = math.sqrt(2.0 / math.pi)
    chunk = 768
    for j in range(FF // chunk):
        cols = slice(j * chunk, (j + 1) * chunk)
        pre = dot_nn(nl, wi[:, cols]) + inner_bias[:, cols]
        square = pre * pre
        th = jnp.tanh(pre * (root + (root * 0.044715) * square))
        hp = 0.5 + 0.5 * th
        act_out[0, :, cols] = (pre * hp).astype(BF)
        gp_s[:, cols] = hp + (0.5 * pre) * (1.0 - th * th) * (
            root + (3.0 * root * 0.044715) * square
        )
    before2 = normed + dot_nt(act_out[0], wout[...]) + outer_bias
    xhat2, rstd2 = normalised(before2)
    row = lax.broadcasted_iota(jnp.int32, (R, 1), 0)
    position = (c ^ k) * span + row % span
    length = jnp.full((R, 1), meta[2], jnp.int32)
    for s in range(1, ns):
        length = jnp.where(row >= s * span, meta[2 + s], length)
    live = (position < length).astype(F32)
    lo_s[k] = (live * (xhat2 * gain2 + shift2)).astype(BF)
    for i in range(C):
        @pl.when(k == i)
        def _():
            pltpu.make_async_copy(lo_s.at[i], los[i], out_sems.at[i]).start()
    grad = cot_s[k].astype(F32) * live
    add_sum(4, grad * xhat2)
    add_sum(5, grad)
    second = norm_back(grad, gain2, xhat2, rstd2)
    og = second.astype(BF)
    og_out[0] = og
    add_sum(3, og.astype(F32))
    for j in range(FF // chunk):
        cols = slice(j * chunk, (j + 1) * chunk)
        ig = (dot_nn(og, wout[:, cols]) * gp_s[:, cols]).astype(BF)
        ig_out[0, :, cols] = ig
    ngrad = dot_nt(ig_out[0], wi[...]) + second
    add_sum(1, ngrad * xhat1)
    add_sum(2, ngrad)
    first = norm_back(ngrad, gain1, xhat1, rstd1)
    first_out[0] = first
    ag = first.astype(BF)
    ag_out[0] = ag
    add_sum(0, ag.astype(F32))
    dctx_out[0] = dot_nn(ag, wo[...]).astype(BF)

    @pl.when(k == C - 1)
    def _():
        for i in range(C):
            pltpu.make_async_copy(lo_s.at[i], los[i], out_sems.at[i]).wait()


def rows_call(dims, FF, meta, x_all, ctx, cots, weights):
    F, C, T, ns, span, D = dims
    R = ns * span
    tile = lambda n: pl.BlockSpec((1, R, n), lambda i: (i, 0, 0))
    widths = [(D, F32), (D, BF), (D, BF), (FF, BF), (D, BF), (FF, BF), (D, BF)]
    out_shape = (
        [jax.ShapeDtypeStruct((R, D), BF)] * C
        + [jax.ShapeDtypeStruct((C, R, n), kind) for n, kind in widths]
        + [jax.ShapeDtypeStruct((EXTRA, D), F32)]
    )
    n_w = F * T
    outs = pl.pallas_call(
        functools.partial(rows_kernel, dims, FF),
        name="rows",
        grid=(C,),
        out_shape=out_shape,
        in_specs=[SMEM, tile(D), tile(D)]
        + [ANY] * (C + len(weights)),
        out_specs=[ANY] * C
        + [tile(n) for n, _ in widths]
        + [const_spec((EXTRA, D))],
        scratch_shapes=[
            pltpu.VMEM((C, R, D), BF),
            pltpu.VMEM((C, R, D), BF),
            pltpu.VMEM((D, FF), BF),
            pltpu.VMEM((D, D), BF),
            pltpu.VMEM((D, FF), BF),
            pltpu.VMEM((R, FF), F32),
            pltpu.VMEM((n_w, EXTRA, FF // T), BF),
            pltpu.VMEM((6, D), F32),
            pltpu.VMEM((1, FF), F32),
            pltpu.SemaphoreType.DMA((5 * n_w + C,)),
            pltpu.SemaphoreType.DMA((C,)),
        ],
        compiler_params=pltpu.CompilerParams(vmem_limit_bytes=VMEM_LIMIT),
        cost_estimate=cost(4 * C * R * D * (2 * FF + D), 50e6, C * R * FF),
    )(meta, x_all, ctx, *cots, *weights)
    return outs[:C], outs[C:]


def back_kernel(dims, qkv, ctx, dctx, e_ref, linv, out, ds_s):
    F, C, T, ns, span, D = dims
    step = pl.program_id(0)
    NP, L, half = D // 128, C * span, D // T
    s = step // NP
    pair = step % NP
    q_col = head_columns(pair, half)
    k_col = pl.multiple_of(q_col + half, 128)
    v_col = pl.multiple_of(q_col + 2 * half, 128)
    c_col = pl.multiple_of(pair * 128, 128)
    q = qkv[:, s, :, pl.ds(q_col, 128)].reshape(L, 128)
    k = qkv[:, s, :, pl.ds(k_col, 128)].reshape(L, 128)
    v = qkv[:, s, :, pl.ds(v_col, 128)].reshape(L, 128)
    grad = dctx[:, s, :, pl.ds(c_col, 128)].reshape(L, 128).astype(F32) * linv[0]
    grad_low = grad.astype(BF)
    product = grad_low.astype(F32) * ctx[:, s, :, pl.ds(c_col, 128)].reshape(L, 128).astype(F32)
    low = lax.broadcasted_iota(jnp.int32, (L, 128), 1) < HD
    zero = jnp.zeros((), BF)
    qs, ks, gs = [], [], []
    for h in range(2):
        mine = low if h == 0 else jnp.logical_not(low)
        row_dot = jnp.sum(jnp.where(mine, product, 0.0), axis=-1, keepdims=True)
        probs_grad = dot_nt(grad_low, jnp.where(mine, v, zero))
        e = e_ref[0, h * L : (h + 1) * L, :].astype(F32)
        ds_s[h * L : (h + 1) * L, :] = (e * (probs_grad - row_dot)).astype(BF)
        qs.append(jnp.where(mine, q, zero))
        ks.append(jnp.where(mine, k, zero))
        gs.append(jnp.where(mine, grad_low, zero))
    scale = 1.0 / math.sqrt(HD)
    dq = (dot_nn(ds_s[:L, :], ks[0]) + dot_nn(ds_s[L:, :], ks[1])) * scale
    dk = dot_tn(ds_s[...], jnp.concatenate(qs, axis=0)) * scale
    dv = dot_tn(e_ref[0], jnp.concatenate(gs, axis=0))
    out[:, s, :, pl.ds(q_col, 128)] = dq.astype(BF).reshape(C, span, 128)
    out[:, s, :, pl.ds(k_col, 128)] = dk.astype(BF).reshape(C, span, 128)
    out[:, s, :, pl.ds(v_col, 128)] = dv.astype(BF).reshape(C, span, 128)


def back_call(dims, qkv, ctx, dctx, e, linv):
    F, C, T, ns, span, D = dims
    NP, L = D // 128, C * span
    return pl.pallas_call(
        functools.partial(back_kernel, dims),
        name="back",
        grid=(ns * NP,),
        out_shape=jax.ShapeDtypeStruct(qkv.shape, BF),
        in_specs=[
            const_spec(qkv.shape),
            const_spec(ctx.shape),
            const_spec(dctx.shape),
            pl.BlockSpec((1, 2 * L, L), lambda i: (i, 0, 0)),
            pl.BlockSpec((1, L, 128), lambda i: (i, 0, 0)),
        ],
        out_specs=const_spec(qkv.shape),
        scratch_shapes=[pltpu.VMEM((2 * L, L), BF)],
        compiler_params=pltpu.CompilerParams(vmem_limit_bytes=VMEM_LIMIT),
        cost_estimate=cost(ns * NP * 16 * L * L * 128, 30e6, 0),
    )(qkv, ctx, dctx, e, linv)


def input_kernel(C, dqkv, w, first, *refs):
    outs, (buf, sems) = refs[:C], refs[C:]
    k = pl.program_id(0)
    buf[k] = (dot_nt(dqkv[0], w[...]) + first[0]).astype(BF)
    for i in range(C):
        @pl.when(k == i)
        def _():
            pltpu.make_async_copy(buf.at[i], outs[i], sems.at[i]).start()

    @pl.when(k == C - 1)
    def _():
        for i in range(C):
            pltpu.make_async_copy(buf.at[i], outs[i], sems.at[i]).wait()


def input_call(dqkv, w, first):
    C, R, W = dqkv.shape
    D = w.shape[0]
    return pl.pallas_call(
        functools.partial(input_kernel, C),
        name="input_grad",
        grid=(C,),
        out_shape=[jax.ShapeDtypeStruct((R, D), BF)] * C,
        in_specs=[
            pl.BlockSpec((1, R, W), lambda i: (i, 0, 0)),
            const_spec(w.shape),
            pl.BlockSpec((1, R, D), lambda i: (i, 0, 0)),
        ],
        out_specs=[ANY] * C,
        scratch_shapes=[pltpu.VMEM((C, R, D), BF), pltpu.SemaphoreType.DMA((C,))],
        compiler_params=pltpu.CompilerParams(vmem_limit_bytes=VMEM_LIMIT),
        cost_estimate=cost(2 * C * R * D * W, 15e6, 0),
    )(dqkv, w, first)


COLS = 384


def weight_kernel(F, pers, with_sums, meta, *refs):
    n = len(pers)
    lefts, rights = refs[:n], refs[n : 2 * n]
    refs = refs[2 * n :]
    sums, refs = (refs[0], refs[1:]) if with_sums else (None, refs)
    keep, send, tile = refs[:3]
    turned = refs[3:]
    D = lefts[0].shape[1]
    Dl = D // F
    b = pl.program_id(1)

    @pl.when((pl.program_id(0) == 0) & (b == 0))
    def _():
        for left, left_t in zip(lefts, turned):
            left_t[:D, :] = left[...].T
            left_t[D:, :] = jnp.ones((EXTRA, left.shape[0]), BF)

    start = 0
    for right, left_t, per in zip(rights, turned, pers):
        @pl.when((b >= start) & (b < start + per))
        def _():
            tile[...] = dot_nn(left_t[...], right[...]).astype(BF)
        start += per
    if with_sums:
        for j in range(D // COLS):
            @pl.when(b == j)
            def _():
                tile[D:, :] = sums[:, j * COLS : (j + 1) * COLS].astype(BF)
    f = meta[0]
    for high in range(F // 2):
        for bit, out in ((0, keep), (1, send)):
            row = pl.multiple_of((f ^ (2 * high + bit)) * Dl, 16)
            out[high, 0, :Dl] = tile[pl.ds(row, Dl), :]
            out[high, 0, Dl:] = tile[D:, :]


def weight_call(dims, meta, pairs, sums=None):
    F, C, T, ns, span, D = dims
    rows = C * ns * span
    pairs = [(left.reshape(rows, -1), right.reshape(rows, -1)) for left, right in pairs]
    pers = [right.shape[1] // T // COLS for _, right in pairs]
    width = sum(pers) * COLS
    out = jax.ShapeDtypeStruct((F // 2, T, D // F + EXTRA, width), BF)
    out_spec = pl.BlockSpec((F // 2, 1, D // F + EXTRA, COLS), lambda a, b: (0, a, 0, b))
    right_specs, start = [], 0
    for per in pers:
        right_specs.append(
            pl.BlockSpec(
                (rows, COLS),
                lambda a, b, per=per, start=start: (0, a * per + jnp.clip(b - start, 0, per - 1)),
            )
        )
        start += per
    return pl.pallas_call(
        functools.partial(weight_kernel, F, pers, sums is not None),
        name="weight_grad",
        grid=(T, sum(pers)),
        out_shape=[out, out],
        in_specs=[SMEM]
        + [const_spec(left.shape) for left, _ in pairs]
        + right_specs
        + ([] if sums is None else [const_spec(sums.shape)]),
        out_specs=[out_spec, out_spec],
        scratch_shapes=[pltpu.VMEM((D + EXTRA, COLS), BF)]
        + [pltpu.VMEM((D + EXTRA, rows), BF) for _ in pairs],
        compiler_params=pltpu.CompilerParams(vmem_limit_bytes=VMEM_LIMIT),
        cost_estimate=cost(
            2 * rows * D * width * T, 2 * (rows * (D + width * T) + D * width * T), 0
        ),
    )(
        meta,
        *[left for left, _ in pairs],
        *[right for _, right in pairs],
        *([] if sums is None else [sums]),
    )


def xor_pairs(count, mask):
    return [(i, i ^ mask) for i in range(count)]


def after(value, others):
    return lax.optimization_barrier((value, *others))[0]


def added(a, b):
    return (a.astype(F32) + b.astype(F32)).astype(BF)


def per_device(
    tokens_in, seq_lengths, query_weight, query_bias, key_weight, value_weight, value_bias,
    output_weight, output_bias, attn_gain, attn_shift, inner_weight, inner_bias, outer_weight,
    outer_bias, ffn_gain, ffn_shift, cotangent,
):
    F, C, T = (lax.axis_size(a) for a in ("fsdp", "ctx", "tp"))
    f, c, t = (lax.axis_index(a) for a in ("fsdp", "ctx", "tp"))
    S, span, D = tokens_in.shape
    ns = S // (C * T)
    Dl, half = D // F, D // T
    fhalf = inner_weight.shape[1]
    FF = fhalf * T
    R = ns * span
    dims = (F, C, T, ns, span, D)

    def sequence_pieces(array):
        return [
            lax.dynamic_slice_in_dim(array, ((c ^ k) * T + t) * ns, ns, 0).reshape(R, D)
            for k in range(C)
        ]

    def ctx_moved(piece, k):
        return lax.ppermute(piece, "ctx", xor_pairs(C, k)) if k else piece

    def tp_moved(pieces):
        both = jnp.concatenate(pieces, axis=0) if len(pieces) > 1 else pieces[0]
        return [both] + [lax.ppermute(both, "tp", xor_pairs(T, dt)) for dt in range(1, T)]

    def to_slots(groups, kind):
        out = lax.full((S, span, D), 0, kind)
        pieces = {}
        for ks, group in groups:
            for dt, merged in enumerate(group):
                for i, k in enumerate(ks):
                    pieces[k, dt] = merged[i * R : (i + 1) * R]
        for k in range(C):
            for dt in range(T):
                got = pieces[k, dt]
                out = lax.dynamic_update_slice_in_dim(
                    out, got.reshape(ns, span, D).astype(kind), ((c ^ k) * T + (t ^ dt)) * ns, 0
                )
        return out

    def swapped(array, axis, bit):
        return lax.ppermute(array, axis, xor_pairs(lax.axis_size(axis), bit))

    def chip_start(shard, across):
        held = shard[None]
        for axis, bit in order_of(F, T, across)[:-1]:
            held = jnp.concatenate([held, swapped(held, axis, bit)], axis=0)
        return held

    def chip_end(held, across):
        axis, bit = order_of(F, T, across)[-1]
        return swapped(held, axis, bit)

    def both_cores(held, got, others=()):
        near = swapped(after(held, others), "fsdp", 1)
        return [held, got, near, swapped(got, "fsdp", 1)]

    def spread(array, width):
        rows, part = array.shape
        owner = lax.broadcasted_iota(jnp.int32, (rows, part * F), 1) // part
        return jnp.where(owner == f, jnp.tile(array, (1, F)), jnp.zeros((), BF)).reshape(-1, width)

    x_pieces = sequence_pieces(tokens_in)
    near_x = ctx_moved(x_pieces[1], 1)
    before = [near_x]
    x_pieces[1] = near_x
    for k in [*range(3, C, 2), *range(2, C, 2)]:
        x_pieces[k] = ctx_moved(after(x_pieces[k], before), k)
        before = [x_pieces[k]]
    vectors = jnp.stack([output_bias, attn_gain, attn_shift, outer_bias, ffn_gain, ffn_shift])
    small = [
        spread(query_bias, half), spread(value_bias, half), spread(inner_bias, fhalf),
        spread(vectors, D),
    ]
    small = jnp.concatenate([jnp.pad(a, ((0, 0), (0, fhalf - a.shape[1]))) for a in small])
    small = jnp.pad(small, ((0, EXTRA - small.shape[0]), (0, 0)))
    low = jnp.concatenate([query_weight, key_weight], axis=1)
    high = jnp.concatenate([value_weight, output_weight.T], axis=1)
    low = chip_start(jnp.concatenate([low, small[:, :D]], axis=0), False)
    high = chip_start(jnp.concatenate([high, small[:, D:]], axis=0), True)
    lows = both_cores(low, chip_end(after(low, [near_x]), False))
    highs = both_cores(high, chip_end(after(high, [near_x]), True))
    halfway = [lows[1], highs[1], *x_pieces[3::2]]
    inner = chip_start(after(inner_weight, halfway), False)
    outer = chip_start(after(outer_weight.T, halfway), True)
    inner_got = chip_end(after(inner, x_pieces[2::2]), False)
    outer_got = chip_end(after(outer, x_pieces[2::2]), True)
    cot_pieces = sequence_pieces(after(cotangent, [*x_pieces[1:], *lows, *highs]))
    cot_pieces = [ctx_moved(piece, k) for k, piece in enumerate(cot_pieces)]
    lengths = lax.dynamic_slice_in_dim(seq_lengths, (c * T + t) * ns, ns, 0)
    meta = jnp.concatenate([jnp.stack([f, c]).astype(jnp.int32), lengths])

    x_all, qkv_w, qkv, e, linv, ctx = front_call(
        dims, after(meta, [inner, outer]), x_pieces, lows, highs
    )
    inners = both_cores(inner, inner_got, [ctx, *cot_pieces[1:]])
    outers = both_cores(outer, outer_got, [ctx, *cot_pieces[1:]])
    los, (first, dctx, nl, act, og, inner_low, ag, sums) = rows_call(
        dims, FF, meta, x_all, ctx.reshape(C, R, D), cot_pieces, lows + highs + inners + outers,
    )

    def core_sum(keep, send):
        return added(keep, lax.ppermute(send, "fsdp", xor_pairs(F, 1)))

    def chip_sum(total, axis, dim):
        got = total
        while total.shape[dim] > 1:
            h = total.shape[dim] // 2
            stay, go = jnp.split(total, 2, axis=dim)
            got = swapped(go, axis, 2 * h if axis == "fsdp" else h)
            total = added(stay, got)
        return total, got

    def y_sum(total):
        return chip_sum(total, "fsdp", 0)

    def x_sum(total):
        return chip_sum(total, "tp", 1)

    def ctx_scatter(total):
        part = total.shape[1] // C
        mine = 0.0
        for k in range(C):
            block = lax.dynamic_slice_in_dim(total, (c ^ k) * part, part, 1)
            mine += ctx_moved(block, k).astype(F32)
        return mine.astype(BF)

    def ctx_gather(mine, like):
        part = mine.shape[1]
        out = like
        for k in range(C):
            out = lax.dynamic_update_slice_in_dim(out, ctx_moved(mine, k), (c ^ k) * part, 1)
        return out.astype(F32)

    outer_parts = weight_call(dims, meta, [(og, act)], sums)
    inner_parts = weight_call(dims, meta, [(after(nl, outer_parts), inner_low)])
    los = [ctx_moved(piece, k) for k, piece in enumerate(los)]
    keep, send = outer_parts
    outer_core = core_sum(keep, after(send, los[1:2]))
    keep, send = inner_parts
    inner_parts = keep, after(send, los[3:4])
    dctx = after(dctx, [outer_core, *inner_parts])
    dqkv = back_call(dims, qkv, ctx, dctx.reshape(ctx.shape), e, linv)
    inner_core = core_sum(*inner_parts)
    outer_y, outer_raw = y_sum(outer_core)
    even = range(2, C, 2)
    early = [0] + list(range(1, C, 2))
    early_lo = tp_moved([los[k] for k in early])
    first = after(first, [inner_core, outer_y, *los[1:], *early_lo[1:]])
    ins = input_call(dqkv.reshape(C, R, 3 * D), qkv_w, first)
    late_lo = tp_moved([after(los[k], [dqkv]) for k in even])
    outer_x, outer_raw = x_sum(outer_y)
    inner_y, inner_raw = y_sum(inner_core)
    ag = after(ag, ins)
    keep, send = weight_call(dims, meta, [(x_all, dqkv), (ag, ctx)])
    ig = [ctx_moved(piece, k) if k % 2 else piece for k, piece in enumerate(ins)]
    send = after(send, [outer_raw, inner_raw] + ig[1::2] + late_lo[1:])
    qkv_core = core_sum(keep, send)
    for k in even:
        ig[k] = ctx_moved(after(ins[k], ig[1::2]), k)
    outer_x = after(outer_x[0, 0], [qkv_core] + [ig[k] for k in even])
    outer_part = ctx_scatter(outer_x)
    early_ig = tp_moved(after(tuple(ig[k] for k in early), [qkv_core]))
    qkv_y, _ = y_sum(qkv_core)
    inner_x, _ = x_sum(after(inner_y, [qkv_core]))
    inner_x = after(inner_x[0, 0], [outer_part])
    inner_part = ctx_scatter(inner_x)
    outer_g = ctx_gather(after(outer_part, [inner_part]), outer_x)
    qkv_x, _ = x_sum(qkv_y)
    qkv_x = after(qkv_x[0, 0], [inner_part])
    qkv_part = ctx_scatter(qkv_x)
    late_ig = tp_moved([after(ig[k], [qkv_x]) for k in even])
    early_lo, late_lo = (after(tuple(part), [qkv_core]) for part in (early_lo, late_lo))
    early_ig = after(tuple(early_ig), [qkv_x])
    layer_out = to_slots([(early, early_lo), (list(even), late_lo)], BF)
    input_grad = to_slots([(early, early_ig), (list(even), late_ig)], F32)
    inner_g = ctx_gather(after(inner_part, [qkv_y]), inner_x)
    qkv_g = ctx_gather(qkv_part, qkv_x)

    def own(row, shape):
        whole = row.reshape(shape[0], shape[1] * F)
        return lax.dynamic_slice_in_dim(whole, f * shape[1], shape[1], 1)

    vec_sums = lax.dynamic_slice_in_dim(outer_g[Dl : Dl + 6, :D], f * Dl, Dl, 1)

    return (
        layer_out,
        input_grad,
        qkv_g[:Dl, :half],
        own(qkv_g[Dl, :half], query_bias.shape),
        qkv_g[:Dl, half : 2 * half],
        qkv_g[:Dl, 2 * half : 3 * half],
        own(qkv_g[Dl, 2 * half : 3 * half], value_bias.shape),
        qkv_g[:Dl, 3 * half :].T,
        vec_sums[0],
        vec_sums[1],
        vec_sums[2],
        inner_g[:Dl],
        own(inner_g[Dl], inner_bias.shape),
        outer_g[:Dl].T,
        vec_sums[3],
        vec_sums[4],
        vec_sums[5],
    )


def solution(mesh):
    rows3, flat = P("fsdp", "ctx", None), P("fsdp")
    wide, tall = P("fsdp", "tp"), P("tp", "fsdp")
    params = (wide, tall, wide, wide, tall, tall, flat, flat, flat, wide, tall, tall, flat, flat, flat)
    return jax.shard_map(
        per_device,
        mesh=mesh,
        in_specs=(rows3, P("fsdp")) + params + (rows3,),
        out_specs=(rows3, rows3) + params,
        check_vma=False,
    )
```

```python
import functools
import math

import jax
import jax.numpy as jnp
from jax import lax
from jax.experimental import pallas as pl
from jax.experimental.pallas import tpu as pltpu
from jax.sharding import PartitionSpec as P

HD = 64
BF = jnp.bfloat16
F32 = jnp.float32
ANY = pl.BlockSpec(memory_space=pl.ANY)
SMEM = pl.BlockSpec(memory_space=pltpu.SMEM)
EXTRA = 16
VMEM_LIMIT = 60 * 1024 * 1024


def dot_nn(a, b):
    return lax.dot_general(a, b, (((1,), (0,)), ((), ())), preferred_element_type=F32)


def dot_nt(a, b):
    return lax.dot_general(a, b, (((1,), (1,)), ((), ())), preferred_element_type=F32)


def dot_tn(a, b):
    return lax.dot_general(a, b, (((0,), (0,)), ((), ())), preferred_element_type=F32)


def const_spec(shape):
    zeros = (0,) * len(shape)
    return pl.BlockSpec(shape, lambda *_: zeros)


def cost(flops, moved, exps=0):
    return pl.CostEstimate(flops=int(flops), bytes_accessed=int(moved), transcendentals=int(exps))


def head_columns(pair, half_cols):
    per = half_cols // 128
    return pl.multiple_of(pair // per * (3 * half_cols) + pair % per * 128, 128)


def order_of(F, T, across):
    chip = [("fsdp", 1 << b) for b in range(1, F.bit_length() - 1)]
    pair = [("tp", 1 << b) for b in range(T.bit_length() - 1)]
    return chip + pair if across else pair + chip


def stacks(F, T, across):
    held, out = [(0, 0)], []
    steps = order_of(F, T, across)
    for n, (axis, bit) in enumerate(steps):
        got = [(df ^ bit, dt) if axis == "fsdp" else (df, dt ^ bit) for df, dt in held]
        if n == len(steps) - 1:
            out += [held, got]
        held = held + got
    return out + [[(df ^ 1, dt) for df, dt in part] for part in out]


def pieces_of(refs, F, T, across):
    return {
        at: ref.at[i] for ref, part in zip(refs, stacks(F, T, across)) for i, at in enumerate(part)
    }


def front_kernel(dims, meta, *refs):
    F, C, T, ns, span, D = dims
    n_w = F * T
    n_a = len(stacks(F, T, False))
    xs, low_refs, high_refs = refs[:C], refs[C : C + n_a], refs[C + n_a : C + 2 * n_a]
    x_out, w_out, qkv, e_out, linv_out, ctx, small, bias, sems = refs[C + 2 * n_a :]
    step = pl.program_id(0)
    NP = D // 128
    L = C * span
    Dl, half = D // F, D // T
    f = meta[0]
    c = meta[1]

    @pl.when(step == 0)
    def _():
        copies = [pltpu.make_async_copy(xs[k], x_out.at[k], sems.at[k]) for k in range(C)]
        qk = pieces_of(low_refs, F, T, False)
        vo = pieces_of(high_refs, F, T, True)
        for df in range(F):
            for dt in range(T):
                n = df * T + dt
                rows = pl.ds(pl.multiple_of((f ^ df) * Dl, 16), Dl)
                start = dt * 3 * half
                copies += [
                    pltpu.make_async_copy(
                        qk[df, dt].at[pl.ds(0, Dl)], w_out.at[rows, pl.ds(start, 2 * half)],
                        sems.at[C + n]),
                    pltpu.make_async_copy(
                        vo[df, dt].at[pl.ds(0, Dl), pl.ds(0, half)],
                        w_out.at[rows, pl.ds(start + 2 * half, half)], sems.at[C + n_w + n]),
                    pltpu.make_async_copy(
                        qk[df, dt].at[pl.ds(Dl, EXTRA), pl.ds(0, half)], small.at[n],
                        sems.at[C + 2 * n_w + n]),
                ]
        for copy in copies:
            copy.start()
        for copy in copies:
            copy.wait()
        bias[...] = jnp.zeros_like(bias)
        for dt in range(T):
            part = sum(small[df * T + dt, :2, :].astype(F32) for df in range(F))
            bias[:, dt * 3 * half : dt * 3 * half + half] = part[0:1]
            bias[:, (dt * 3 + 2) * half : (dt * 3 + 3) * half] = part[1:2]

        def project(j, carry):
            cols = pl.ds(pl.multiple_of(j * 384, 128), 384)
            y = dot_nn(x_out[...].reshape(L * ns, D), w_out[:, cols]) + bias[:, cols]
            qkv[:, :, :, cols] = y.astype(BF).reshape(C, ns, span, 384)
            return carry

        lax.fori_loop(0, 3 * D // 384, project, 0)

    s = step // NP
    pair = step % NP
    q_col = head_columns(pair, half)
    q = qkv[:, s, :, pl.ds(q_col, 128)].reshape(L, 128)
    k = qkv[:, s, :, pl.ds(pl.multiple_of(q_col + half, 128), 128)].reshape(L, 128)
    v = qkv[:, s, :, pl.ds(pl.multiple_of(q_col + 2 * half, 128), 128)].reshape(L, 128)
    low = lax.broadcasted_iota(jnp.int32, (L, 128), 1) < HD
    zero = jnp.zeros((), BF)
    one = jnp.ones((L, 128), BF)
    lane = lax.broadcasted_iota(jnp.int32, (1, L), 1)
    pos = ((lane // span) ^ c) * span + lane % span
    mask = jnp.where(pos < meta[2 + s], 0.0, -1e30)
    values = []
    for h in range(2):
        mine = low if h == 0 else jnp.logical_not(low)
        scores = dot_nt(q, jnp.where(mine, k, zero)) * (math.log2(math.e) / math.sqrt(HD)) + mask
        top = jnp.max(scores, axis=-1, keepdims=True)
        e_out[0, h * L : (h + 1) * L, :] = jnp.exp2(scores - top).astype(BF)
        values.append(
            jnp.concatenate([jnp.where(mine, v, zero), jnp.where(mine, one, zero)], axis=1)
        )
    acc = dot_nn(e_out[0, :L, :], values[0]) + dot_nn(e_out[0, L:, :], values[1])
    linv = 1.0 / acc[:, 128:]
    linv_out[0] = linv
    ctx[:, s, :, pl.ds(pl.multiple_of(pair * 128, 128), 128)] = (
        (acc[:, :128] * linv).astype(BF).reshape(C, span, 128)
    )


def front_call(dims, meta, xs, lows, highs):
    F, C, T, ns, span, D = dims
    NP, L = D // 128, C * span
    rows = ns * span
    shapes = [
        jax.ShapeDtypeStruct((C, rows, D), BF),
        jax.ShapeDtypeStruct((D, 3 * D), BF),
        jax.ShapeDtypeStruct((C, ns, span, 3 * D), BF),
        jax.ShapeDtypeStruct((ns * NP, 2 * L, L), BF),
        jax.ShapeDtypeStruct((ns * NP, L, 128), F32),
        jax.ShapeDtypeStruct((C, ns, span, D), BF),
    ]
    return pl.pallas_call(
        functools.partial(front_kernel, dims),
        name="front",
        grid=(ns * NP,),
        out_shape=shapes,
        in_specs=[SMEM] + [ANY] * (C + len(lows) + len(highs)),
        out_specs=[
            const_spec(shapes[0].shape),
            const_spec(shapes[1].shape),
            const_spec(shapes[2].shape),
            pl.BlockSpec((1, 2 * L, L), lambda i: (i, 0, 0)),
            pl.BlockSpec((1, L, 128), lambda i: (i, 0, 0)),
            const_spec(shapes[5].shape),
        ],
        scratch_shapes=[
            pltpu.VMEM((F * T, EXTRA, D // T), BF),
            pltpu.VMEM((1, 3 * D), F32),
            pltpu.SemaphoreType.DMA((C + 3 * F * T,)),
        ],
        compiler_params=pltpu.CompilerParams(vmem_limit_bytes=VMEM_LIMIT),
        cost_estimate=cost(2 * L * ns * D * 3 * D, 40e6, ns * 12 * L * L),
    )(meta, *xs, *lows, *highs)


def normalised(values):
    centre = values - jnp.mean(values, axis=-1, keepdims=True)
    spread = jnp.mean(centre * centre, axis=-1, keepdims=True)
    rstd = lax.rsqrt(spread + 1e-12)
    return centre * rstd, rstd


def norm_back(grad, gain, xhat, rstd):
    scaled = grad * gain
    first = jnp.mean(scaled, axis=-1, keepdims=True)
    second = jnp.mean(scaled * xhat, axis=-1, keepdims=True)
    return rstd * (scaled - first - xhat * second)


def rows_kernel(dims, FF, meta, x_ref, ctx_ref, *refs):
    F, C, T, ns, span, D = dims
    n_w = F * T
    n_a = len(stacks(F, T, False))
    cots = refs[:C]
    qk, vo, inner, outer = (
        pieces_of(refs[C + i * n_a : C + (i + 1) * n_a], F, T, i % 2 == 1) for i in range(4)
    )
    refs = refs[C + 4 * n_a :]
    los = refs[:C]
    (
        first_out, dctx_out, nl_out, act_out, og_out, ig_out, ag_out, sums,
        cot_s, lo_s, wi, wo, wout, gp_s, small, vec, inner_bias, sems, out_sems,
    ) = refs[C:]
    k = pl.program_id(0)
    R = ns * span
    Dl, half, fhalf = D // F, D // T, FF // T
    f = meta[0]
    c = meta[1]

    def weight_copies():
        copies = []
        for df in range(F):
            row = pl.multiple_of((f ^ df) * Dl, 16)
            for dt in range(T):
                n = df * T + dt
                rows = pl.ds(row, Dl)
                copies.append((
                    pltpu.make_async_copy(
                        vo[df, dt].at[pl.ds(0, Dl), pl.ds(half, half)],
                        wo.at[rows, pl.ds(dt * half, half)], sems.at[n]),
                    pltpu.make_async_copy(
                        inner[df, dt],
                        wi.at[rows, pl.ds(dt * fhalf, fhalf)], sems.at[n_w + n]),
                    pltpu.make_async_copy(
                        outer[df, dt],
                        wout.at[rows, pl.ds(dt * fhalf, fhalf)], sems.at[2 * n_w + n]),
                ) + tuple(
                    pltpu.make_async_copy(
                        (qk if part == 0 else vo)[df, dt].at[pl.ds(Dl, EXTRA)],
                        small.at[n, :, pl.ds(part * D, D)], sems.at[(3 + part) * n_w + n])
                    for part in range(2)
                ))
        return copies

    def cot_copies():
        return [
            pltpu.make_async_copy(cots[i], cot_s.at[i], sems.at[5 * n_w + i]) for i in range(C)
        ]

    @pl.when(k == 0)
    def _():
        copies = weight_copies()
        for which in range(5):
            for group in copies:
                group[which].start()
        for copy in cot_copies():
            copy.start()
        sums[...] = jnp.zeros_like(sums)
        for which in range(5):
            for group in copies:
                group[which].wait()
        for copy in cot_copies():
            copy.wait()
        for dt in range(T):
            part = sum(small[df * T + dt, :EXTRA, :].astype(F32) for df in range(F))
            inner_bias[:, dt * fhalf : (dt + 1) * fhalf] = part[2:3]
            if dt == 0:
                vec[...] = part[3:9, :D]

    def add_sum(row, value):
        sums[row : row + 1, :] += jnp.sum(value, axis=0, keepdims=True)

    out_bias, gain1, shift1 = vec[0:1, :], vec[1:2, :], vec[2:3, :]
    outer_bias, gain2, shift2 = vec[3:4, :], vec[4:5, :], vec[5:6, :]
    ctx_low = ctx_ref[0]
    before = x_ref[0].astype(F32) + dot_nt(ctx_low, wo[...]) + out_bias
    xhat1, rstd1 = normalised(before)
    normed = xhat1 * gain1 + shift1
    nl = normed.astype(BF)
    nl_out[0] = nl
    root = math.sqrt(2.0 / math.pi)
    chunk = 768
    for j in range(FF // chunk):
        cols = slice(j * chunk, (j + 1) * chunk)
        pre = dot_nn(nl, wi[:, cols]) + inner_bias[:, cols]
        square = pre * pre
        th = jnp.tanh(pre * (root + (root * 0.044715) * square))
        hp = 0.5 + 0.5 * th
        act_out[0, :, cols] = (pre * hp).astype(BF)
        gp_s[:, cols] = hp + (0.5 * pre) * (1.0 - th * th) * (
            root + (3.0 * root * 0.044715) * square
        )
    before2 = normed + dot_nt(act_out[0], wout[...]) + outer_bias
    xhat2, rstd2 = normalised(before2)
    row = lax.broadcasted_iota(jnp.int32, (R, 1), 0)
    position = (c ^ k) * span + row % span
    length = jnp.full((R, 1), meta[2], jnp.int32)
    for s in range(1, ns):
        length = jnp.where(row >= s * span, meta[2 + s], length)
    live = (position < length).astype(F32)
    lo_s[k] = (live * (xhat2 * gain2 + shift2)).astype(BF)
    for i in range(C):
        @pl.when(k == i)
        def _():
            pltpu.make_async_copy(lo_s.at[i], los[i], out_sems.at[i]).start()
    grad = cot_s[k].astype(F32) * live
    add_sum(4, grad * xhat2)
    add_sum(5, grad)
    second = norm_back(grad, gain2, xhat2, rstd2)
    og = second.astype(BF)
    og_out[0] = og
    add_sum(3, og.astype(F32))
    for j in range(FF // chunk):
        cols = slice(j * chunk, (j + 1) * chunk)
        ig = (dot_nn(og, wout[:, cols]) * gp_s[:, cols]).astype(BF)
        ig_out[0, :, cols] = ig
    ngrad = dot_nt(ig_out[0], wi[...]) + second
    add_sum(1, ngrad * xhat1)
    add_sum(2, ngrad)
    first = norm_back(ngrad, gain1, xhat1, rstd1)
    first_out[0] = first
    ag = first.astype(BF)
    ag_out[0] = ag
    add_sum(0, ag.astype(F32))
    dctx_out[0] = dot_nn(ag, wo[...]).astype(BF)

    @pl.when(k == C - 1)
    def _():
        for i in range(C):
            pltpu.make_async_copy(lo_s.at[i], los[i], out_sems.at[i]).wait()


def rows_call(dims, FF, meta, x_all, ctx, cots, weights):
    F, C, T, ns, span, D = dims
    R = ns * span
    tile = lambda n: pl.BlockSpec((1, R, n), lambda i: (i, 0, 0))
    widths = [(D, F32), (D, BF), (D, BF), (FF, BF), (D, BF), (FF, BF), (D, BF)]
    out_shape = (
        [jax.ShapeDtypeStruct((R, D), BF)] * C
        + [jax.ShapeDtypeStruct((C, R, n), kind) for n, kind in widths]
        + [jax.ShapeDtypeStruct((EXTRA, D), F32)]
    )
    n_w = F * T
    outs = pl.pallas_call(
        functools.partial(rows_kernel, dims, FF),
        name="rows",
        grid=(C,),
        out_shape=out_shape,
        in_specs=[SMEM, tile(D), tile(D)]
        + [ANY] * (C + len(weights)),
        out_specs=[ANY] * C
        + [tile(n) for n, _ in widths]
        + [const_spec((EXTRA, D))],
        scratch_shapes=[
            pltpu.VMEM((C, R, D), BF),
            pltpu.VMEM((C, R, D), BF),
            pltpu.VMEM((D, FF), BF),
            pltpu.VMEM((D, D), BF),
            pltpu.VMEM((D, FF), BF),
            pltpu.VMEM((R, FF), F32),
            pltpu.VMEM((n_w, EXTRA, FF // T), BF),
            pltpu.VMEM((6, D), F32),
            pltpu.VMEM((1, FF), F32),
            pltpu.SemaphoreType.DMA((5 * n_w + C,)),
            pltpu.SemaphoreType.DMA((C,)),
        ],
        compiler_params=pltpu.CompilerParams(vmem_limit_bytes=VMEM_LIMIT),
        cost_estimate=cost(4 * C * R * D * (2 * FF + D), 50e6, C * R * FF),
    )(meta, x_all, ctx, *cots, *weights)
    return outs[:C], outs[C:]


def back_kernel(dims, qkv, ctx, dctx, e_ref, linv, out, ds_s):
    F, C, T, ns, span, D = dims
    step = pl.program_id(0)
    NP, L, half = D // 128, C * span, D // T
    s = step // NP
    pair = step % NP
    q_col = head_columns(pair, half)
    k_col = pl.multiple_of(q_col + half, 128)
    v_col = pl.multiple_of(q_col + 2 * half, 128)
    c_col = pl.multiple_of(pair * 128, 128)
    q = qkv[:, s, :, pl.ds(q_col, 128)].reshape(L, 128)
    k = qkv[:, s, :, pl.ds(k_col, 128)].reshape(L, 128)
    v = qkv[:, s, :, pl.ds(v_col, 128)].reshape(L, 128)
    grad = dctx[:, s, :, pl.ds(c_col, 128)].reshape(L, 128).astype(F32) * linv[0]
    grad_low = grad.astype(BF)
    product = grad_low.astype(F32) * ctx[:, s, :, pl.ds(c_col, 128)].reshape(L, 128).astype(F32)
    low = lax.broadcasted_iota(jnp.int32, (L, 128), 1) < HD
    zero = jnp.zeros((), BF)
    qs, ks, gs = [], [], []
    for h in range(2):
        mine = low if h == 0 else jnp.logical_not(low)
        row_dot = jnp.sum(jnp.where(mine, product, 0.0), axis=-1, keepdims=True)
        probs_grad = dot_nt(grad_low, jnp.where(mine, v, zero))
        e = e_ref[0, h * L : (h + 1) * L, :].astype(F32)
        ds_s[h * L : (h + 1) * L, :] = (e * (probs_grad - row_dot)).astype(BF)
        qs.append(jnp.where(mine, q, zero))
        ks.append(jnp.where(mine, k, zero))
        gs.append(jnp.where(mine, grad_low, zero))
    scale = 1.0 / math.sqrt(HD)
    dq = (dot_nn(ds_s[:L, :], ks[0]) + dot_nn(ds_s[L:, :], ks[1])) * scale
    dk = dot_tn(ds_s[...], jnp.concatenate(qs, axis=0)) * scale
    dv = dot_tn(e_ref[0], jnp.concatenate(gs, axis=0))
    out[:, s, :, pl.ds(q_col, 128)] = dq.astype(BF).reshape(C, span, 128)
    out[:, s, :, pl.ds(k_col, 128)] = dk.astype(BF).reshape(C, span, 128)
    out[:, s, :, pl.ds(v_col, 128)] = dv.astype(BF).reshape(C, span, 128)


def back_call(dims, qkv, ctx, dctx, e, linv):
    F, C, T, ns, span, D = dims
    NP, L = D // 128, C * span
    return pl.pallas_call(
        functools.partial(back_kernel, dims),
        name="back",
        grid=(ns * NP,),
        out_shape=jax.ShapeDtypeStruct(qkv.shape, BF),
        in_specs=[
            const_spec(qkv.shape),
            const_spec(ctx.shape),
            const_spec(dctx.shape),
            pl.BlockSpec((1, 2 * L, L), lambda i: (i, 0, 0)),
            pl.BlockSpec((1, L, 128), lambda i: (i, 0, 0)),
        ],
        out_specs=const_spec(qkv.shape),
        scratch_shapes=[pltpu.VMEM((2 * L, L), BF)],
        compiler_params=pltpu.CompilerParams(vmem_limit_bytes=VMEM_LIMIT),
        cost_estimate=cost(ns * NP * 16 * L * L * 128, 30e6, 0),
    )(qkv, ctx, dctx, e, linv)


def input_kernel(C, dqkv, w, first, *refs):
    outs, (buf, sems) = refs[:C], refs[C:]
    k = pl.program_id(0)
    buf[k] = (dot_nt(dqkv[0], w[...]) + first[0]).astype(BF)
    for i in range(C):
        @pl.when(k == i)
        def _():
            pltpu.make_async_copy(buf.at[i], outs[i], sems.at[i]).start()

    @pl.when(k == C - 1)
    def _():
        for i in range(C):
            pltpu.make_async_copy(buf.at[i], outs[i], sems.at[i]).wait()


def input_call(dqkv, w, first):
    C, R, W = dqkv.shape
    D = w.shape[0]
    return pl.pallas_call(
        functools.partial(input_kernel, C),
        name="input_grad",
        grid=(C,),
        out_shape=[jax.ShapeDtypeStruct((R, D), BF)] * C,
        in_specs=[
            pl.BlockSpec((1, R, W), lambda i: (i, 0, 0)),
            const_spec(w.shape),
            pl.BlockSpec((1, R, D), lambda i: (i, 0, 0)),
        ],
        out_specs=[ANY] * C,
        scratch_shapes=[pltpu.VMEM((C, R, D), BF), pltpu.SemaphoreType.DMA((C,))],
        compiler_params=pltpu.CompilerParams(vmem_limit_bytes=VMEM_LIMIT),
        cost_estimate=cost(2 * C * R * D * W, 15e6, 0),
    )(dqkv, w, first)


COLS = 384


def weight_kernel(F, pers, with_sums, meta, *refs):
    n = len(pers)
    lefts, rights = refs[:n], refs[n : 2 * n]
    refs = refs[2 * n :]
    sums, refs = (refs[0], refs[1:]) if with_sums else (None, refs)
    keep, send, tile = refs[:3]
    turned = refs[3:]
    D = lefts[0].shape[1]
    Dl = D // F
    b = pl.program_id(1)

    @pl.when((pl.program_id(0) == 0) & (b == 0))
    def _():
        for left, left_t in zip(lefts, turned):
            left_t[:D, :] = left[...].T
            left_t[D:, :] = jnp.ones((EXTRA, left.shape[0]), BF)

    start = 0
    for right, left_t, per in zip(rights, turned, pers):
        @pl.when((b >= start) & (b < start + per))
        def _():
            tile[...] = dot_nn(left_t[...], right[...]).astype(BF)
        start += per
    if with_sums:
        for j in range(D // COLS):
            @pl.when(b == j)
            def _():
                tile[D:, :] = sums[:, j * COLS : (j + 1) * COLS].astype(BF)
    f = meta[0]
    for high in range(F // 2):
        for bit, out in ((0, keep), (1, send)):
            row = pl.multiple_of((f ^ (2 * high + bit)) * Dl, 16)
            out[high, 0, :Dl] = tile[pl.ds(row, Dl), :]
            out[high, 0, Dl:] = tile[D:, :]


def weight_call(dims, meta, pairs, sums=None):
    F, C, T, ns, span, D = dims
    rows = C * ns * span
    pairs = [(left.reshape(rows, -1), right.reshape(rows, -1)) for left, right in pairs]
    pers = [right.shape[1] // T // COLS for _, right in pairs]
    width = sum(pers) * COLS
    out = jax.ShapeDtypeStruct((F // 2, T, D // F + EXTRA, width), BF)
    out_spec = pl.BlockSpec((F // 2, 1, D // F + EXTRA, COLS), lambda a, b: (0, a, 0, b))
    right_specs, start = [], 0
    for per in pers:
        right_specs.append(
            pl.BlockSpec(
                (rows, COLS),
                lambda a, b, per=per, start=start: (0, a * per + jnp.clip(b - start, 0, per - 1)),
            )
        )
        start += per
    return pl.pallas_call(
        functools.partial(weight_kernel, F, pers, sums is not None),
        name="weight_grad",
        grid=(T, sum(pers)),
        out_shape=[out, out],
        in_specs=[SMEM]
        + [const_spec(left.shape) for left, _ in pairs]
        + right_specs
        + ([] if sums is None else [const_spec(sums.shape)]),
        out_specs=[out_spec, out_spec],
        scratch_shapes=[pltpu.VMEM((D + EXTRA, COLS), BF)]
        + [pltpu.VMEM((D + EXTRA, rows), BF) for _ in pairs],
        compiler_params=pltpu.CompilerParams(vmem_limit_bytes=VMEM_LIMIT),
        cost_estimate=cost(
            2 * rows * D * width * T, 2 * (rows * (D + width * T) + D * width * T), 0
        ),
    )(
        meta,
        *[left for left, _ in pairs],
        *[right for _, right in pairs],
        *([] if sums is None else [sums]),
    )


def xor_pairs(count, mask):
    return [(i, i ^ mask) for i in range(count)]


def after(value, others):
    return lax.optimization_barrier((value, *others))[0]


def added(a, b):
    return (a.astype(F32) + b.astype(F32)).astype(BF)


def per_device(
    tokens_in, seq_lengths, query_weight, query_bias, key_weight, value_weight, value_bias,
    output_weight, output_bias, attn_gain, attn_shift, inner_weight, inner_bias, outer_weight,
    outer_bias, ffn_gain, ffn_shift, cotangent,
):
    F, C, T = (lax.axis_size(a) for a in ("fsdp", "ctx", "tp"))
    f, c, t = (lax.axis_index(a) for a in ("fsdp", "ctx", "tp"))
    S, span, D = tokens_in.shape
    ns = S // (C * T)
    Dl, half = D // F, D // T
    fhalf = inner_weight.shape[1]
    FF = fhalf * T
    R = ns * span
    dims = (F, C, T, ns, span, D)

    def sequence_pieces(array):
        return [
            lax.dynamic_slice_in_dim(array, ((c ^ k) * T + t) * ns, ns, 0).reshape(R, D)
            for k in range(C)
        ]

    def ctx_moved(piece, k):
        return lax.ppermute(piece, "ctx", xor_pairs(C, k)) if k else piece

    def tp_moved(pieces):
        both = jnp.concatenate(pieces, axis=0) if len(pieces) > 1 else pieces[0]
        return [both] + [lax.ppermute(both, "tp", xor_pairs(T, dt)) for dt in range(1, T)]

    def to_slots(groups, kind):
        out = lax.full((S, span, D), 0, kind)
        pieces = {}
        for ks, group in groups:
            for dt, merged in enumerate(group):
                for i, k in enumerate(ks):
                    pieces[k, dt] = merged[i * R : (i + 1) * R]
        for k in range(C):
            for dt in range(T):
                got = pieces[k, dt]
                out = lax.dynamic_update_slice_in_dim(
                    out, got.reshape(ns, span, D).astype(kind), ((c ^ k) * T + (t ^ dt)) * ns, 0
                )
        return out

    def swapped(array, axis, bit):
        return lax.ppermute(array, axis, xor_pairs(lax.axis_size(axis), bit))

    def chip_start(shard, across):
        held = shard[None]
        for axis, bit in order_of(F, T, across)[:-1]:
            held = jnp.concatenate([held, swapped(held, axis, bit)], axis=0)
        return held

    def chip_end(held, across):
        axis, bit = order_of(F, T, across)[-1]
        return swapped(held, axis, bit)

    def both_cores(held, got, others=()):
        near = swapped(after(held, others), "fsdp", 1)
        return [held, got, near, swapped(got, "fsdp", 1)]

    def spread(array, width):
        rows, part = array.shape
        owner = lax.broadcasted_iota(jnp.int32, (rows, part * F), 1) // part
        return jnp.where(owner == f, jnp.tile(array, (1, F)), jnp.zeros((), BF)).reshape(-1, width)

    x_pieces = sequence_pieces(tokens_in)
    near_x = ctx_moved(x_pieces[1], 1)
    before = [near_x]
    x_pieces[1] = near_x
    for k in [*range(3, C, 2), *range(2, C, 2)]:
        x_pieces[k] = ctx_moved(after(x_pieces[k], before), k)
        before = [x_pieces[k]]
    vectors = [output_bias, attn_gain, attn_shift, outer_bias, ffn_gain, ffn_shift]
    vectors = jnp.concatenate(vectors).reshape(len(vectors), Dl)
    small = [
        spread(query_bias, half), spread(value_bias, half), spread(inner_bias, fhalf),
        spread(vectors, D),
    ]
    small = jnp.concatenate([jnp.pad(a, ((0, 0), (0, fhalf - a.shape[1]))) for a in small])
    small = jnp.pad(small, ((0, EXTRA - small.shape[0]), (0, 0)))
    low = jnp.concatenate([query_weight, key_weight], axis=1)
    high = jnp.concatenate([value_weight, output_weight.T], axis=1)
    low = chip_start(jnp.concatenate([low, small[:, :D]], axis=0), False)
    high = chip_start(jnp.concatenate([high, small[:, D:]], axis=0), True)
    lows = both_cores(low, chip_end(after(low, [near_x]), False))
    highs = both_cores(high, chip_end(after(high, [near_x]), True))
    halfway = [lows[1], highs[1], *x_pieces[3::2]]
    inner = chip_start(after(inner_weight, halfway), False)
    outer = chip_start(after(outer_weight.T, halfway), True)
    inner_got = chip_end(after(inner, x_pieces[2::2]), False)
    outer_got = chip_end(after(outer, x_pieces[2::2]), True)
    cot_pieces = sequence_pieces(after(cotangent, [*x_pieces[1:], *lows, *highs]))
    cot_pieces = [ctx_moved(piece, k) for k, piece in enumerate(cot_pieces)]
    lengths = lax.dynamic_slice_in_dim(seq_lengths, (c * T + t) * ns, ns, 0)
    meta = jnp.concatenate([jnp.stack([f, c]).astype(jnp.int32), lengths])

    x_all, qkv_w, qkv, e, linv, ctx = front_call(
        dims, after(meta, [inner, outer]), x_pieces, lows, highs
    )
    inners = both_cores(inner, inner_got, [ctx, *cot_pieces[1:]])
    outers = both_cores(outer, outer_got, [ctx, *cot_pieces[1:]])
    los, (first, dctx, nl, act, og, inner_low, ag, sums) = rows_call(
        dims, FF, meta, x_all, ctx.reshape(C, R, D), cot_pieces, lows + highs + inners + outers,
    )

    def core_sum(keep, send):
        return added(keep, lax.ppermute(send, "fsdp", xor_pairs(F, 1)))

    def chip_sum(total, axis, dim):
        got = total
        while total.shape[dim] > 1:
            h = total.shape[dim] // 2
            stay, go = jnp.split(total, 2, axis=dim)
            got = swapped(go, axis, 2 * h if axis == "fsdp" else h)
            total = added(stay, got)
        return total, got

    def y_sum(total):
        return chip_sum(total, "fsdp", 0)

    def x_sum(total):
        return chip_sum(total, "tp", 1)

    def ctx_scatter(totals):
        part = totals[0].shape[1] // C
        sums_in = []
        for k in range(C):
            blocks = [lax.dynamic_slice_in_dim(a, (c ^ k) * part, part, 1) for a in totals]
            block = jnp.concatenate(blocks, axis=0) if len(blocks) > 1 else blocks[0]
            sums_in.append(ctx_moved(block, k).astype(F32))
        while len(sums_in) > 1:
            sums_in = [a + b for a, b in zip(sums_in[::2], sums_in[1::2])]
        return sums_in[0].astype(BF)

    def ctx_gather(mine, likes):
        rows, part = likes[0].shape[0], mine.shape[1]
        outs = list(likes)
        for k in range(C):
            got = ctx_moved(mine, k)
            for i in range(len(likes)):
                outs[i] = lax.dynamic_update_slice_in_dim(
                    outs[i], got[i * rows : (i + 1) * rows], (c ^ k) * part, 1
                )
        return [out.astype(F32) for out in outs]

    outer_parts = weight_call(dims, meta, [(og, act)], sums)
    inner_parts = weight_call(dims, meta, [(after(nl, outer_parts), inner_low)])
    los = [ctx_moved(piece, k) for k, piece in enumerate(los)]
    keep, send = outer_parts
    outer_core = core_sum(keep, after(send, los[1:2]))
    keep, send = inner_parts
    inner_parts = keep, after(send, los[3:4])
    dctx = after(dctx, [outer_core, *inner_parts])
    dqkv = back_call(dims, qkv, ctx, dctx.reshape(ctx.shape), e, linv)
    inner_core = core_sum(*inner_parts)
    outer_y, outer_raw = y_sum(outer_core)
    even = range(2, C, 2)
    early = [0] + list(range(1, C, 2))
    early_lo = tp_moved([los[k] for k in early])
    first = after(first, [inner_core, outer_y, *los[1:], *early_lo[1:]])
    ins = input_call(dqkv.reshape(C, R, 3 * D), qkv_w, first)
    late_lo = tp_moved([after(los[k], [dqkv]) for k in even])
    outer_x, outer_raw = x_sum(outer_y)
    inner_y, inner_raw = y_sum(inner_core)
    ag = after(ag, ins)
    keep, send = weight_call(dims, meta, [(x_all, dqkv), (ag, ctx)])
    ig = [ctx_moved(piece, k) if k % 2 else piece for k, piece in enumerate(ins)]
    send = after(send, [outer_raw, inner_raw] + ig[1::2] + late_lo[1:])
    qkv_core = core_sum(keep, send)
    for k in even:
        ig[k] = ctx_moved(after(ins[k], ig[1::2]), k)
    outer_x = after(outer_x[0, 0], [qkv_core])
    early_ig = tp_moved(after(tuple(ig[k] for k in early), [qkv_core]))
    qkv_y, _ = y_sum(qkv_core)
    inner_x, _ = x_sum(after(inner_y, [qkv_core]))
    inner_x = inner_x[0, 0]
    two_parts = ctx_scatter([outer_x, inner_x])
    outer_g, inner_g = ctx_gather(after(two_parts, [qkv_y] + [ig[k] for k in even]), [outer_x, inner_x])
    qkv_x, _ = x_sum(qkv_y)
    qkv_x = after(qkv_x[0, 0], [two_parts])
    qkv_part = ctx_scatter([qkv_x])
    late_ig = tp_moved([after(ig[k], [qkv_x]) for k in even])
    early_lo, late_lo = (after(tuple(part), [qkv_core]) for part in (early_lo, late_lo))
    early_ig = after(tuple(early_ig), [qkv_x])
    layer_out = to_slots([(early, early_lo), (list(even), late_lo)], BF)
    input_grad = to_slots([(early, early_ig), (list(even), late_ig)], F32)
    (qkv_g,) = ctx_gather(qkv_part, [qkv_x])

    def own(row, shape):
        whole = row.reshape(shape[0], shape[1] * F)
        return lax.dynamic_slice_in_dim(whole, f * shape[1], shape[1], 1)

    vec_sums = lax.dynamic_slice_in_dim(outer_g[Dl : Dl + 6, :D], f * Dl, Dl, 1)

    return (
        layer_out,
        input_grad,
        qkv_g[:Dl, :half],
        own(qkv_g[Dl, :half], query_bias.shape),
        qkv_g[:Dl, half : 2 * half],
        qkv_g[:Dl, 2 * half : 3 * half],
        own(qkv_g[Dl, 2 * half : 3 * half], value_bias.shape),
        qkv_g[:Dl, 3 * half :].T,
        vec_sums[0],
        vec_sums[1],
        vec_sums[2],
        inner_g[:Dl],
        own(inner_g[Dl], inner_bias.shape),
        outer_g[:Dl].T,
        vec_sums[3],
        vec_sums[4],
        vec_sums[5],
    )


def solution(mesh):
    rows3, flat = P("fsdp", "ctx", None), P("fsdp")
    wide, tall = P("fsdp", "tp"), P("tp", "fsdp")
    params = (wide, tall, wide, wide, tall, tall, flat, flat, flat, wide, tall, tall, flat, flat, flat)
    return jax.shard_map(
        per_device,
        mesh=mesh,
        in_specs=(rows3, P("fsdp")) + params + (rows3,),
        out_specs=(rows3, rows3) + params,
        check_vma=False,
    )
```

```python
import functools
import math

import jax
import jax.numpy as jnp
from jax import lax
from jax.experimental import pallas as pl
from jax.experimental.pallas import tpu as pltpu
from jax.sharding import PartitionSpec as P

HD = 64
BF = jnp.bfloat16
F32 = jnp.float32
ANY = pl.BlockSpec(memory_space=pl.ANY)
SMEM = pl.BlockSpec(memory_space=pltpu.SMEM)
EXTRA = 16
VMEM_LIMIT = 60 * 1024 * 1024


def dot_nn(a, b):
    return lax.dot_general(a, b, (((1,), (0,)), ((), ())), preferred_element_type=F32)


def dot_nt(a, b):
    return lax.dot_general(a, b, (((1,), (1,)), ((), ())), preferred_element_type=F32)


def dot_tn(a, b):
    return lax.dot_general(a, b, (((0,), (0,)), ((), ())), preferred_element_type=F32)


def const_spec(shape):
    zeros = (0,) * len(shape)
    return pl.BlockSpec(shape, lambda *_: zeros)


def cost(flops, moved, exps=0):
    return pl.CostEstimate(flops=int(flops), bytes_accessed=int(moved), transcendentals=int(exps))


def head_columns(pair, half_cols):
    per = half_cols // 128
    return pl.multiple_of(pair // per * (3 * half_cols) + pair % per * 128, 128)


def order_of(F, T, across):
    chip = [("fsdp", 1 << b) for b in range(1, F.bit_length() - 1)]
    pair = [("tp", 1 << b) for b in range(T.bit_length() - 1)]
    return chip + pair if across else pair + chip


def stacks(F, T, across):
    held, out = [(0, 0)], []
    steps = order_of(F, T, across)
    for n, (axis, bit) in enumerate(steps):
        got = [(df ^ bit, dt) if axis == "fsdp" else (df, dt ^ bit) for df, dt in held]
        if n == len(steps) - 1:
            out += [held, got]
        held = held + got
    return out + [[(df ^ 1, dt) for df, dt in part] for part in out]


def pieces_of(refs, F, T, across):
    return {
        at: ref.at[i] for ref, part in zip(refs, stacks(F, T, across)) for i, at in enumerate(part)
    }


def front_kernel(dims, meta, *refs):
    F, C, T, ns, span, D = dims
    n_w = F * T
    n_a = len(stacks(F, T, False))
    xs, low_refs, high_refs = refs[:C], refs[C : C + n_a], refs[C + n_a : C + 2 * n_a]
    x_out, w_out, qkv, e_out, linv_out, ctx, small, bias, sems = refs[C + 2 * n_a :]
    step = pl.program_id(0)
    NP = D // 128
    L = C * span
    Dl, half = D // F, D // T
    f = meta[0]
    c = meta[1]

    @pl.when(step == 0)
    def _():
        copies = [pltpu.make_async_copy(xs[k], x_out.at[k], sems.at[k]) for k in range(C)]
        qk = pieces_of(low_refs, F, T, False)
        vo = pieces_of(high_refs, F, T, True)
        for df in range(F):
            for dt in range(T):
                n = df * T + dt
                rows = pl.ds(pl.multiple_of((f ^ df) * Dl, 16), Dl)
                start = dt * 3 * half
                copies += [
                    pltpu.make_async_copy(
                        qk[df, dt].at[pl.ds(0, Dl)], w_out.at[rows, pl.ds(start, 2 * half)],
                        sems.at[C + n]),
                    pltpu.make_async_copy(
                        vo[df, dt].at[pl.ds(0, Dl), pl.ds(0, half)],
                        w_out.at[rows, pl.ds(start + 2 * half, half)], sems.at[C + n_w + n]),
                    pltpu.make_async_copy(
                        qk[df, dt].at[pl.ds(Dl, EXTRA), pl.ds(0, half)], small.at[n],
                        sems.at[C + 2 * n_w + n]),
                ]
        for copy in copies:
            copy.start()
        for copy in copies:
            copy.wait()
        bias[...] = jnp.zeros_like(bias)
        for dt in range(T):
            part = sum(small[df * T + dt, :2, :].astype(F32) for df in range(F))
            bias[:, dt * 3 * half : dt * 3 * half + half] = part[0:1]
            bias[:, (dt * 3 + 2) * half : (dt * 3 + 3) * half] = part[1:2]

        def project(j, carry):
            cols = pl.ds(pl.multiple_of(j * 384, 128), 384)
            y = dot_nn(x_out[...].reshape(L * ns, D), w_out[:, cols]) + bias[:, cols]
            qkv[:, :, :, cols] = y.astype(BF).reshape(C, ns, span, 384)
            return carry

        lax.fori_loop(0, 3 * D // 384, project, 0)

    s = step // NP
    pair = step % NP
    q_col = head_columns(pair, half)
    q = qkv[:, s, :, pl.ds(q_col, 128)].reshape(L, 128)
    k = qkv[:, s, :, pl.ds(pl.multiple_of(q_col + half, 128), 128)].reshape(L, 128)
    v = qkv[:, s, :, pl.ds(pl.multiple_of(q_col + 2 * half, 128), 128)].reshape(L, 128)
    low = lax.broadcasted_iota(jnp.int32, (L, 128), 1) < HD
    zero = jnp.zeros((), BF)
    one = jnp.ones((L, 128), BF)
    lane = lax.broadcasted_iota(jnp.int32, (1, L), 1)
    pos = ((lane // span) ^ c) * span + lane % span
    mask = jnp.where(pos < meta[2 + s], 0.0, -1e30)
    values = []
    for h in range(2):
        mine = low if h == 0 else jnp.logical_not(low)
        scores = dot_nt(q, jnp.where(mine, k, zero)) * (math.log2(math.e) / math.sqrt(HD)) + mask
        top = jnp.max(scores, axis=-1, keepdims=True)
        e_out[0, h * L : (h + 1) * L, :] = jnp.exp2(scores - top).astype(BF)
        values.append(
            jnp.concatenate([jnp.where(mine, v, zero), jnp.where(mine, one, zero)], axis=1)
        )
    acc = dot_nn(e_out[0, :L, :], values[0]) + dot_nn(e_out[0, L:, :], values[1])
    linv = 1.0 / acc[:, 128:]
    linv_out[0] = linv
    ctx[:, s, :, pl.ds(pl.multiple_of(pair * 128, 128), 128)] = (
        (acc[:, :128] * linv).astype(BF).reshape(C, span, 128)
    )


def front_call(dims, meta, xs, lows, highs):
    F, C, T, ns, span, D = dims
    NP, L = D // 128, C * span
    rows = ns * span
    shapes = [
        jax.ShapeDtypeStruct((C, rows, D), BF),
        jax.ShapeDtypeStruct((D, 3 * D), BF),
        jax.ShapeDtypeStruct((C, ns, span, 3 * D), BF),
        jax.ShapeDtypeStruct((ns * NP, 2 * L, L), BF),
        jax.ShapeDtypeStruct((ns * NP, L, 128), F32),
        jax.ShapeDtypeStruct((C, ns, span, D), BF),
    ]
    return pl.pallas_call(
        functools.partial(front_kernel, dims),
        name="front",
        grid=(ns * NP,),
        out_shape=shapes,
        in_specs=[SMEM] + [ANY] * (C + len(lows) + len(highs)),
        out_specs=[
            const_spec(shapes[0].shape),
            const_spec(shapes[1].shape),
            const_spec(shapes[2].shape),
            pl.BlockSpec((1, 2 * L, L), lambda i: (i, 0, 0)),
            pl.BlockSpec((1, L, 128), lambda i: (i, 0, 0)),
            const_spec(shapes[5].shape),
        ],
        scratch_shapes=[
            pltpu.VMEM((F * T, EXTRA, D // T), BF),
            pltpu.VMEM((1, 3 * D), F32),
            pltpu.SemaphoreType.DMA((C + 3 * F * T,)),
        ],
        compiler_params=pltpu.CompilerParams(vmem_limit_bytes=VMEM_LIMIT),
        cost_estimate=cost(2 * L * ns * D * 3 * D, 40e6, ns * 12 * L * L),
    )(meta, *xs, *lows, *highs)


def normalised(values):
    centre = values - jnp.mean(values, axis=-1, keepdims=True)
    spread = jnp.mean(centre * centre, axis=-1, keepdims=True)
    rstd = lax.rsqrt(spread + 1e-12)
    return centre * rstd, rstd


def norm_back(grad, gain, xhat, rstd):
    scaled = grad * gain
    first = jnp.mean(scaled, axis=-1, keepdims=True)
    second = jnp.mean(scaled * xhat, axis=-1, keepdims=True)
    return rstd * (scaled - first - xhat * second)


def rows_kernel(dims, FF, meta, x_ref, ctx_ref, *refs):
    F, C, T, ns, span, D = dims
    n_w = F * T
    n_a = len(stacks(F, T, False))
    cots = refs[:C]
    qk, vo, inner, outer = (
        pieces_of(refs[C + i * n_a : C + (i + 1) * n_a], F, T, i % 2 == 1) for i in range(4)
    )
    refs = refs[C + 4 * n_a :]
    los = refs[:C]
    (
        first_out, dctx_out, nl_out, act_out, og_out, ig_out, ag_out, sums,
        cot_s, lo_s, wi, wo, wout, gp_s, small, vec, inner_bias, sems, out_sems,
    ) = refs[C:]
    k = pl.program_id(0)
    R = ns * span
    Dl, half, fhalf = D // F, D // T, FF // T
    f = meta[0]
    c = meta[1]

    def weight_copies():
        copies = []
        for df in range(F):
            row = pl.multiple_of((f ^ df) * Dl, 16)
            for dt in range(T):
                n = df * T + dt
                rows = pl.ds(row, Dl)
                copies.append((
                    functools.partial(
                        pltpu.make_async_copy,
                        vo[df, dt].at[pl.ds(0, Dl), pl.ds(half, half)],
                        wo.at[rows, pl.ds(dt * half, half)], sems.at[n]),
                    functools.partial(
                        pltpu.make_async_copy,
                        inner[df, dt],
                        wi.at[rows, pl.ds(dt * fhalf, fhalf)], sems.at[n_w + n]),
                    functools.partial(
                        pltpu.make_async_copy,
                        outer[df, dt],
                        wout.at[rows, pl.ds(dt * fhalf, fhalf)], sems.at[2 * n_w + n]),
                ) + tuple(
                    functools.partial(
                        pltpu.make_async_copy,
                        (qk if part == 0 else vo)[df, dt].at[pl.ds(Dl, EXTRA)],
                        small.at[n, :, pl.ds(part * D, D)], sems.at[(3 + part) * n_w + n])
                    for part in range(2)
                ))
        return copies

    def cot_copies():
        return [
            pltpu.make_async_copy(cots[i], cot_s.at[i], sems.at[5 * n_w + i]) for i in range(C)
        ]

    @pl.when(k == 0)
    def _():
        copies = weight_copies()
        for which in (3, 4, 0, 1, 2):
            for group in copies:
                group[which]().start()
        for copy in cot_copies():
            copy.start()
        sums[...] = jnp.zeros_like(sums)
        for which in (3, 4, 0):
            for group in copies:
                group[which]().wait()
        for dt in range(T):
            part = sum(small[df * T + dt, :EXTRA, :].astype(F32) for df in range(F))
            inner_bias[:, dt * fhalf : (dt + 1) * fhalf] = part[2:3]
            if dt == 0:
                vec[...] = part[3:9, :D]

    def add_sum(row, value):
        sums[row : row + 1, :] += jnp.sum(value, axis=0, keepdims=True)

    out_bias, gain1, shift1 = vec[0:1, :], vec[1:2, :], vec[2:3, :]
    outer_bias, gain2, shift2 = vec[3:4, :], vec[4:5, :], vec[5:6, :]
    ctx_low = ctx_ref[0]
    before = x_ref[0].astype(F32) + dot_nt(ctx_low, wo[...]) + out_bias
    xhat1, rstd1 = normalised(before)
    normed = xhat1 * gain1 + shift1
    nl = normed.astype(BF)
    nl_out[0] = nl
    root = math.sqrt(2.0 / math.pi)
    chunk = 768

    @pl.when(k == 0)
    def _():
        for group in weight_copies():
            group[1]().wait()

    for j in range(FF // chunk):
        cols = slice(j * chunk, (j + 1) * chunk)
        pre = dot_nn(nl, wi[:, cols]) + inner_bias[:, cols]
        square = pre * pre
        th = jnp.tanh(pre * (root + (root * 0.044715) * square))
        hp = 0.5 + 0.5 * th
        act_out[0, :, cols] = (pre * hp).astype(BF)
        gp_s[:, cols] = hp + (0.5 * pre) * (1.0 - th * th) * (
            root + (3.0 * root * 0.044715) * square
        )

    @pl.when(k == 0)
    def _():
        for group in weight_copies():
            group[2]().wait()
        for copy in cot_copies():
            copy.wait()

    before2 = normed + dot_nt(act_out[0], wout[...]) + outer_bias
    xhat2, rstd2 = normalised(before2)
    row = lax.broadcasted_iota(jnp.int32, (R, 1), 0)
    position = (c ^ k) * span + row % span
    length = jnp.full((R, 1), meta[2], jnp.int32)
    for s in range(1, ns):
        length = jnp.where(row >= s * span, meta[2 + s], length)
    live = (position < length).astype(F32)
    lo_s[k] = (live * (xhat2 * gain2 + shift2)).astype(BF)
    for i in range(C):
        @pl.when(k == i)
        def _():
            pltpu.make_async_copy(lo_s.at[i], los[i], out_sems.at[i]).start()
    grad = cot_s[k].astype(F32) * live
    add_sum(4, grad * xhat2)
    add_sum(5, grad)
    second = norm_back(grad, gain2, xhat2, rstd2)
    og = second.astype(BF)
    og_out[0] = og
    add_sum(3, og.astype(F32))
    for j in range(FF // chunk):
        cols = slice(j * chunk, (j + 1) * chunk)
        ig = (dot_nn(og, wout[:, cols]) * gp_s[:, cols]).astype(BF)
        ig_out[0, :, cols] = ig
    ngrad = dot_nt(ig_out[0], wi[...]) + second
    add_sum(1, ngrad * xhat1)
    add_sum(2, ngrad)
    first = norm_back(ngrad, gain1, xhat1, rstd1)
    first_out[0] = first
    ag = first.astype(BF)
    ag_out[0] = ag
    add_sum(0, ag.astype(F32))
    dctx_out[0] = dot_nn(ag, wo[...]).astype(BF)

    @pl.when(k == C - 1)
    def _():
        for i in range(C):
            pltpu.make_async_copy(lo_s.at[i], los[i], out_sems.at[i]).wait()


def rows_call(dims, FF, meta, x_all, ctx, cots, weights):
    F, C, T, ns, span, D = dims
    R = ns * span
    tile = lambda n: pl.BlockSpec((1, R, n), lambda i: (i, 0, 0))
    widths = [(D, F32), (D, BF), (D, BF), (FF, BF), (D, BF), (FF, BF), (D, BF)]
    out_shape = (
        [jax.ShapeDtypeStruct((R, D), BF)] * C
        + [jax.ShapeDtypeStruct((C, R, n), kind) for n, kind in widths]
        + [jax.ShapeDtypeStruct((EXTRA, D), F32)]
    )
    n_w = F * T
    outs = pl.pallas_call(
        functools.partial(rows_kernel, dims, FF),
        name="rows",
        grid=(C,),
        out_shape=out_shape,
        in_specs=[SMEM, tile(D), tile(D)]
        + [ANY] * (C + len(weights)),
        out_specs=[ANY] * C
        + [tile(n) for n, _ in widths]
        + [const_spec((EXTRA, D))],
        scratch_shapes=[
            pltpu.VMEM((C, R, D), BF),
            pltpu.VMEM((C, R, D), BF),
            pltpu.VMEM((D, FF), BF),
            pltpu.VMEM((D, D), BF),
            pltpu.VMEM((D, FF), BF),
            pltpu.VMEM((R, FF), F32),
            pltpu.VMEM((n_w, EXTRA, FF // T), BF),
            pltpu.VMEM((6, D), F32),
            pltpu.VMEM((1, FF), F32),
            pltpu.SemaphoreType.DMA((5 * n_w + C,)),
            pltpu.SemaphoreType.DMA((C,)),
        ],
        compiler_params=pltpu.CompilerParams(vmem_limit_bytes=VMEM_LIMIT),
        cost_estimate=cost(4 * C * R * D * (2 * FF + D), 50e6, C * R * FF),
    )(meta, x_all, ctx, *cots, *weights)
    return outs[:C], outs[C:]


def back_kernel(dims, qkv, ctx, dctx, e_ref, linv, out, ds_s):
    F, C, T, ns, span, D = dims
    step = pl.program_id(0)
    NP, L, half = D // 128, C * span, D // T
    s = step // NP
    pair = step % NP
    q_col = head_columns(pair, half)
    k_col = pl.multiple_of(q_col + half, 128)
    v_col = pl.multiple_of(q_col + 2 * half, 128)
    c_col = pl.multiple_of(pair * 128, 128)
    q = qkv[:, s, :, pl.ds(q_col, 128)].reshape(L, 128)
    k = qkv[:, s, :, pl.ds(k_col, 128)].reshape(L, 128)
    v = qkv[:, s, :, pl.ds(v_col, 128)].reshape(L, 128)
    grad = dctx[:, s, :, pl.ds(c_col, 128)].reshape(L, 128).astype(F32) * linv[0]
    grad_low = grad.astype(BF)
    product = grad_low.astype(F32) * ctx[:, s, :, pl.ds(c_col, 128)].reshape(L, 128).astype(F32)
    low = lax.broadcasted_iota(jnp.int32, (L, 128), 1) < HD
    zero = jnp.zeros((), BF)
    qs, ks, gs = [], [], []
    for h in range(2):
        mine = low if h == 0 else jnp.logical_not(low)
        row_dot = jnp.sum(jnp.where(mine, product, 0.0), axis=-1, keepdims=True)
        probs_grad = dot_nt(grad_low, jnp.where(mine, v, zero))
        e = e_ref[0, h * L : (h + 1) * L, :].astype(F32)
        ds_s[h * L : (h + 1) * L, :] = (e * (probs_grad - row_dot)).astype(BF)
        qs.append(jnp.where(mine, q, zero))
        ks.append(jnp.where(mine, k, zero))
        gs.append(jnp.where(mine, grad_low, zero))
    scale = 1.0 / math.sqrt(HD)
    dq = (dot_nn(ds_s[:L, :], ks[0]) + dot_nn(ds_s[L:, :], ks[1])) * scale
    dk = dot_tn(ds_s[...], jnp.concatenate(qs, axis=0)) * scale
    dv = dot_tn(e_ref[0], jnp.concatenate(gs, axis=0))
    out[:, s, :, pl.ds(q_col, 128)] = dq.astype(BF).reshape(C, span, 128)
    out[:, s, :, pl.ds(k_col, 128)] = dk.astype(BF).reshape(C, span, 128)
    out[:, s, :, pl.ds(v_col, 128)] = dv.astype(BF).reshape(C, span, 128)


def back_call(dims, qkv, ctx, dctx, e, linv):
    F, C, T, ns, span, D = dims
    NP, L = D // 128, C * span
    return pl.pallas_call(
        functools.partial(back_kernel, dims),
        name="back",
        grid=(ns * NP,),
        out_shape=jax.ShapeDtypeStruct(qkv.shape, BF),
        in_specs=[
            const_spec(qkv.shape),
            const_spec(ctx.shape),
            const_spec(dctx.shape),
            pl.BlockSpec((1, 2 * L, L), lambda i: (i, 0, 0)),
            pl.BlockSpec((1, L, 128), lambda i: (i, 0, 0)),
        ],
        out_specs=const_spec(qkv.shape),
        scratch_shapes=[pltpu.VMEM((2 * L, L), BF)],
        compiler_params=pltpu.CompilerParams(vmem_limit_bytes=VMEM_LIMIT),
        cost_estimate=cost(ns * NP * 16 * L * L * 128, 30e6, 0),
    )(qkv, ctx, dctx, e, linv)


def input_kernel(C, dqkv, w, first, *refs):
    outs, (buf, sems) = refs[:C], refs[C:]
    k = pl.program_id(0)
    buf[k] = (dot_nt(dqkv[0], w[...]) + first[0]).astype(BF)
    for i in range(C):
        @pl.when(k == i)
        def _():
            pltpu.make_async_copy(buf.at[i], outs[i], sems.at[i]).start()

    @pl.when(k == C - 1)
    def _():
        for i in range(C):
            pltpu.make_async_copy(buf.at[i], outs[i], sems.at[i]).wait()


def input_call(dqkv, w, first):
    C, R, W = dqkv.shape
    D = w.shape[0]
    return pl.pallas_call(
        functools.partial(input_kernel, C),
        name="input_grad",
        grid=(C,),
        out_shape=[jax.ShapeDtypeStruct((R, D), BF)] * C,
        in_specs=[
            pl.BlockSpec((1, R, W), lambda i: (i, 0, 0)),
            const_spec(w.shape),
            pl.BlockSpec((1, R, D), lambda i: (i, 0, 0)),
        ],
        out_specs=[ANY] * C,
        scratch_shapes=[pltpu.VMEM((C, R, D), BF), pltpu.SemaphoreType.DMA((C,))],
        compiler_params=pltpu.CompilerParams(vmem_limit_bytes=VMEM_LIMIT),
        cost_estimate=cost(2 * C * R * D * W, 15e6, 0),
    )(dqkv, w, first)


COLS = 384


def weight_kernel(F, pers, with_sums, meta, *refs):
    n = len(pers)
    lefts, rights = refs[:n], refs[n : 2 * n]
    refs = refs[2 * n :]
    sums, refs = (refs[0], refs[1:]) if with_sums else (None, refs)
    keep, send, tile = refs[:3]
    turned = refs[3:]
    D = lefts[0].shape[1]
    Dl = D // F
    b = pl.program_id(1)

    @pl.when((pl.program_id(0) == 0) & (b == 0))
    def _():
        for left, left_t in zip(lefts, turned):
            left_t[:D, :] = left[...].T
            left_t[D:, :] = jnp.ones((EXTRA, left.shape[0]), BF)

    start = 0
    for right, left_t, per in zip(rights, turned, pers):
        @pl.when((b >= start) & (b < start + per))
        def _():
            tile[...] = dot_nn(left_t[...], right[...]).astype(BF)
        start += per
    if with_sums:
        for j in range(D // COLS):
            @pl.when(b == j)
            def _():
                tile[D:, :] = sums[:, j * COLS : (j + 1) * COLS].astype(BF)
    f = meta[0]
    for high in range(F // 2):
        for bit, out in ((0, keep), (1, send)):
            row = pl.multiple_of((f ^ (2 * high + bit)) * Dl, 16)
            out[high, 0, :Dl] = tile[pl.ds(row, Dl), :]
            out[high, 0, Dl:] = tile[D:, :]


def weight_call(dims, meta, pairs, sums=None):
    F, C, T, ns, span, D = dims
    rows = C * ns * span
    pairs = [(left.reshape(rows, -1), right.reshape(rows, -1)) for left, right in pairs]
    pers = [right.shape[1] // T // COLS for _, right in pairs]
    width = sum(pers) * COLS
    out = jax.ShapeDtypeStruct((F // 2, T, D // F + EXTRA, width), BF)
    out_spec = pl.BlockSpec((F // 2, 1, D // F + EXTRA, COLS), lambda a, b: (0, a, 0, b))
    right_specs, start = [], 0
    for per in pers:
        right_specs.append(
            pl.BlockSpec(
                (rows, COLS),
                lambda a, b, per=per, start=start: (0, a * per + jnp.clip(b - start, 0, per - 1)),
            )
        )
        start += per
    return pl.pallas_call(
        functools.partial(weight_kernel, F, pers, sums is not None),
        name="weight_grad",
        grid=(T, sum(pers)),
        out_shape=[out, out],
        in_specs=[SMEM]
        + [const_spec(left.shape) for left, _ in pairs]
        + right_specs
        + ([] if sums is None else [const_spec(sums.shape)]),
        out_specs=[out_spec, out_spec],
        scratch_shapes=[pltpu.VMEM((D + EXTRA, COLS), BF)]
        + [pltpu.VMEM((D + EXTRA, rows), BF) for _ in pairs],
        compiler_params=pltpu.CompilerParams(vmem_limit_bytes=VMEM_LIMIT),
        cost_estimate=cost(
            2 * rows * D * width * T, 2 * (rows * (D + width * T) + D * width * T), 0
        ),
    )(
        meta,
        *[left for left, _ in pairs],
        *[right for _, right in pairs],
        *([] if sums is None else [sums]),
    )


def xor_pairs(count, mask):
    return [(i, i ^ mask) for i in range(count)]


def after(value, others):
    return lax.optimization_barrier((value, *others))[0]


def added(a, b):
    return (a.astype(F32) + b.astype(F32)).astype(BF)


def per_device(
    tokens_in, seq_lengths, query_weight, query_bias, key_weight, value_weight, value_bias,
    output_weight, output_bias, attn_gain, attn_shift, inner_weight, inner_bias, outer_weight,
    outer_bias, ffn_gain, ffn_shift, cotangent,
):
    F, C, T = (lax.axis_size(a) for a in ("fsdp", "ctx", "tp"))
    f, c, t = (lax.axis_index(a) for a in ("fsdp", "ctx", "tp"))
    S, span, D = tokens_in.shape
    ns = S // (C * T)
    Dl, half = D // F, D // T
    fhalf = inner_weight.shape[1]
    FF = fhalf * T
    R = ns * span
    dims = (F, C, T, ns, span, D)

    def sequence_pieces(array):
        return [
            lax.dynamic_slice_in_dim(array, ((c ^ k) * T + t) * ns, ns, 0).reshape(R, D)
            for k in range(C)
        ]

    def ctx_moved(piece, k):
        return lax.ppermute(piece, "ctx", xor_pairs(C, k)) if k else piece

    def tp_moved(pieces):
        both = jnp.concatenate(pieces, axis=0) if len(pieces) > 1 else pieces[0]
        return [both] + [lax.ppermute(both, "tp", xor_pairs(T, dt)) for dt in range(1, T)]

    def to_slots(groups, kind):
        out = lax.full((S, span, D), 0, kind)
        pieces = {}
        for ks, group in groups:
            for dt, merged in enumerate(group):
                for i, k in enumerate(ks):
                    pieces[k, dt] = merged[i * R : (i + 1) * R]
        for k in range(C):
            for dt in range(T):
                got = pieces[k, dt]
                out = lax.dynamic_update_slice_in_dim(
                    out, got.reshape(ns, span, D).astype(kind), ((c ^ k) * T + (t ^ dt)) * ns, 0
                )
        return out

    def swapped(array, axis, bit):
        return lax.ppermute(array, axis, xor_pairs(lax.axis_size(axis), bit))

    def chip_start(shard, across):
        held = shard[None]
        for axis, bit in order_of(F, T, across)[:-1]:
            held = jnp.concatenate([held, swapped(held, axis, bit)], axis=0)
        return held

    def chip_end(held, across):
        axis, bit = order_of(F, T, across)[-1]
        return swapped(held, axis, bit)

    def both_cores(held, got, others=()):
        near = swapped(after(held, others), "fsdp", 1)
        return [held, got, near, swapped(got, "fsdp", 1)]

    def spread(array, width):
        rows, part = array.shape
        owner = lax.broadcasted_iota(jnp.int32, (rows, part * F), 1) // part
        return jnp.where(owner == f, jnp.tile(array, (1, F)), jnp.zeros((), BF)).reshape(-1, width)

    x_pieces = sequence_pieces(tokens_in)
    near_x = ctx_moved(x_pieces[1], 1)
    before = [near_x]
    x_pieces[1] = near_x
    for k in [*range(3, C, 2), *range(2, C, 2)]:
        x_pieces[k] = ctx_moved(after(x_pieces[k], before), k)
        before = [x_pieces[k]]
    vectors = [output_bias, attn_gain, attn_shift, outer_bias, ffn_gain, ffn_shift]
    vectors = jnp.concatenate(vectors).reshape(len(vectors), Dl)
    small = [
        spread(query_bias, half), spread(value_bias, half), spread(inner_bias, fhalf),
        spread(vectors, D),
    ]
    small = jnp.concatenate([jnp.pad(a, ((0, 0), (0, fhalf - a.shape[1]))) for a in small])
    small = jnp.pad(small, ((0, EXTRA - small.shape[0]), (0, 0)))
    low = jnp.concatenate([query_weight, key_weight], axis=1)
    high = jnp.concatenate([value_weight, output_weight.T], axis=1)
    low = chip_start(jnp.concatenate([low, small[:, :D]], axis=0), False)
    high = chip_start(jnp.concatenate([high, small[:, D:]], axis=0), True)
    lows = both_cores(low, chip_end(after(low, [near_x]), False))
    highs = both_cores(high, chip_end(after(high, [near_x]), True))
    halfway = [lows[1], highs[1], *x_pieces[3::2]]
    inner = chip_start(after(inner_weight, halfway), False)
    outer = chip_start(after(outer_weight.T, halfway), True)
    inner_got = chip_end(after(inner, x_pieces[2::2]), False)
    outer_got = chip_end(after(outer, x_pieces[2::2]), True)
    cot_pieces = sequence_pieces(after(cotangent, [*x_pieces[1:], *lows, *highs]))
    cot_pieces = [ctx_moved(piece, k) for k, piece in enumerate(cot_pieces)]
    lengths = lax.dynamic_slice_in_dim(seq_lengths, (c * T + t) * ns, ns, 0)
    meta = jnp.concatenate([jnp.stack([f, c]).astype(jnp.int32), lengths])

    x_all, qkv_w, qkv, e, linv, ctx = front_call(
        dims, after(meta, [inner, outer]), x_pieces, lows, highs
    )
    inners = both_cores(inner, inner_got, [ctx, *cot_pieces[1:]])
    outers = both_cores(outer, outer_got, [ctx, *cot_pieces[1:]])
    los, (first, dctx, nl, act, og, inner_low, ag, sums) = rows_call(
        dims, FF, meta, x_all, ctx.reshape(C, R, D), cot_pieces, lows + highs + inners + outers,
    )

    def core_sum(keep, send):
        return added(keep, lax.ppermute(send, "fsdp", xor_pairs(F, 1)))

    def chip_sum(total, axis, dim):
        got = total
        while total.shape[dim] > 1:
            h = total.shape[dim] // 2
            stay, go = jnp.split(total, 2, axis=dim)
            got = swapped(go, axis, 2 * h if axis == "fsdp" else h)
            total = added(stay, got)
        return total, got

    def y_sum(total):
        return chip_sum(total, "fsdp", 0)

    def x_sum(total):
        return chip_sum(total, "tp", 1)

    def ctx_scatter(totals):
        part = totals[0].shape[1] // C
        sums_in = []
        for k in range(C):
            blocks = [lax.dynamic_slice_in_dim(a, (c ^ k) * part, part, 1) for a in totals]
            block = jnp.concatenate(blocks, axis=0) if len(blocks) > 1 else blocks[0]
            sums_in.append(ctx_moved(block, k).astype(F32))
        while len(sums_in) > 1:
            sums_in = [a + b for a, b in zip(sums_in[::2], sums_in[1::2])]
        return sums_in[0].astype(BF)

    def ctx_gather(mine, likes):
        rows, part = likes[0].shape[0], mine.shape[1]
        outs = list(likes)
        for k in range(C):
            got = ctx_moved(mine, k)
            for i in range(len(likes)):
                outs[i] = lax.dynamic_update_slice_in_dim(
                    outs[i], got[i * rows : (i + 1) * rows], (c ^ k) * part, 1
                )
        return [out.astype(F32) for out in outs]

    outer_parts = weight_call(dims, meta, [(og, act)], sums)
    inner_parts = weight_call(dims, meta, [(after(nl, outer_parts), inner_low)])
    los = [ctx_moved(piece, k) for k, piece in enumerate(los)]
    keep, send = outer_parts
    outer_core = core_sum(keep, after(send, los[1:2]))
    keep, send = inner_parts
    inner_parts = keep, after(send, los[3:4])
    dctx = after(dctx, [outer_core, *inner_parts])
    dqkv = back_call(dims, qkv, ctx, dctx.reshape(ctx.shape), e, linv)
    inner_core = core_sum(*inner_parts)
    outer_y, outer_raw = y_sum(outer_core)
    even = range(2, C, 2)
    early = [0] + list(range(1, C, 2))
    early_lo = tp_moved([los[k] for k in early])
    first = after(first, [inner_core, outer_y, *los[1:], *early_lo[1:]])
    ins = input_call(dqkv.reshape(C, R, 3 * D), qkv_w, first)
    late_lo = tp_moved([after(los[k], [dqkv]) for k in even])
    outer_x, outer_raw = x_sum(outer_y)
    inner_y, inner_raw = y_sum(inner_core)
    ag = after(ag, ins)
    keep, send = weight_call(dims, meta, [(x_all, dqkv), (ag, ctx)])
    ig = [ctx_moved(piece, k) if k % 2 else piece for k, piece in enumerate(ins)]
    send = after(send, [outer_raw, inner_raw] + ig[1::2] + late_lo[1:])
    qkv_core = core_sum(keep, send)
    for k in even:
        ig[k] = ctx_moved(after(ins[k], ig[1::2]), k)
    outer_x = after(outer_x[0, 0], [qkv_core])
    early_ig = tp_moved(after(tuple(ig[k] for k in early), [qkv_core]))
    qkv_y, _ = y_sum(qkv_core)
    inner_x, _ = x_sum(after(inner_y, [qkv_core]))
    inner_x = inner_x[0, 0]
    two_parts = ctx_scatter([outer_x, inner_x])
    outer_g, inner_g = ctx_gather(after(two_parts, [qkv_y] + [ig[k] for k in even]), [outer_x, inner_x])
    qkv_x, _ = x_sum(qkv_y)
    qkv_x = after(qkv_x[0, 0], [two_parts])
    qkv_part = ctx_scatter([qkv_x])
    late_ig = tp_moved([after(ig[k], [qkv_x]) for k in even])
    early_lo, late_lo = (after(tuple(part), [qkv_core]) for part in (early_lo, late_lo))
    early_ig = after(tuple(early_ig), [qkv_x])
    layer_out = to_slots([(early, early_lo), (list(even), late_lo)], BF)
    input_grad = to_slots([(early, early_ig), (list(even), late_ig)], F32)
    (qkv_g,) = ctx_gather(qkv_part, [qkv_x])

    def own(row, shape):
        whole = row.reshape(shape[0], shape[1] * F)
        return lax.dynamic_slice_in_dim(whole, f * shape[1], shape[1], 1)

    vec_sums = lax.dynamic_slice_in_dim(outer_g[Dl : Dl + 6, :D], f * Dl, Dl, 1)

    return (
        layer_out,
        input_grad,
        qkv_g[:Dl, :half],
        own(qkv_g[Dl, :half], query_bias.shape),
        qkv_g[:Dl, half : 2 * half],
        qkv_g[:Dl, 2 * half : 3 * half],
        own(qkv_g[Dl, 2 * half : 3 * half], value_bias.shape),
        qkv_g[:Dl, 3 * half :].T,
        vec_sums[0],
        vec_sums[1],
        vec_sums[2],
        inner_g[:Dl],
        own(inner_g[Dl], inner_bias.shape),
        outer_g[:Dl].T,
        vec_sums[3],
        vec_sums[4],
        vec_sums[5],
    )


def solution(mesh):
    rows3, flat = P("fsdp", "ctx", None), P("fsdp")
    wide, tall = P("fsdp", "tp"), P("tp", "fsdp")
    params = (wide, tall, wide, wide, tall, tall, flat, flat, flat, wide, tall, tall, flat, flat, flat)
    return jax.shard_map(
        per_device,
        mesh=mesh,
        in_specs=(rows3, P("fsdp")) + params + (rows3,),
        out_specs=(rows3, rows3) + params,
        check_vma=False,
    )
```

```python
import functools
import math

import jax
import jax.numpy as jnp
from jax import lax
from jax.experimental import pallas as pl
from jax.experimental.pallas import tpu as pltpu
from jax.sharding import PartitionSpec as P

HD = 64
BF = jnp.bfloat16
F32 = jnp.float32
ANY = pl.BlockSpec(memory_space=pl.ANY)
SMEM = pl.BlockSpec(memory_space=pltpu.SMEM)
EXTRA = 16
VMEM_LIMIT = 60 * 1024 * 1024


def dot_nn(a, b):
    return lax.dot_general(a, b, (((1,), (0,)), ((), ())), preferred_element_type=F32)


def dot_nt(a, b):
    return lax.dot_general(a, b, (((1,), (1,)), ((), ())), preferred_element_type=F32)


def dot_tn(a, b):
    return lax.dot_general(a, b, (((0,), (0,)), ((), ())), preferred_element_type=F32)


def const_spec(shape):
    zeros = (0,) * len(shape)
    return pl.BlockSpec(shape, lambda *_: zeros)


def cost(flops, moved, exps=0):
    return pl.CostEstimate(flops=int(flops), bytes_accessed=int(moved), transcendentals=int(exps))


def head_columns(pair, half_cols):
    per = half_cols // 128
    return pl.multiple_of(pair // per * (3 * half_cols) + pair % per * 128, 128)


def order_of(F, T, across):
    chip = [("fsdp", 1 << b) for b in range(1, F.bit_length() - 1)]
    pair = [("tp", 1 << b) for b in range(T.bit_length() - 1)]
    return chip + pair if across else pair + chip


def stacks(F, T, across):
    held, out = [(0, 0)], []
    steps = order_of(F, T, across)
    for n, (axis, bit) in enumerate(steps):
        got = [(df ^ bit, dt) if axis == "fsdp" else (df, dt ^ bit) for df, dt in held]
        if n == len(steps) - 1:
            out += [held, got]
        held = held + got
    return out + [[(df ^ 1, dt) for df, dt in part] for part in out]


def pieces_of(refs, F, T, across):
    return {
        at: ref.at[i] for ref, part in zip(refs, stacks(F, T, across)) for i, at in enumerate(part)
    }


def front_kernel(dims, meta, *refs):
    F, C, T, ns, span, D = dims
    n_w = F * T
    n_a = len(stacks(F, T, False))
    xs, low_refs, high_refs = refs[:C], refs[C : C + n_a], refs[C + n_a : C + 2 * n_a]
    x_out, w_out, qkv, e_out, linv_out, ctx, small, bias, sems = refs[C + 2 * n_a :]
    step = pl.program_id(0)
    NP = D // 128
    L = C * span
    Dl, half = D // F, D // T
    f = meta[0]
    c = meta[1]

    @pl.when(step == 0)
    def _():
        copies = [pltpu.make_async_copy(xs[k], x_out.at[k], sems.at[k]) for k in range(C)]
        qk = pieces_of(low_refs, F, T, False)
        vo = pieces_of(high_refs, F, T, True)
        for df in range(F):
            for dt in range(T):
                n = df * T + dt
                rows = pl.ds(pl.multiple_of((f ^ df) * Dl, 16), Dl)
                start = dt * 3 * half
                copies += [
                    pltpu.make_async_copy(
                        qk[df, dt].at[pl.ds(0, Dl)], w_out.at[rows, pl.ds(start, 2 * half)],
                        sems.at[C + n]),
                    pltpu.make_async_copy(
                        vo[df, dt].at[pl.ds(0, Dl), pl.ds(0, half)],
                        w_out.at[rows, pl.ds(start + 2 * half, half)], sems.at[C + n_w + n]),
                    pltpu.make_async_copy(
                        qk[df, dt].at[pl.ds(Dl, EXTRA), pl.ds(0, half)], small.at[n],
                        sems.at[C + 2 * n_w + n]),
                ]
        for copy in copies:
            copy.start()
        for copy in copies:
            copy.wait()
        bias[...] = jnp.zeros_like(bias)
        for dt in range(T):
            part = sum(small[df * T + dt, :2, :].astype(F32) for df in range(F))
            bias[:, dt * 3 * half : dt * 3 * half + half] = part[0:1]
            bias[:, (dt * 3 + 2) * half : (dt * 3 + 3) * half] = part[1:2]

        def project(j, carry):
            cols = pl.ds(pl.multiple_of(j * 384, 128), 384)
            y = dot_nn(x_out[...].reshape(L * ns, D), w_out[:, cols]) + bias[:, cols]
            qkv[:, :, :, cols] = y.astype(BF).reshape(C, ns, span, 384)
            return carry

        lax.fori_loop(0, 3 * D // 384, project, 0)

    s = step // NP
    pair = step % NP
    q_col = head_columns(pair, half)
    q = qkv[:, s, :, pl.ds(q_col, 128)].reshape(L, 128)
    k = qkv[:, s, :, pl.ds(pl.multiple_of(q_col + half, 128), 128)].reshape(L, 128)
    v = qkv[:, s, :, pl.ds(pl.multiple_of(q_col + 2 * half, 128), 128)].reshape(L, 128)
    low = lax.broadcasted_iota(jnp.int32, (L, 128), 1) < HD
    zero = jnp.zeros((), BF)
    one = jnp.ones((L, 128), BF)
    lane = lax.broadcasted_iota(jnp.int32, (1, L), 1)
    pos = ((lane // span) ^ c) * span + lane % span
    mask = jnp.where(pos < meta[2 + s], 0.0, -1e30)
    values = []
    for h in range(2):
        mine = low if h == 0 else jnp.logical_not(low)
        scores = dot_nt(q, jnp.where(mine, k, zero)) * (math.log2(math.e) / math.sqrt(HD)) + mask
        top = jnp.max(scores, axis=-1, keepdims=True)
        e_out[0, h * L : (h + 1) * L, :] = jnp.exp2(scores - top).astype(BF)
        values.append(
            jnp.concatenate([jnp.where(mine, v, zero), jnp.where(mine, one, zero)], axis=1)
        )
    acc = dot_nn(e_out[0, :L, :], values[0]) + dot_nn(e_out[0, L:, :], values[1])
    linv = 1.0 / acc[:, 128:]
    linv_out[0] = linv
    ctx[:, s, :, pl.ds(pl.multiple_of(pair * 128, 128), 128)] = (
        (acc[:, :128] * linv).astype(BF).reshape(C, span, 128)
    )


def front_call(dims, meta, xs, lows, highs):
    F, C, T, ns, span, D = dims
    NP, L = D // 128, C * span
    rows = ns * span
    shapes = [
        jax.ShapeDtypeStruct((C, rows, D), BF),
        jax.ShapeDtypeStruct((D, 3 * D), BF),
        jax.ShapeDtypeStruct((C, ns, span, 3 * D), BF),
        jax.ShapeDtypeStruct((ns * NP, 2 * L, L), BF),
        jax.ShapeDtypeStruct((ns * NP, L, 128), F32),
        jax.ShapeDtypeStruct((C, ns, span, D), BF),
    ]
    return pl.pallas_call(
        functools.partial(front_kernel, dims),
        name="front",
        grid=(ns * NP,),
        out_shape=shapes,
        in_specs=[SMEM] + [ANY] * (C + len(lows) + len(highs)),
        out_specs=[
            const_spec(shapes[0].shape),
            const_spec(shapes[1].shape),
            const_spec(shapes[2].shape),
            pl.BlockSpec((1, 2 * L, L), lambda i: (i, 0, 0)),
            pl.BlockSpec((1, L, 128), lambda i: (i, 0, 0)),
            const_spec(shapes[5].shape),
        ],
        scratch_shapes=[
            pltpu.VMEM((F * T, EXTRA, D // T), BF),
            pltpu.VMEM((1, 3 * D), F32),
            pltpu.SemaphoreType.DMA((C + 3 * F * T,)),
        ],
        compiler_params=pltpu.CompilerParams(vmem_limit_bytes=VMEM_LIMIT),
        cost_estimate=cost(2 * L * ns * D * 3 * D, 40e6, ns * 12 * L * L),
    )(meta, *xs, *lows, *highs)


def normalised(values):
    centre = values - jnp.mean(values, axis=-1, keepdims=True)
    spread = jnp.mean(centre * centre, axis=-1, keepdims=True)
    rstd = lax.rsqrt(spread + 1e-12)
    return centre * rstd, rstd


def norm_back(grad, gain, xhat, rstd):
    scaled = grad * gain
    first = jnp.mean(scaled, axis=-1, keepdims=True)
    second = jnp.mean(scaled * xhat, axis=-1, keepdims=True)
    return rstd * (scaled - first - xhat * second)


def rows_kernel(dims, FF, meta, x_ref, ctx_ref, *refs):
    F, C, T, ns, span, D = dims
    n_w = F * T
    n_a = len(stacks(F, T, False))
    cots = refs[:C]
    qk, vo, inner, outer = (
        pieces_of(refs[C + i * n_a : C + (i + 1) * n_a], F, T, i % 2 == 1) for i in range(4)
    )
    refs = refs[C + 4 * n_a :]
    los = refs[:C]
    (
        first_out, dctx_out, nl_out, act_out, og_out, ig_out, ag_out, sums,
        cot_s, lo_s, wi, wo, wout, gp_s, small, vec, inner_bias, sems, out_sems,
    ) = refs[C:]
    k = pl.program_id(0)
    R = ns * span
    Dl, half, fhalf = D // F, D // T, FF // T
    f = meta[0]
    c = meta[1]

    def weight_copies():
        copies = []
        for df in range(F):
            row = pl.multiple_of((f ^ df) * Dl, 16)
            for dt in range(T):
                n = df * T + dt
                rows = pl.ds(row, Dl)
                copies.append((
                    functools.partial(
                        pltpu.make_async_copy,
                        vo[df, dt].at[pl.ds(0, Dl), pl.ds(half, half)],
                        wo.at[rows, pl.ds(dt * half, half)], sems.at[n]),
                    functools.partial(
                        pltpu.make_async_copy,
                        inner[df, dt],
                        wi.at[rows, pl.ds(dt * fhalf, fhalf)], sems.at[n_w + n]),
                    functools.partial(
                        pltpu.make_async_copy,
                        outer[df, dt],
                        wout.at[rows, pl.ds(dt * fhalf, fhalf)], sems.at[2 * n_w + n]),
                ) + tuple(
                    functools.partial(
                        pltpu.make_async_copy,
                        (qk if part == 0 else vo)[df, dt].at[pl.ds(Dl, EXTRA)],
                        small.at[n, :, pl.ds(part * D, D)], sems.at[(3 + part) * n_w + n])
                    for part in range(2)
                ))
        return copies

    def cot_copies():
        return [
            pltpu.make_async_copy(cots[i], cot_s.at[i], sems.at[5 * n_w + i]) for i in range(C)
        ]

    @pl.when(k == 0)
    def _():
        copies = weight_copies()
        for which in (3, 4, 0, 1, 2):
            for group in copies:
                group[which]().start()
        for copy in cot_copies():
            copy.start()
        sums[...] = jnp.zeros_like(sums)
        for which in (3, 4, 0):
            for group in copies:
                group[which]().wait()
        for dt in range(T):
            part = sum(small[df * T + dt, :EXTRA, :].astype(F32) for df in range(F))
            inner_bias[:, dt * fhalf : (dt + 1) * fhalf] = part[2:3]
            if dt == 0:
                vec[...] = part[3:9, :D]

    def add_sum(row, value):
        sums[row : row + 1, :] += jnp.sum(value, axis=0, keepdims=True)

    out_bias, gain1, shift1 = vec[0:1, :], vec[1:2, :], vec[2:3, :]
    outer_bias, gain2, shift2 = vec[3:4, :], vec[4:5, :], vec[5:6, :]
    ctx_low = ctx_ref[0]
    before = x_ref[0].astype(F32) + dot_nt(ctx_low, wo[...]) + out_bias
    xhat1, rstd1 = normalised(before)
    normed = xhat1 * gain1 + shift1
    nl = normed.astype(BF)
    nl_out[0] = nl
    root = math.sqrt(2.0 / math.pi)
    chunk = 768

    @pl.when(k == 0)
    def _():
        for group in weight_copies():
            group[1]().wait()

    for j in range(FF // chunk):
        cols = slice(j * chunk, (j + 1) * chunk)
        pre = dot_nn(nl, wi[:, cols]) + inner_bias[:, cols]
        square = pre * pre
        th = jnp.tanh(pre * (root + (root * 0.044715) * square))
        hp = 0.5 + 0.5 * th
        act_out[0, :, cols] = (pre * hp).astype(BF)
        gp_s[:, cols] = hp + (0.5 * pre) * (1.0 - th * th) * (
            root + (3.0 * root * 0.044715) * square
        )

    @pl.when(k == 0)
    def _():
        for group in weight_copies():
            group[2]().wait()
        for copy in cot_copies():
            copy.wait()

    before2 = normed + dot_nt(act_out[0], wout[...]) + outer_bias
    xhat2, rstd2 = normalised(before2)
    row = lax.broadcasted_iota(jnp.int32, (R, 1), 0)
    position = (c ^ k) * span + row % span
    length = jnp.full((R, 1), meta[2], jnp.int32)
    for s in range(1, ns):
        length = jnp.where(row >= s * span, meta[2 + s], length)
    live = (position < length).astype(F32)
    lo_s[k] = (live * (xhat2 * gain2 + shift2)).astype(BF)
    for i in range(C):
        @pl.when(k == i)
        def _():
            pltpu.make_async_copy(lo_s.at[i], los[i], out_sems.at[i]).start()
    grad = cot_s[k].astype(F32) * live
    add_sum(4, grad * xhat2)
    add_sum(5, grad)
    second = norm_back(grad, gain2, xhat2, rstd2)
    og = second.astype(BF)
    og_out[0] = og
    add_sum(3, og.astype(F32))
    for j in range(FF // chunk):
        cols = slice(j * chunk, (j + 1) * chunk)
        ig = (dot_nn(og, wout[:, cols]) * gp_s[:, cols]).astype(BF)
        ig_out[0, :, cols] = ig
    ngrad = dot_nt(ig_out[0], wi[...]) + second
    add_sum(1, ngrad * xhat1)
    add_sum(2, ngrad)
    first = norm_back(ngrad, gain1, xhat1, rstd1)
    first_out[0] = first
    ag = first.astype(BF)
    ag_out[0] = ag
    add_sum(0, ag.astype(F32))
    dctx_out[0] = dot_nn(ag, wo[...]).astype(BF)

    @pl.when(k == C - 1)
    def _():
        for i in range(C):
            pltpu.make_async_copy(lo_s.at[i], los[i], out_sems.at[i]).wait()


def rows_call(dims, FF, meta, x_all, ctx, cots, weights):
    F, C, T, ns, span, D = dims
    R = ns * span
    tile = lambda n: pl.BlockSpec((1, R, n), lambda i: (i, 0, 0))
    widths = [(D, F32), (D, BF), (D, BF), (FF, BF), (D, BF), (FF, BF), (D, BF)]
    out_shape = (
        [jax.ShapeDtypeStruct((R, D), BF)] * C
        + [jax.ShapeDtypeStruct((C, R, n), kind) for n, kind in widths]
        + [jax.ShapeDtypeStruct((EXTRA, D), F32)]
    )
    n_w = F * T
    outs = pl.pallas_call(
        functools.partial(rows_kernel, dims, FF),
        name="rows",
        grid=(C,),
        out_shape=out_shape,
        in_specs=[SMEM, tile(D), tile(D)]
        + [ANY] * (C + len(weights)),
        out_specs=[ANY] * C
        + [tile(n) for n, _ in widths]
        + [const_spec((EXTRA, D))],
        scratch_shapes=[
            pltpu.VMEM((C, R, D), BF),
            pltpu.VMEM((C, R, D), BF),
            pltpu.VMEM((D, FF), BF),
            pltpu.VMEM((D, D), BF),
            pltpu.VMEM((D, FF), BF),
            pltpu.VMEM((R, FF), F32),
            pltpu.VMEM((n_w, EXTRA, FF // T), BF),
            pltpu.VMEM((6, D), F32),
            pltpu.VMEM((1, FF), F32),
            pltpu.SemaphoreType.DMA((5 * n_w + C,)),
            pltpu.SemaphoreType.DMA((C,)),
        ],
        compiler_params=pltpu.CompilerParams(vmem_limit_bytes=VMEM_LIMIT),
        cost_estimate=cost(4 * C * R * D * (2 * FF + D), 50e6, C * R * FF),
    )(meta, x_all, ctx, *cots, *weights)
    return outs[:C], outs[C:]


def back_kernel(dims, qkv, ctx, dctx, e_ref, linv, out, ds_s):
    F, C, T, ns, span, D = dims
    step = pl.program_id(0)
    NP, L, half = D // 128, C * span, D // T
    s = step // NP
    pair = step % NP
    q_col = head_columns(pair, half)
    k_col = pl.multiple_of(q_col + half, 128)
    v_col = pl.multiple_of(q_col + 2 * half, 128)
    c_col = pl.multiple_of(pair * 128, 128)
    q = qkv[:, s, :, pl.ds(q_col, 128)].reshape(L, 128)
    k = qkv[:, s, :, pl.ds(k_col, 128)].reshape(L, 128)
    v = qkv[:, s, :, pl.ds(v_col, 128)].reshape(L, 128)
    grad = dctx[:, s, :, pl.ds(c_col, 128)].reshape(L, 128).astype(F32) * linv[0]
    grad_low = grad.astype(BF)
    product = grad_low.astype(F32) * ctx[:, s, :, pl.ds(c_col, 128)].reshape(L, 128).astype(F32)
    low = lax.broadcasted_iota(jnp.int32, (L, 128), 1) < HD
    zero = jnp.zeros((), BF)
    qs, ks, gs = [], [], []
    for h in range(2):
        mine = low if h == 0 else jnp.logical_not(low)
        row_dot = jnp.sum(jnp.where(mine, product, 0.0), axis=-1, keepdims=True)
        probs_grad = dot_nt(grad_low, jnp.where(mine, v, zero))
        e = e_ref[0, h * L : (h + 1) * L, :].astype(F32)
        ds_s[h * L : (h + 1) * L, :] = (e * (probs_grad - row_dot)).astype(BF)
        qs.append(jnp.where(mine, q, zero))
        ks.append(jnp.where(mine, k, zero))
        gs.append(jnp.where(mine, grad_low, zero))
    scale = 1.0 / math.sqrt(HD)
    dq = (dot_nn(ds_s[:L, :], ks[0]) + dot_nn(ds_s[L:, :], ks[1])) * scale
    dk = dot_tn(ds_s[...], jnp.concatenate(qs, axis=0)) * scale
    dv = dot_tn(e_ref[0], jnp.concatenate(gs, axis=0))
    out[:, s, :, pl.ds(q_col, 128)] = dq.astype(BF).reshape(C, span, 128)
    out[:, s, :, pl.ds(k_col, 128)] = dk.astype(BF).reshape(C, span, 128)
    out[:, s, :, pl.ds(v_col, 128)] = dv.astype(BF).reshape(C, span, 128)


def back_call(dims, qkv, ctx, dctx, e, linv):
    F, C, T, ns, span, D = dims
    NP, L = D // 128, C * span
    return pl.pallas_call(
        functools.partial(back_kernel, dims),
        name="back",
        grid=(ns * NP,),
        out_shape=jax.ShapeDtypeStruct(qkv.shape, BF),
        in_specs=[
            const_spec(qkv.shape),
            const_spec(ctx.shape),
            const_spec(dctx.shape),
            pl.BlockSpec((1, 2 * L, L), lambda i: (i, 0, 0)),
            pl.BlockSpec((1, L, 128), lambda i: (i, 0, 0)),
        ],
        out_specs=const_spec(qkv.shape),
        scratch_shapes=[pltpu.VMEM((2 * L, L), BF)],
        compiler_params=pltpu.CompilerParams(vmem_limit_bytes=VMEM_LIMIT),
        cost_estimate=cost(ns * NP * 16 * L * L * 128, 30e6, 0),
    )(qkv, ctx, dctx, e, linv)


def input_kernel(C, dqkv, w, first, *refs):
    outs, (buf, sems) = refs[:C], refs[C:]
    k = pl.program_id(0)
    buf[k] = (dot_nt(dqkv[0], w[...]) + first[0]).astype(BF)
    for i in range(C):
        @pl.when(k == i)
        def _():
            pltpu.make_async_copy(buf.at[i], outs[i], sems.at[i]).start()

    @pl.when(k == C - 1)
    def _():
        for i in range(C):
            pltpu.make_async_copy(buf.at[i], outs[i], sems.at[i]).wait()


def input_call(dqkv, w, first):
    C, R, W = dqkv.shape
    D = w.shape[0]
    return pl.pallas_call(
        functools.partial(input_kernel, C),
        name="input_grad",
        grid=(C,),
        out_shape=[jax.ShapeDtypeStruct((R, D), BF)] * C,
        in_specs=[
            pl.BlockSpec((1, R, W), lambda i: (i, 0, 0)),
            const_spec(w.shape),
            pl.BlockSpec((1, R, D), lambda i: (i, 0, 0)),
        ],
        out_specs=[ANY] * C,
        scratch_shapes=[pltpu.VMEM((C, R, D), BF), pltpu.SemaphoreType.DMA((C,))],
        compiler_params=pltpu.CompilerParams(vmem_limit_bytes=VMEM_LIMIT),
        cost_estimate=cost(2 * C * R * D * W, 15e6, 0),
    )(dqkv, w, first)


COLS = 384


def weight_kernel(F, pers, with_sums, meta, *refs):
    n = len(pers)
    lefts, rights = refs[:n], refs[n : 2 * n]
    refs = refs[2 * n :]
    sums, refs = (refs[0], refs[1:]) if with_sums else (None, refs)
    keep, send, tile = refs[:3]
    turned = refs[3:]
    D = lefts[0].shape[1]
    Dl = D // F
    b = pl.program_id(1)

    @pl.when((pl.program_id(0) == 0) & (b == 0))
    def _():
        for left, left_t in zip(lefts, turned):
            left_t[:D, :] = left[...].T
            left_t[D:, :] = jnp.ones((EXTRA, left.shape[0]), BF)

    start = 0
    for right, left_t, per in zip(rights, turned, pers):
        @pl.when((b >= start) & (b < start + per))
        def _():
            tile[...] = dot_nn(left_t[...], right[...]).astype(BF)
        start += per
    if with_sums:
        for j in range(D // COLS):
            @pl.when(b == j)
            def _():
                tile[D:, :] = sums[:, j * COLS : (j + 1) * COLS].astype(BF)
    f = meta[0]
    for high in range(F // 2):
        for bit, out in ((0, keep), (1, send)):
            row = pl.multiple_of((f ^ (2 * high + bit)) * Dl, 16)
            out[high, 0, :Dl] = tile[pl.ds(row, Dl), :]
            out[high, 0, Dl:] = tile[D:, :]


def weight_call(dims, meta, pairs, sums=None):
    F, C, T, ns, span, D = dims
    rows = C * ns * span
    pairs = [(left.reshape(rows, -1), right.reshape(rows, -1)) for left, right in pairs]
    pers = [right.shape[1] // T // COLS for _, right in pairs]
    width = sum(pers) * COLS
    out = jax.ShapeDtypeStruct((F // 2, T, D // F + EXTRA, width), BF)
    out_spec = pl.BlockSpec((F // 2, 1, D // F + EXTRA, COLS), lambda a, b: (0, a, 0, b))
    right_specs, start = [], 0
    for per in pers:
        right_specs.append(
            pl.BlockSpec(
                (rows, COLS),
                lambda a, b, per=per, start=start: (0, a * per + jnp.clip(b - start, 0, per - 1)),
            )
        )
        start += per
    return pl.pallas_call(
        functools.partial(weight_kernel, F, pers, sums is not None),
        name="weight_grad",
        grid=(T, sum(pers)),
        out_shape=[out, out],
        in_specs=[SMEM]
        + [const_spec(left.shape) for left, _ in pairs]
        + right_specs
        + ([] if sums is None else [const_spec(sums.shape)]),
        out_specs=[out_spec, out_spec],
        scratch_shapes=[pltpu.VMEM((D + EXTRA, COLS), BF)]
        + [pltpu.VMEM((D + EXTRA, rows), BF) for _ in pairs],
        compiler_params=pltpu.CompilerParams(vmem_limit_bytes=VMEM_LIMIT),
        cost_estimate=cost(
            2 * rows * D * width * T, 2 * (rows * (D + width * T) + D * width * T), 0
        ),
    )(
        meta,
        *[left for left, _ in pairs],
        *[right for _, right in pairs],
        *([] if sums is None else [sums]),
    )


def xor_pairs(count, mask):
    return [(i, i ^ mask) for i in range(count)]


def after(value, others):
    return lax.optimization_barrier((value, *others))[0]


def added(a, b):
    return (a.astype(F32) + b.astype(F32)).astype(BF)


def per_device(
    tokens_in, seq_lengths, query_weight, query_bias, key_weight, value_weight, value_bias,
    output_weight, output_bias, attn_gain, attn_shift, inner_weight, inner_bias, outer_weight,
    outer_bias, ffn_gain, ffn_shift, cotangent,
):
    F, C, T = (lax.axis_size(a) for a in ("fsdp", "ctx", "tp"))
    f, c, t = (lax.axis_index(a) for a in ("fsdp", "ctx", "tp"))
    S, span, D = tokens_in.shape
    ns = S // (C * T)
    Dl, half = D // F, D // T
    fhalf = inner_weight.shape[1]
    FF = fhalf * T
    R = ns * span
    dims = (F, C, T, ns, span, D)

    def sequence_pieces(array):
        return [
            lax.dynamic_slice_in_dim(array, ((c ^ k) * T + t) * ns, ns, 0).reshape(R, D)
            for k in range(C)
        ]

    def ctx_moved(piece, k):
        return lax.ppermute(piece, "ctx", xor_pairs(C, k)) if k else piece

    def tp_moved(pieces):
        both = jnp.concatenate(pieces, axis=0) if len(pieces) > 1 else pieces[0]
        return [both] + [lax.ppermute(both, "tp", xor_pairs(T, dt)) for dt in range(1, T)]

    def to_slots(groups, kind):
        out = lax.full((S, span, D), 0, kind)
        pieces = {}
        for ks, group in groups:
            for dt, merged in enumerate(group):
                for i, k in enumerate(ks):
                    pieces[k, dt] = merged[i * R : (i + 1) * R]
        for k in range(C):
            for dt in range(T):
                got = pieces[k, dt]
                out = lax.dynamic_update_slice_in_dim(
                    out, got.reshape(ns, span, D).astype(kind), ((c ^ k) * T + (t ^ dt)) * ns, 0
                )
        return out

    def swapped(array, axis, bit):
        return lax.ppermute(array, axis, xor_pairs(lax.axis_size(axis), bit))

    def chip_start(shard, across):
        held = shard[None]
        for axis, bit in order_of(F, T, across)[:-1]:
            held = jnp.concatenate([held, swapped(held, axis, bit)], axis=0)
        return held

    def chip_end(held, across):
        axis, bit = order_of(F, T, across)[-1]
        return swapped(held, axis, bit)

    def both_cores(held, got, others=()):
        near = swapped(after(held, others), "fsdp", 1)
        return [held, got, near, swapped(got, "fsdp", 1)]

    def spread(array, width):
        rows, part = array.shape
        owner = lax.broadcasted_iota(jnp.int32, (rows, part * F), 1) // part
        return jnp.where(owner == f, jnp.tile(array, (1, F)), jnp.zeros((), BF)).reshape(-1, width)

    x_pieces = sequence_pieces(tokens_in)
    near_x = ctx_moved(x_pieces[1], 1)
    before = [near_x]
    x_pieces[1] = near_x
    for k in [*range(2, C, 2), *range(3, C, 2)]:
        x_pieces[k] = ctx_moved(after(x_pieces[k], before), k)
        before = [x_pieces[k]]
    vectors = [output_bias, attn_gain, attn_shift, outer_bias, ffn_gain, ffn_shift]
    vectors = jnp.concatenate(vectors).reshape(len(vectors), Dl)
    small = [
        spread(query_bias, half), spread(value_bias, half), spread(inner_bias, fhalf),
        spread(vectors, D),
    ]
    small = jnp.concatenate([jnp.pad(a, ((0, 0), (0, fhalf - a.shape[1]))) for a in small])
    small = jnp.pad(small, ((0, EXTRA - small.shape[0]), (0, 0)))
    low = jnp.concatenate([query_weight, key_weight], axis=1)
    high = jnp.concatenate([value_weight, output_weight.T], axis=1)
    low = chip_start(jnp.concatenate([low, small[:, :D]], axis=0), False)
    high = chip_start(jnp.concatenate([high, small[:, D:]], axis=0), True)
    lows = both_cores(low, chip_end(after(low, [near_x]), False))
    highs = both_cores(high, chip_end(after(high, [near_x]), True))
    halfway = [lows[1], highs[1], *x_pieces[2::2]]
    inner = chip_start(after(inner_weight, halfway), False)
    outer = chip_start(after(outer_weight.T, halfway), True)
    inner_got = chip_end(after(inner, x_pieces[3::2]), False)
    outer_got = chip_end(after(outer, x_pieces[3::2]), True)
    cot_pieces = sequence_pieces(after(cotangent, [*x_pieces[1:], *lows, *highs]))
    cot_pieces = [ctx_moved(piece, k) for k, piece in enumerate(cot_pieces)]
    lengths = lax.dynamic_slice_in_dim(seq_lengths, (c * T + t) * ns, ns, 0)
    meta = jnp.concatenate([jnp.stack([f, c]).astype(jnp.int32), lengths])

    x_all, qkv_w, qkv, e, linv, ctx = front_call(
        dims, after(meta, [inner, outer]), x_pieces, lows, highs
    )
    inners = both_cores(inner, inner_got, [ctx, *cot_pieces[1:]])
    outers = both_cores(outer, outer_got, [ctx, *cot_pieces[1:]])
    los, (first, dctx, nl, act, og, inner_low, ag, sums) = rows_call(
        dims, FF, meta, x_all, ctx.reshape(C, R, D), cot_pieces, lows + highs + inners + outers,
    )

    def core_sum(keep, send):
        return added(keep, lax.ppermute(send, "fsdp", xor_pairs(F, 1)))

    def chip_sum(total, axis, dim):
        got = total
        while total.shape[dim] > 1:
            h = total.shape[dim] // 2
            stay, go = jnp.split(total, 2, axis=dim)
            got = swapped(go, axis, 2 * h if axis == "fsdp" else h)
            total = added(stay, got)
        return total, got

    def y_sum(total):
        return chip_sum(total, "fsdp", 0)

    def x_sum(total):
        return chip_sum(total, "tp", 1)

    def ctx_scatter(totals):
        part = totals[0].shape[1] // C
        sums_in = []
        for k in range(C):
            blocks = [lax.dynamic_slice_in_dim(a, (c ^ k) * part, part, 1) for a in totals]
            block = jnp.concatenate(blocks, axis=0) if len(blocks) > 1 else blocks[0]
            sums_in.append(ctx_moved(block, k).astype(F32))
        while len(sums_in) > 1:
            sums_in = [a + b for a, b in zip(sums_in[::2], sums_in[1::2])]
        return sums_in[0].astype(BF)

    def ctx_gather(mine, likes):
        rows, part = likes[0].shape[0], mine.shape[1]
        outs = list(likes)
        for k in range(C):
            got = ctx_moved(mine, k)
            for i in range(len(likes)):
                outs[i] = lax.dynamic_update_slice_in_dim(
                    outs[i], got[i * rows : (i + 1) * rows], (c ^ k) * part, 1
                )
        return [out.astype(F32) for out in outs]

    outer_parts = weight_call(dims, meta, [(og, act)], sums)
    inner_parts = weight_call(dims, meta, [(after(nl, outer_parts), inner_low)])
    los = [ctx_moved(piece, k) for k, piece in enumerate(los)]
    keep, send = outer_parts
    outer_core = core_sum(keep, after(send, los[1:2]))
    keep, send = inner_parts
    inner_parts = keep, after(send, los[3:4])
    dctx = after(dctx, [outer_core, *inner_parts])
    dqkv = back_call(dims, qkv, ctx, dctx.reshape(ctx.shape), e, linv)
    inner_core = core_sum(*inner_parts)
    outer_y, outer_raw = y_sum(outer_core)
    even = range(2, C, 2)
    early = [0] + list(range(1, C, 2))
    early_lo = tp_moved([los[k] for k in early])
    first = after(first, [inner_core, outer_y, *los[1:], *early_lo[1:]])
    ins = input_call(dqkv.reshape(C, R, 3 * D), qkv_w, first)
    late_lo = tp_moved([after(los[k], [dqkv]) for k in even])
    outer_x, outer_raw = x_sum(outer_y)
    inner_y, inner_raw = y_sum(inner_core)
    ag = after(ag, ins)
    keep, send = weight_call(dims, meta, [(x_all, dqkv), (ag, ctx)])
    ig = [ctx_moved(piece, k) if k % 2 else piece for k, piece in enumerate(ins)]
    send = after(send, [outer_raw, inner_raw] + ig[1::2] + late_lo[1:])
    qkv_core = core_sum(keep, send)
    for k in even:
        ig[k] = ctx_moved(after(ins[k], ig[1::2]), k)
    outer_x = after(outer_x[0, 0], [qkv_core])
    early_ig = tp_moved(after(tuple(ig[k] for k in early), [qkv_core]))
    qkv_y, _ = y_sum(qkv_core)
    inner_x, _ = x_sum(after(inner_y, [qkv_core]))
    inner_x = inner_x[0, 0]
    two_parts = ctx_scatter([outer_x, inner_x])
    outer_g, inner_g = ctx_gather(after(two_parts, [qkv_y] + [ig[k] for k in even]), [outer_x, inner_x])
    qkv_x, _ = x_sum(qkv_y)
    qkv_x = after(qkv_x[0, 0], [two_parts])
    qkv_part = ctx_scatter([qkv_x])
    late_ig = tp_moved([after(ig[k], [qkv_x]) for k in even])
    early_lo, late_lo = (after(tuple(part), [qkv_core]) for part in (early_lo, late_lo))
    early_ig = after(tuple(early_ig), [qkv_x])
    layer_out = to_slots([(early, early_lo), (list(even), late_lo)], BF)
    input_grad = to_slots([(early, early_ig), (list(even), late_ig)], F32)
    (qkv_g,) = ctx_gather(qkv_part, [qkv_x])

    def own(row, shape):
        whole = row.reshape(shape[0], shape[1] * F)
        return lax.dynamic_slice_in_dim(whole, f * shape[1], shape[1], 1)

    vec_sums = lax.dynamic_slice_in_dim(outer_g[Dl : Dl + 6, :D], f * Dl, Dl, 1)

    return (
        layer_out,
        input_grad,
        qkv_g[:Dl, :half],
        own(qkv_g[Dl, :half], query_bias.shape),
        qkv_g[:Dl, half : 2 * half],
        qkv_g[:Dl, 2 * half : 3 * half],
        own(qkv_g[Dl, 2 * half : 3 * half], value_bias.shape),
        qkv_g[:Dl, 3 * half :].T,
        vec_sums[0],
        vec_sums[1],
        vec_sums[2],
        inner_g[:Dl],
        own(inner_g[Dl], inner_bias.shape),
        outer_g[:Dl].T,
        vec_sums[3],
        vec_sums[4],
        vec_sums[5],
    )


def solution(mesh):
    rows3, flat = P("fsdp", "ctx", None), P("fsdp")
    wide, tall = P("fsdp", "tp"), P("tp", "fsdp")
    params = (wide, tall, wide, wide, tall, tall, flat, flat, flat, wide, tall, tall, flat, flat, flat)
    return jax.shard_map(
        per_device,
        mesh=mesh,
        in_specs=(rows3, P("fsdp")) + params + (rows3,),
        out_specs=(rows3, rows3) + params,
        check_vma=False,
    )
```
